512 devices in a mesh: gy: 32 (over z, core), gx: 16 (over x, y).
Axes of the slice: x: 4, y: 4, z: 16, core: 2. Of those that a mesh axis runs over, the one named last changes fastest.
Arguments:
- level_in: bfloat16 [256, 1024, 128], P('gy', 'gx'), may hold values from -6 to 6
- w_level: bfloat16 [3, 3, 128, 128], replicated, may hold values from -0.1875 to 0.1875
- w_down: bfloat16 [2, 2, 128, 256], replicated, may hold values from -0.25 to 0.25
- w_neck: bfloat16 [3, 3, 256, 256], replicated, may hold values from -0.125 to 0.125
- cotangent: bfloat16 [128, 512, 256], P('gy', None, 'gx'), may hold values from -6 to 6
Outputs:
- neck_out: bfloat16 [128, 512, 256], P('gy', None, 'gx')
- grad_input: bfloat16 [256, 1024, 128], P('gy', 'gx')
- grad_level: bfloat16 [3, 3, 128, 128], replicated
- grad_down: bfloat16 [2, 2, 128, 256], replicated
- grad_neck: bfloat16 [3, 3, 256, 256], replicated
The draws below stay inside these ranges and needn't reach their ends.
All inputs are finite; a program needn't handle non-finite values.
Results may differ from the reference program's by a relative error of at most 0.012.
Values may be sent and summed in bfloat16 or wider, within the bound.
A program may use at most 64 MiB of HBM per device.

```python
import math
import jax
import jax.numpy as jnp

C4 = 128
CB = 256
H4 = 256
W4 = 1024
HB = 128
WB = 512


def block_scale(key, shape, pieces, low, largest):
    gain, own = 1.0, jax.random.fold_in(key, 6)
    for dim, shards_of in pieces:
        steps = jnp.exp(jax.random.uniform(jax.random.fold_in(own, dim), (shards_of,), jnp.float32, low / len(pieces), largest / len(pieces)))
        gain = gain * jnp.repeat(steps, shape[dim] // shards_of).reshape([-1 if axis == dim else 1 for axis in range(len(shape))])
    return gain


def bell_draw(key, dims, width, reach, pieces=(), dtype=jnp.bfloat16):
    values = width * jax.random.normal(key, dims, jnp.float32)
    if pieces:
        values = values * block_scale(key, dims, pieces, -0.22, 0.18)
    return jnp.clip(values, -reach, reach).astype(dtype)


def setup_inputs(seed: int = 0) -> dict:
    key_list = jax.random.split(jax.random.key(seed), 6)
    level_in = bell_draw(key_list[0], (H4, W4, C4), 1.0, 6.0, ((0, 32), (1, 16)))
    w_level = bell_draw(key_list[1], (3, 3, C4, C4), (9 * C4) ** -0.5, 0.1875)
    w_down = bell_draw(key_list[2], (2, 2, C4, CB), (4 * C4) ** -0.5, 0.25)
    w_neck = bell_draw(key_list[3], (3, 3, CB, CB), (9 * CB) ** -0.5, 0.125)
    cotangent = bell_draw(key_list[4], (HB, WB, CB), 1.0, 6.0, ((0, 32), (2, 16)))
    return dict(level_in=level_in, w_level=w_level, w_down=w_down, w_neck=w_neck, cotangent=cotangent)


def slope_of(value):
    gate = jax.nn.sigmoid(value)
    return gate + value * gate * (1.0 - gate)

def conv_same(field_in, weights):
    height = field_in.shape[0]
    col_count = field_in.shape[1]
    padded = jnp.pad(field_in.astype(jnp.float32), ((1, 1), (1, 1), (0, 0)))
    kernel = weights.astype(jnp.float32)
    result = jnp.zeros((height, col_count, weights.shape[3]), jnp.float32)
    for offset_y in range(3):
        for offset_x in range(3):
            window = padded[offset_y:offset_y + height, offset_x:offset_x + col_count]
            result = result + jnp.einsum('hwc,cd->hwd', window, kernel[offset_y, offset_x])
    return result

def weight_terms(field_in, grads):
    height = field_in.shape[0]
    col_count = field_in.shape[1]
    padded = jnp.pad(field_in.astype(jnp.float32), ((1, 1), (1, 1), (0, 0)))
    grad_float = grads.astype(jnp.float32)
    kernel_rows = []
    for offset_y in range(3):
        kernel_row = []
        for offset_x in range(3):
            window = padded[offset_y:offset_y + height, offset_x:offset_x + col_count]
            kernel_row.append(jnp.einsum('hwc,hwd->cd', window, grad_float))
        kernel_rows.append(jnp.stack(kernel_row))
    return jnp.stack(kernel_rows)

def reference(level_in, w_level, w_down, w_neck, cotangent):
    level_pre = conv_same(level_in, w_level)
    level_act = (level_in.astype(jnp.float32) + jax.nn.silu(level_pre)).astype(jnp.bfloat16)
    level_grid = level_act.astype(jnp.float32).reshape(HB, 2, WB, 2, C4)
    neck_in = jnp.einsum('hpwqc,pqcd->hwd', level_grid, w_down.astype(jnp.float32)).astype(jnp.bfloat16)
    neck_pre = conv_same(neck_in, w_neck)
    neck_out = (neck_in.astype(jnp.float32) + jax.nn.silu(neck_pre)).astype(jnp.bfloat16)
    cot_float = cotangent.astype(jnp.float32)
    neck_gate = (cot_float * slope_of(neck_pre)).astype(jnp.bfloat16)
    flip_neck = jnp.transpose(w_neck[::-1, ::-1], (0, 1, 3, 2))
    neck_grad = (cot_float + conv_same(neck_gate, flip_neck)).astype(jnp.bfloat16)
    neck_scale = 1.0 / math.sqrt(HB * WB)
    grad_neck = (weight_terms(neck_in, neck_gate) * neck_scale).astype(jnp.bfloat16)
    level_back = jnp.einsum('hwd,pqcd->hpwqc', neck_grad.astype(jnp.float32), w_down.astype(jnp.float32)).reshape(H4, W4, C4)
    grad_down = (jnp.einsum('hpwqc,hwd->pqcd', level_grid, neck_grad.astype(jnp.float32)) * neck_scale).astype(jnp.bfloat16)
    level_gate = (level_back * slope_of(level_pre)).astype(jnp.bfloat16)
    flip_level = jnp.transpose(w_level[::-1, ::-1], (0, 1, 3, 2))
    grad_input = (level_back + conv_same(level_gate, flip_level)).astype(jnp.bfloat16)
    grad_level = (weight_terms(level_in, level_gate) * (1.0 / math.sqrt(H4 * W4))).astype(jnp.bfloat16)
    return (neck_out, grad_input, grad_level, grad_down, grad_neck)
```

```python
import functools
import math

import jax
import jax.numpy as jnp
from jax import lax
from jax.experimental import pallas as pl
from jax.experimental.pallas import tpu as pltpu
from jax.sharding import PartitionSpec as P

MESH = pl.DeviceIdType.MESH


def extended(cells, sides, width):
    for axis, dim in sides:
        count = lax.axis_size(axis)
        ends = count - 1
        head = lax.slice_in_dim(cells, 0, width, axis=dim)
        tail = lax.slice_in_dim(cells, cells.shape[dim] - width, cells.shape[dim], axis=dim)
        cells = jnp.concatenate(
            [
                lax.ppermute(tail, axis, [(i, (i + 1) % count) for i in range(ends)]),
                cells,
                lax.ppermute(head, axis, [((i + 1) % count, i) for i in range(ends)]),
            ],
            axis=dim,
        )
    return cells


def slope_of(value):
    gate = jax.nn.sigmoid(value)
    return gate + value * gate * (1.0 - gate)


def tile_rims(field_in):
    return extended(field_in, (("gy", 0), ("gx", 1)), 1)


def conv_padded(padded, weights):
    row_count = padded.shape[0] - 2
    col_count = padded.shape[1] - 2
    result = jnp.zeros((row_count * col_count, weights.shape[3]), jnp.float32)
    for offset_y in range(3):
        for offset_x in range(3):
            window = padded[offset_y : offset_y + row_count, offset_x : offset_x + col_count]
            window = window.reshape(row_count * col_count, padded.shape[2])
            result = result + jnp.dot(
                window, weights[offset_y, offset_x], preferred_element_type=jnp.float32
            )
    return result


def weight_terms(padded, grads):
    row_count = grads.shape[0]
    col_count = grads.shape[1]
    flat_grads = grads.reshape(row_count * col_count, grads.shape[2])
    kernel_rows = []
    for offset_y in range(3):
        kernel_row = []
        for offset_x in range(3):
            window = padded[offset_y : offset_y + row_count, offset_x : offset_x + col_count]
            window = window.reshape(row_count * col_count, padded.shape[2])
            kernel_row.append(
                lax.dot_general(
                    window, flat_grads, (((0,), (0,)), ((), ())), preferred_element_type=jnp.float32
                )
            )
        kernel_rows.append(jnp.stack(kernel_row))
    return jnp.stack(kernel_rows)


TILES = 14
HALF = 7
LEVEL_OWNERS = 12


def sums_kernel(
    scales,
    neck_ref, down_ref, level_ref,
    neck_out, down_out, level_out,
    pair_send, pair_recv, work, near_a, near_b, far_a, far_b, piece, z_recv, whole, fin,
    pair_sems, near_sems, far_sems, z_sems, zb_sems, out1_sems, out2_sems,
):
    gy, gx = lax.axis_index("gy"), lax.axis_index("gx")
    z, core = gy // 2, gy % 2
    x, y = gx // 4, gx % 4
    other = 1 - core

    def at(zz, cc, xx, yy):
        return (zz * 2 + cc, xx * 4 + yy)

    pair_dev = at(z, other, x, y)
    x_dev = [None] + [at(z, core, (x + k) % 4, y) for k in range(1, 4)]
    y_dev = [None] + [at(z, core, x, (y + k) % 4) for k in range(1, 4)]
    z_dev = [None] + [at((z + k) % 16, core, x, y) for k in range(1, 16)]

    barrier = pltpu.get_barrier_semaphore()
    peers = [pair_dev] + x_dev[1:] + y_dev[1:] + z_dev[1:]
    for peer in peers:
        pl.semaphore_signal(barrier, inc=1, device_id=peer, device_id_type=MESH)

    def lanes(half):
        return pl.ds(pl.multiple_of(half * 128, 128), 128)

    def terms(half, o):
        neck = neck_ref[pl.ds(pl.multiple_of(o * 144, 16), 144), lanes(half)]
        down = down_ref[pl.ds(pl.multiple_of(o * 32, 16), 32), lanes(half)]
        return neck.reshape(9, 16, 128), down.reshape(2, 16, 128)

    def level_terms(half, o):
        start = pl.multiple_of((half * LEVEL_OWNERS + o) * 48, 16)
        return level_ref[pl.ds(start, 48), :].reshape(3, 16, 128)

    def fill(o, carry):
        neck, down = terms(other, o)
        pair_send[o, 0:9] = neck.astype(jnp.bfloat16)
        pair_send[o, 9:11] = down.astype(jnp.bfloat16)
        return carry

    def fill_level(o, carry):
        pair_send[o, 11:14] = level_terms(other, o).astype(jnp.bfloat16)
        return carry

    lax.fori_loop(0, 16, fill, 0)
    lax.fori_loop(0, LEVEL_OWNERS, fill_level, 0)
    pair_send[LEVEL_OWNERS:, 11:14] = jnp.zeros((16 - LEVEL_OWNERS, 3, 16, 128), jnp.bfloat16)

    pl.semaphore_wait(barrier, len(peers))

    def copy(src, dst, sems, k, dev):
        return pltpu.make_async_remote_copy(
            src_ref=src, dst_ref=dst, send_sem=sems.at[0, k], recv_sem=sems.at[1, k],
            device_id=dev, device_id_type=MESH,
        )

    pair = copy(pair_send, pair_recv, pair_sems, 0, pair_dev)
    pair.start()
    pair.wait()

    def join(o, carry):
        neck, down = terms(core, o)
        xo, yo = o // 4, o % 4
        work[xo, yo, 0:9] = (neck + pair_recv[o, 0:9].astype(jnp.float32)).astype(jnp.bfloat16)
        work[xo, yo, 9:11] = (down + pair_recv[o, 9:11].astype(jnp.float32)).astype(jnp.bfloat16)
        return carry

    def join_level(o, carry):
        total = level_terms(core, o) + pair_recv[o, 11:14].astype(jnp.float32)
        work[o // 4, o % 4, 11:14] = total.astype(jnp.bfloat16)
        return carry

    lax.fori_loop(0, 16, join, 0)
    lax.fori_loop(0, LEVEL_OWNERS, join_level, 0)
    work[LEVEL_OWNERS // 4:, :, 11:14] = jnp.zeros((1, 4, 3, 16, 128), jnp.bfloat16)

    stage = []
    for k in range(1, 4):
        xp, yp = (x + k) % 4, (y + k) % 4
        stage.append(copy(work.at[xp, :, 0:HALF], near_a.at[k], near_sems, k, x_dev[k]))
        stage.append(copy(work.at[:, yp, HALF:], near_b.at[k], near_sems, 4 + k, y_dev[k]))
    for c in stage:
        c.start()
    for c in stage:
        c.wait_recv()
    f32 = jnp.float32
    for p in range(4):
        a = work[x, p, 0:HALF].astype(f32)
        b = work[p, y, HALF:].astype(f32)
        for k in range(1, 4):
            a = a + near_a[k, p].astype(f32)
            b = b + near_b[k, p].astype(f32)
        near_a[0, p] = a.astype(jnp.bfloat16)
        near_b[0, p] = b.astype(jnp.bfloat16)
    for c in stage:
        c.wait_send()
    stage = []
    for k in range(1, 4):
        xp, yp = (x + k) % 4, (y + k) % 4
        stage.append(copy(near_a.at[0, yp], far_a.at[k], far_sems, k, y_dev[k]))
        stage.append(copy(near_b.at[0, xp], far_b.at[k], far_sems, 4 + k, x_dev[k]))
    for c in stage:
        c.start()
    for c in stage:
        c.wait_recv()
    a = near_a[0, y].astype(f32)
    b = near_b[0, x].astype(f32)
    for k in range(1, 4):
        a = a + far_a[k].astype(f32)
        b = b + far_b[k].astype(f32)
    piece[0:HALF] = a.astype(jnp.bfloat16)
    piece[HALF:TILES] = b.astype(jnp.bfloat16)
    piece[TILES:] = jnp.zeros((2, 16, 128), jnp.bfloat16)
    for c in stage:
        c.wait_send()

    stage = [copy(piece.at[(z + k) % 16], z_recv.at[k], z_sems, k, z_dev[k]) for k in range(1, 16)]
    for c in stage:
        c.start()
    for c in stage:
        c.wait_recv()
    total = piece[z].astype(f32)
    for k in range(1, 16):
        total = total + z_recv[k].astype(f32)
    scale = jnp.where(z < 11, scales[0], scales[1])
    fin[z] = (total * scale).astype(jnp.bfloat16)
    for c in stage:
        c.wait_send()

    stage = []
    for k in range(1, 16):
        stage.append(copy(fin.at[z], fin.at[z], zb_sems, k, z_dev[k]))
    for c in stage:
        c.start()
    for c in stage:
        c.wait_recv()
    for c in stage:
        c.wait_send()
    whole[core, x, y] = fin[0:TILES]
    stage = []
    for k in range(1, 4):
        mine_a, mine_b = whole.at[core, x, y, 0:HALF], whole.at[core, x, y, HALF:]
        stage.append(copy(mine_a, mine_a, out1_sems, k, y_dev[k]))
        stage.append(copy(mine_b, mine_b, out1_sems, 4 + k, x_dev[k]))
    for c in stage:
        c.start()
    for c in stage:
        c.wait_recv()
    for c in stage:
        c.wait_send()
    stage = []
    for k in range(1, 4):
        mine_a, mine_b = whole.at[core, x, :, 0:HALF], whole.at[core, :, y, HALF:]
        stage.append(copy(mine_a, mine_a, out2_sems, k, x_dev[k]))
        stage.append(copy(mine_b, mine_b, out2_sems, 4 + k, y_dev[k]))
    for c in stage:
        c.start()
    for c in stage:
        c.wait_recv()
    for c in stage:
        c.wait_send()
    pair = copy(whole.at[core], whole.at[core], pair_sems, 1, pair_dev)
    pair.start()
    pair.wait()

    for half in range(2):
        def spread(o, carry, half=half):
            xo, yo = o // 4, o % 4
            cols = slice(half * 128, half * 128 + 128)
            neck_out[pl.ds(pl.multiple_of(o * 144, 16), 144), cols] = whole[half, xo, yo, 0:9].reshape(144, 128)
            down_out[pl.ds(pl.multiple_of(o * 32, 16), 32), cols] = whole[half, xo, yo, 9:11].reshape(32, 128)
            return carry

        def spread_level(o, carry, half=half):
            start = pl.multiple_of((half * LEVEL_OWNERS + o) * 48, 16)
            level_out[pl.ds(start, 48), :] = whole[half, o // 4, o % 4, 11:14].reshape(48, 128)
            return carry

        lax.fori_loop(0, 16, spread, 0)
        lax.fori_loop(0, LEVEL_OWNERS, spread_level, 0)


def summed(neck, down, level, neck_scale, level_scale):
    bf16 = jnp.bfloat16
    vmem = pl.BlockSpec(memory_space=pltpu.VMEM)
    dma = pltpu.SemaphoreType.DMA
    return pl.pallas_call(
        functools.partial(sums_kernel, (neck_scale, level_scale)),
        out_shape=[jax.ShapeDtypeStruct(t.shape, bf16) for t in (neck, down, level)],
        in_specs=[vmem] * 3,
        out_specs=[vmem] * 3,
        scratch_shapes=[
            pltpu.VMEM((16, TILES, 16, 128), bf16),
            pltpu.VMEM((16, TILES, 16, 128), bf16),
            pltpu.VMEM((4, 4, TILES, 16, 128), bf16),
            pltpu.VMEM((4, 4, HALF, 16, 128), bf16),
            pltpu.VMEM((4, 4, HALF, 16, 128), bf16),
            pltpu.VMEM((4, HALF, 16, 128), bf16),
            pltpu.VMEM((4, HALF, 16, 128), bf16),
            pltpu.VMEM((16, 16, 128), bf16),
            pltpu.VMEM((16, 16, 128), bf16),
            pltpu.VMEM((2, 4, 4, TILES, 16, 128), bf16),
            pltpu.VMEM((16, 16, 128), bf16),
            dma((2, 2)), dma((2, 8)), dma((2, 8)), dma((2, 16)), dma((2, 16)), dma((2, 8)), dma((2, 8)),
        ],
        compiler_params=pltpu.CompilerParams(
            collective_id=0, has_side_effects=True, vmem_limit_bytes=48 * 1024 * 1024
        ),
    )(neck, down, level)


def local(level_in, w_level, w_down, w_neck, cotangent):
    tile_rows = level_in.shape[0]
    tile_cols = level_in.shape[1]
    level_width = level_in.shape[2]
    neck_width = w_neck.shape[3]
    half_rows = tile_rows // 2
    half_cols = tile_cols // 2
    level_pad = tile_rims(level_in)
    level_pre = conv_padded(level_pad, w_level)
    level_flat = level_in.reshape(tile_rows * tile_cols, level_width).astype(jnp.float32)
    level_act = (level_flat + jax.nn.silu(level_pre)).astype(jnp.bfloat16)
    level_grid = level_act.reshape(half_rows, 2, half_cols, 2, level_width)
    neck_in = jnp.einsum(
        "hpwqc,pqcd->hwd", level_grid, w_down, preferred_element_type=jnp.float32
    ).astype(jnp.bfloat16)
    neck_pad = tile_rims(neck_in)
    neck_pre = conv_padded(neck_pad, w_neck)
    neck_flat = neck_in.reshape(half_rows * half_cols, neck_width).astype(jnp.float32)
    neck_tile = (
        (neck_flat + jax.nn.silu(neck_pre))
        .astype(jnp.bfloat16)
        .reshape(half_rows, half_cols, neck_width)
    )
    neck_out = lax.all_to_all(neck_tile, "gx", split_axis=2, concat_axis=1, tiled=True)
    neck_cot = lax.all_to_all(cotangent, "gx", split_axis=1, concat_axis=2, tiled=True)
    cot_flat = neck_cot.reshape(half_rows * half_cols, neck_width).astype(jnp.float32)
    neck_gate = (
        (cot_flat * slope_of(neck_pre))
        .astype(jnp.bfloat16)
        .reshape(half_rows, half_cols, neck_width)
    )
    flip_neck = jnp.transpose(w_neck[::-1, ::-1], (0, 1, 3, 2))
    gate_pad = tile_rims(neck_gate)
    neck_back = conv_padded(gate_pad, flip_neck)
    cot_tile = neck_cot.reshape(half_rows * half_cols, neck_width).astype(jnp.float32)
    neck_grad = (
        (cot_tile + neck_back).astype(jnp.bfloat16).reshape(half_rows, half_cols, neck_width)
    )
    neck_wgrad = weight_terms(neck_pad, neck_gate)
    level_back = jnp.einsum(
        "hwd,pqcd->hpwqc", neck_grad, w_down, preferred_element_type=jnp.float32
    )
    level_back = level_back.reshape(tile_rows * tile_cols, level_width)
    down_wgrad = jnp.einsum(
        "hpwqc,hwd->pqcd", level_grid, neck_grad, preferred_element_type=jnp.float32
    )
    level_gate = (
        (level_back * slope_of(level_pre))
        .astype(jnp.bfloat16)
        .reshape(tile_rows, tile_cols, level_width)
    )
    flip_level = jnp.transpose(w_level[::-1, ::-1], (0, 1, 3, 2))
    level_gpad = tile_rims(level_gate)
    grad_input = (level_back + conv_padded(level_gpad, flip_level)).astype(jnp.bfloat16)
    grad_input = grad_input.reshape(tile_rows, tile_cols, level_width)
    level_wgrad = weight_terms(level_pad, level_gate)
    device_count = lax.axis_size("gy") * lax.axis_size("gx")
    level_count = tile_rows * tile_cols * device_count
    level_scale = 1.0 / math.sqrt(level_count)
    neck_scale = 1.0 / math.sqrt(level_count // 4)
    neck_sum, down_sum, level_sum = summed(
        neck_wgrad.reshape(9 * neck_width, neck_width),
        down_wgrad.reshape(4 * level_width, neck_width),
        level_wgrad.reshape(9 * level_width, level_width),
        neck_scale,
        level_scale,
    )
    grad_level = level_sum.reshape(w_level.shape)
    grad_down = down_sum.reshape(w_down.shape)
    grad_neck = neck_sum.reshape(w_neck.shape)
    return (neck_out, grad_input, grad_level, grad_down, grad_neck)


def solution(mesh):
    return jax.shard_map(
        local,
        mesh=mesh,
        in_specs=(P("gy", "gx", None), P(), P(), P(), P("gy", None, "gx")),
        out_specs=(P("gy", None, "gx"), P("gy", "gx", None), P(), P(), P()),
        check_vma=False,
    )
```

```python
import functools
import math

import jax
import jax.numpy as jnp
from jax import lax
from jax.experimental import pallas as pl
from jax.experimental.pallas import tpu as pltpu
from jax.sharding import PartitionSpec as P

MESH = pl.DeviceIdType.MESH
BF16, F32 = jnp.bfloat16, jnp.float32

RIM = 5
WIDE = 96
NARROW = 48
SIDES = [(dy, dx) for dy in (-1, 0, 1) for dx in (-1, 0, 1) if (dy, dx) != (0, 0)]
NECK_TILES = 9
REST_TILES = 5
LEVEL_OWNERS = 12


def sigmoid(v):
    return 1.0 / (1.0 + jnp.exp(-v))


def slope_of(v):
    s = jax.nn.sigmoid(v)
    return s + v * s * (1.0 - s)


def dot(a, b):
    return jnp.dot(a, b, preferred_element_type=F32)


def dot_nt(a, b):
    return lax.dot_general(a, b, (((1,), (1,)), ((), ())), preferred_element_type=F32)


def dot_tn(a, b):
    return lax.dot_general(a, b, (((0,), (0,)), ((), ())), preferred_element_type=F32)


def kernel(
    scales,
    level_in, wl_hbm, wd_hbm, wn_hbm, cot_in,
    neck_out, grad_input, grad_level, grad_down, grad_neck,
    wl, wd, wn, wlt,
    lp, lf, im_l, pre_l, act, dn, nf, im_n, cf, gf, im_g, gate_own, ng, lbf, gp, g2f, im_b,
    cot_send, cot_recv, ct, hr, hc, hx, no_send, no_recv,
    neck_own, level_acc, down_acc,
    a_pair_s, a_pair_r, a_work, a_xy, a_piece, a_z, a_fin, a_all,
    b_pair_s, b_pair_r, b_work, b_xy, b_piece, b_z, b_fin, b_all,
    w_sem, e1_sem, cot_sem, ch_sem, no_sem, e4_sem,
    pair_sem, xy_sem, z_sem, zb_sem, xyb_sem,
):
    gy, gx = lax.axis_index("gy"), lax.axis_index("gx")
    z, core = gy // 2, gy % 2
    other = 1 - core

    def side(dy, dx):
        return ((gy + dy + 32) % 32, (gx + dx + 16) % 16)

    pair_dev = (z * 2 + other, gx)
    plane = [None] + [(gy, (gx + k) % 16) for k in range(1, 16)]

    def column(zz):
        return (zz * 2 + core, gx)

    barrier = pltpu.get_barrier_semaphore()
    peers = plane[1:] + [column((z + k) % 16) for k in range(1, 16)] + [side(dy, dx) for dy, dx in SIDES if dy != 0]
    for peer in peers:
        pl.semaphore_signal(barrier, inc=1, device_id=peer, device_id_type=MESH)

    loads = [
        pltpu.make_async_copy(wl_hbm, wl, w_sem.at[0]),
        pltpu.make_async_copy(wd_hbm, wd, w_sem.at[1]),
        pltpu.make_async_copy(wn_hbm, wn, w_sem.at[2]),
    ]
    for load in loads:
        load.start()

    def copy(src, dst, sems, k, dev):
        return pltpu.make_async_remote_copy(
            src_ref=src, dst_ref=dst, send_sem=sems.at[0, k], recv_sem=sems.at[1, k],
            device_id=dev, device_id_type=MESH,
        )

    sent = []

    def go(copies):
        for c in copies:
            c.start()
        sent.extend(copies)
        return copies

    lane = lax.broadcasted_iota(jnp.int32, (16, 128), 1)
    for q in range(4):
        rows = [cot_in[r, :, 128 * q:128 * q + 128].astype(F32) for r in range(4)]
        for j in range(4):
            out = pltpu.roll(rows[3], (32 * (3 - j)) % 128, 1) if j != 3 else rows[3]
            for r in (2, 1, 0):
                part = pltpu.roll(rows[r], (32 * (r - j)) % 128, 1) if r != j else rows[r]
                out = jnp.where(lane < 32 * (r + 1), part, out)
            cot_send[4 * q + j] = out.astype(BF16)
    cot_recv[gx] = cot_send[gx]

    top_ok = jnp.where(gy > 0, 1.0, 0.0).astype(F32)
    bottom_ok = jnp.where(gy < 31, 1.0, 0.0).astype(F32)
    left_ok = jnp.where(gx > 0, 1.0, 0.0).astype(F32)
    right_ok = jnp.where(gx < 15, 1.0, 0.0).astype(F32)

    lf[0:8] = jnp.zeros((8, 128), F32)
    lf[8 + 18 * WIDE:] = jnp.zeros((8, 128), F32)
    for r in range(8):
        start = 8 + (r + RIM) * WIDE + 16
        lf[start:start + 64] = level_in[r].astype(F32)

    pl.semaphore_wait(barrier, len(peers))

    cot_copies = go([
        copy(cot_send.at[(gx + k) % 16], cot_recv.at[gx], cot_sem, k, plane[k]) for k in range(1, 16)
    ])
    src_rows = {-1: slice(0, RIM), 0: slice(0, 8), 1: slice(8 - RIM, 8)}
    src_cols = {-1: slice(0, 16), 0: slice(0, 64), 1: slice(48, 64)}
    dst_rows = {-1: slice(RIM + 8, RIM + 8 + RIM), 0: slice(RIM, RIM + 8), 1: slice(0, RIM)}
    dst_cols = {-1: slice(80, 96), 0: slice(16, 80), 1: slice(0, 16)}
    e1 = go([
        copy(level_in.at[src_rows[dy], src_cols[dx]], lp.at[dst_rows[dy], dst_cols[dx]], e1_sem, n, side(dy, dx))
        for n, (dy, dx) in enumerate(SIDES)
    ])

    loads[0].wait()
    for ky in range(3):
        for kx in range(3):
            w = wl[2 - ky, (2 - kx) * 128:(3 - kx) * 128, :].astype(F32)
            wlt[ky, kx * 128:(kx + 1) * 128, :] = w.T.astype(BF16)

    for c in cot_copies:
        c.wait_recv()
    ct[...] = cot_recv[...].reshape(256, 128).astype(F32).T.astype(BF16).reshape(4, 32, 256)
    one_row = {-1: slice(0, 1), 0: slice(0, 4), 1: slice(3, 4)}
    half_cols = {-1: slice(0, 16), 0: slice(0, 32), 1: slice(16, 32)}

    def rim_buffer(dy, dx):
        if dx == 0:
            return hr.at[(dy + 1) // 2]
        if dy == 0:
            return hc.at[(dx + 1) // 2]
        return hx.at[(dy + 1) // 2, (dx + 1) // 2]

    ch = go([
        copy(ct.at[one_row[dy], half_cols[dx]], rim_buffer(dy, dx), ch_sem, n, side(dy, dx))
        for n, (dy, dx) in enumerate(SIDES)
    ])

    for c in e1:
        c.wait_recv()
    for r in range(18):
        row_ok = top_ok if r < RIM else bottom_ok if r >= RIM + 8 else None
        base = 8 + r * WIDE
        left = lp[r, 0:16].astype(F32) * left_ok
        right = lp[r, 80:96].astype(F32) * right_ok
        if row_ok is not None:
            left, right = left * row_ok, right * row_ok
            lf[base + 16:base + 80] = lp[r, 16:80].astype(F32) * row_ok
        lf[base:base + 16] = left
        lf[base + 80:base + 96] = right
    for r in range(18):
        for kx in range(3):
            start = 7 + kx + r * WIDE
            im_l[r * WIDE:(r + 1) * WIDE, kx * 128:(kx + 1) * 128] = lf[start:start + WIDE].astype(BF16)

    for q in range(4):
        pre = dot(im_l[4 * q * WIDE:(4 * q + 4) * WIDE], wl[0])
        for ky in (1, 2):
            pre = pre + dot(im_l[(4 * q + ky) * WIDE:(4 * q + ky + 4) * WIDE], wl[ky])
        own = lf[8 + (4 * q + 1) * WIDE:8 + (4 * q + 5) * WIDE]
        act[4 * q * WIDE:(4 * q + 4) * WIDE] = own + pre * jax.nn.sigmoid(pre)
        if q in (1, 2):
            pre_l[(q - 1) * 4 * WIDE:q * 4 * WIDE] = pre

    for rr in range(16):
        for q in range(2):
            lanes = slice(128 * (2 * (rr % 2) + q), 128 * (2 * (rr % 2) + q) + 128)
            dn[(rr // 2) * NARROW:(rr // 2 + 1) * NARROW, lanes] = act[pl.ds(rr * WIDE + q, NARROW, stride=2), :].astype(BF16)
    loads[1].wait()
    col = lax.broadcasted_iota(jnp.int32, (NARROW, 256), 0)
    col_ok = jnp.where(col < 8, left_ok, jnp.where(col >= 40, right_ok, 1.0))
    col_own = jnp.where((col >= 8) & (col < 40), 1.0, 0.0)
    nf[0:8] = jnp.zeros((8, 256), F32)
    nf[8 + 8 * NARROW:] = jnp.zeros((8, 256), F32)
    neck_in = dot(dn[...], wd[...]).astype(BF16).astype(F32)
    for r in range(8):
        row = neck_in[r * NARROW:(r + 1) * NARROW] * col_ok
        if r < 2:
            row = row * top_ok
        if r >= 6:
            row = row * bottom_ok
        nf[8 + r * NARROW:8 + (r + 1) * NARROW] = row
    for kx in range(3):
        im_n[:, kx * 256:(kx + 1) * 256] = nf[7 + kx:7 + kx + 8 * NARROW].astype(BF16)
    loads[2].wait()
    neck_pre = dot(im_n[0:6 * NARROW], wn[0])
    for ky in (1, 2):
        neck_pre = neck_pre + dot(im_n[ky * NARROW:(ky + 6) * NARROW], wn[ky])

    for c in ch:
        c.wait_recv()
    for r in range(6):
        if 1 <= r <= 4:
            mid = ct[r - 1].astype(F32)
            left = hc[1, r - 1, 8:16].astype(F32) * left_ok
            right = hc[0, r - 1, 0:8].astype(F32) * right_ok
        else:
            n, ok = (1, top_ok) if r == 0 else (0, bottom_ok)
            mid = hr[n, 0].astype(F32) * ok
            left = hx[n, 1, 0, 8:16].astype(F32) * (left_ok * ok)
            right = hx[n, 0, 0, 0:8].astype(F32) * (right_ok * ok)
        base = r * NARROW
        cf[base:base + 8] = left
        cf[base + 8:base + 40] = mid
        cf[base + 40:base + 48] = right

    gate = (cf[...] * slope_of(neck_pre)).astype(BF16).astype(F32)
    gf[0:8] = jnp.zeros((8, 256), F32)
    gf[8 + 6 * NARROW:] = jnp.zeros((8, 256), F32)
    gf[8:8 + 6 * NARROW] = gate
    for r in range(4):
        gate_own[r * NARROW:(r + 1) * NARROW] = (gate[(r + 1) * NARROW:(r + 2) * NARROW] * col_own).astype(BF16)

    def half_lanes(half):
        return pl.ds(pl.multiple_of(half * 128, 128), 128)

    theirs = gate_own[:, half_lanes(other)]
    for ky in range(3):
        part = dot_tn(im_n[(1 + ky) * NARROW:(5 + ky) * NARROW], theirs)
        a_pair_s[48 * ky:48 * ky + 48] = part.astype(BF16).reshape(48, 16, 128)
    a_pair = go([copy(a_pair_s, a_pair_r, pair_sem, 0, pair_dev)])
    mine = gate_own[:, half_lanes(core)]
    for ky in range(3):
        neck_own[48 * ky:48 * ky + 48] = dot_tn(im_n[(1 + ky) * NARROW:(5 + ky) * NARROW], mine).reshape(48, 16, 128)

    rows = []
    for r in range(4):
        v = neck_pre[(r + 1) * NARROW + 8:(r + 1) * NARROW + 40]
        rows.append(nf[8 + (r + 2) * NARROW + 8:8 + (r + 2) * NARROW + 40] + v * jax.nn.sigmoid(v))
    no_send[...] = jnp.concatenate(rows, axis=0).T.astype(BF16).reshape(16, 16, 128)
    no_recv[gx] = no_send[gx]
    no_copies = go([copy(no_send.at[(gx + k) % 16], no_recv.at[gx], no_sem, k, plane[k]) for k in range(1, 16)])

    for kx in range(3):
        im_g[:, kx * 256:(kx + 1) * 256] = gf[7 + kx:7 + kx + 6 * NARROW].astype(BF16)
    back = None
    for ky in range(3):
        for kx in range(3):
            term = dot_nt(
                im_g[ky * NARROW:(ky + 4) * NARROW, kx * 256:(kx + 1) * 256],
                wn[2 - ky, (2 - kx) * 256:(3 - kx) * 256, :],
            )
            back = term if back is None else back + term
    for r in range(4):
        v = cf[(r + 1) * NARROW:(r + 2) * NARROW] + back[r * NARROW:(r + 1) * NARROW]
        ng[r * NARROW:(r + 1) * NARROW] = (v * col_own).astype(BF16)
    spread = dot_nt(ng[...], wd[...])
    for r in range(4):
        for p in range(2):
            for q in range(2):
                lanes = slice(128 * (2 * p + q), 128 * (2 * p + q) + 128)
                lbf[pl.ds((2 * r + p) * WIDE + q, NARROW, stride=2), :] = spread[r * NARROW:(r + 1) * NARROW, lanes]
    for r in range(8):
        rows_r = slice(r * WIDE + 16, r * WIDE + 80)
        gp[r + 1, 16:80] = (lbf[rows_r] * slope_of(pre_l[rows_r])).astype(BF16)
    e4_src = {-1: slice(1, 2), 0: slice(1, 9), 1: slice(8, 9)}
    e4_dst = {-1: slice(9, 10), 0: slice(1, 9), 1: slice(0, 1)}
    e4_scol = {-1: slice(16, 32), 0: slice(16, 80), 1: slice(64, 80)}
    e4 = go([
        copy(gp.at[e4_src[dy], e4_scol[dx]], gp.at[e4_dst[dy], dst_cols[dx]], e4_sem, n, side(dy, dx))
        for n, (dy, dx) in enumerate(SIDES)
    ])

    own_gate = gp[1:9, 16:80].reshape(512, 128)
    for ky in range(3):
        window = jnp.concatenate(
            [im_l[(4 + ky + r) * WIDE + 16:(4 + ky + r) * WIDE + 80] for r in range(8)], axis=0
        )
        level_acc[ky * 384:(ky + 1) * 384] = dot_tn(window, own_gate)
    down_acc[...] = dot_tn(dn[2 * NARROW:6 * NARROW], ng[...])

    def rest_terms(half):
        down = down_acc[:, half_lanes(half)].reshape(16, 2, 16, 128)
        level = level_acc[pl.ds(pl.multiple_of(half * 576, 576), 576), :].reshape(LEVEL_OWNERS, 3, 16, 128)
        return down, level

    down, level = rest_terms(other)
    nothing = jnp.zeros((16 - LEVEL_OWNERS, 3, 16, 128), BF16)
    b_pair_s[:, 0:2] = down.astype(BF16)
    b_pair_s[0:LEVEL_OWNERS, 2:5] = level.astype(BF16)
    b_pair_s[LEVEL_OWNERS:, 2:5] = nothing
    b_pair = go([copy(b_pair_s, b_pair_r, pair_sem, 1, pair_dev)])

    def plane_stage(work, buf, sems, first):
        return go([copy(work(( gx + k) % 16), buf.at[k], sems, first + k, plane[k]) for k in range(1, 16)])

    def a_piece_of(o):
        return a_work.at[pl.ds(o * NECK_TILES, NECK_TILES)]

    def b_piece_of(o):
        return b_work.at[o]

    a_pair[0].wait_recv()
    for n in range(16):
        part = slice(n * NECK_TILES, (n + 1) * NECK_TILES)
        a_work[part] = (neck_own[part] + a_pair_r[part].astype(F32)).astype(BF16)
    a_plane = plane_stage(a_piece_of, a_xy, xy_sem, 0)

    b_pair[0].wait_recv()
    down, level = rest_terms(core)
    b_work[:, 0:2] = (down + b_pair_r[:, 0:2].astype(F32)).astype(BF16)
    b_work[0:LEVEL_OWNERS, 2:5] = (level + b_pair_r[0:LEVEL_OWNERS, 2:5].astype(F32)).astype(BF16)
    b_work[LEVEL_OWNERS:, 2:5] = nothing
    b_plane = plane_stage(b_piece_of, b_xy, xy_sem, 16)

    for c in e4:
        c.wait_recv()
    g2f[0:8] = jnp.zeros((8, 128), F32)
    g2f[8 + 10 * WIDE:] = jnp.zeros((8, 128), F32)
    for r in range(10):
        row_ok = top_ok if r == 0 else bottom_ok if r == 9 else None
        base = 8 + r * WIDE
        left, mid, right = gp[r, 0:16].astype(F32) * left_ok, gp[r, 16:80].astype(F32), gp[r, 80:96].astype(F32) * right_ok
        if row_ok is not None:
            left, mid, right = left * row_ok, mid * row_ok, right * row_ok
        g2f[base:base + 16] = left
        g2f[base + 16:base + 80] = mid
        g2f[base + 80:base + 96] = right
    for r in range(10):
        for kx in range(3):
            start = 7 + kx + r * WIDE
            im_b[r * WIDE:(r + 1) * WIDE, kx * 128:(kx + 1) * 128] = g2f[start:start + WIDE].astype(BF16)
    for q in range(2):
        total = lbf[4 * q * WIDE:(4 * q + 4) * WIDE]
        for ky in range(3):
            total = total + dot(im_b[(4 * q + ky) * WIDE:(4 * q + ky + 4) * WIDE], wlt[ky])
        grad_input[4 * q:4 * q + 4] = total.reshape(4, WIDE, 128)[:, 16:80].astype(BF16)

    for c in no_copies:
        c.wait_recv()
    for q in range(4):
        pieces = [no_recv[4 * q + j].astype(F32) for j in range(4)]
        for r in range(4):
            out = pltpu.roll(pieces[3], (32 * (3 - r)) % 128, 1) if r != 3 else pieces[3]
            for j in (2, 1, 0):
                part = pltpu.roll(pieces[j], (32 * (j - r)) % 128, 1) if r != j else pieces[j]
                out = jnp.where(lane < 32 * (j + 1), part, out)
            neck_out[r, :, 128 * q:128 * q + 128] = out.astype(BF16)

    def z_send(piece, buf, tiles, first, sems, offset):
        copies = []
        for t in range(tiles):
            c = copy_z(piece.at[t], buf.at[z], sems, offset + t, offset + z, column(first + t))
            copies.append((z != first + t, c))
        return copies

    def copy_z(src, dst, sems, ks, kr, dev):
        return pltpu.make_async_remote_copy(
            src_ref=src, dst_ref=dst, send_sem=sems.at[0, ks], recv_sem=sems.at[1, kr],
            device_id=dev, device_id_type=MESH,
        )

    def start_all(copies):
        for cond, c in copies:
            pl.when(cond)(c.start)

    def plane_sum(piece_of, buf, own_ref, copies, out):
        for c in copies:
            c.wait_recv()
        total = own_ref[...].astype(F32)
        for k in range(1, 16):
            total = total + buf[k].astype(F32)
        out[...] = total.astype(BF16)

    def owns(first, tiles):
        return (z >= first) & (z < first + tiles)

    def z_sum(piece, buf, fin, tiles, first, sems, offset, scale):
        @pl.when(owns(first, tiles))
        def _():
            mine = z - first
            for s in range(16):
                @pl.when(z != s)
                def _(s=s):
                    copy_z(piece.at[0], buf.at[s], sems, offset, offset + s, column(s)).wait_recv()
            buf[z] = piece[mine]
            total = buf[0].astype(F32)
            for s in range(1, 16):
                total = total + buf[s].astype(F32)
            fin[mine] = (total * scale).astype(BF16)
            for s in range(16):
                @pl.when(z != s)
                def _(s=s):
                    copy_z(fin.at[mine], fin.at[mine], zb_sem, offset + s, offset + mine, column(s)).start()

    def z_back(fin, tiles, first, offset):
        for t in range(tiles):
            @pl.when(z != first + t)
            def _(t=t):
                copy_z(fin.at[t], fin.at[t], zb_sem, offset, offset + t, column(first + t)).wait_recv()

    def z_back_sent(fin, tiles, first, offset):
        @pl.when(owns(first, tiles))
        def _():
            for s in range(16):
                @pl.when(z != s)
                def _(s=s):
                    copy_z(fin.at[0], fin.at[0], zb_sem, offset + s, offset, column(s)).wait_send()

    plane_sum(a_piece_of, a_xy, a_piece_of(gx), a_plane, a_piece)
    a_zs = z_send(a_piece, a_z, NECK_TILES, 0, z_sem, 0)
    start_all(a_zs)
    plane_sum(b_piece_of, b_xy, b_piece_of(gx), b_plane, b_piece)
    b_zs = z_send(b_piece, b_z, REST_TILES, NECK_TILES, z_sem, 16)
    start_all(b_zs)
    z_sum(a_piece, a_z, a_fin, NECK_TILES, 0, z_sem, 0, scales[0])
    z_sum(b_piece, b_z, b_fin, REST_TILES, NECK_TILES, z_sem, 16, jnp.where(z < NECK_TILES + 2, scales[0], scales[1]))

    z_back(a_fin, NECK_TILES, 0, 0)
    a_all[core, gx] = a_fin[...]
    a_mine = a_all.at[core, gx]
    a_back = go([copy(a_mine, a_mine, xyb_sem, k, plane[k]) for k in range(1, 16)])
    z_back(b_fin, REST_TILES, NECK_TILES, 16)
    b_all[core, gx] = b_fin[...]
    b_mine = b_all.at[core, gx]
    b_back = go([copy(b_mine, b_mine, xyb_sem, 16 + k, plane[k]) for k in range(1, 16)])

    def landed(ref, tiles, sems, first):
        for k in range(1, 16):
            slot = ref.at[core, (gx + 16 - k) % 16]
            copy(slot, slot, sems, first + k, plane[k]).wait_recv()

    landed(a_all, NECK_TILES, xyb_sem, 0)
    a_swap = go([copy(a_all.at[core], a_all.at[core], pair_sem, 2, pair_dev)])
    landed(b_all, REST_TILES, xyb_sem, 16)
    b_swap = go([copy(b_all.at[core], b_all.at[core], pair_sem, 3, pair_dev)])
    copy(a_all.at[other], a_all.at[other], pair_sem, 2, pair_dev).wait_recv()
    for half in range(2):
        lanes = slice(half * 128, half * 128 + 128)
        grad_neck[:, lanes] = a_all[half].reshape(2304, 128)
    copy(b_all.at[other], b_all.at[other], pair_sem, 3, pair_dev).wait_recv()
    for half in range(2):
        lanes = slice(half * 128, half * 128 + 128)
        grad_down[:, lanes] = b_all[half, :, 0:2].reshape(512, 128)
        grad_level[half * 576:(half + 1) * 576] = b_all[half, 0:LEVEL_OWNERS, 2:5].reshape(576, 128)

    for c in sent:
        c.wait_send()
    for cond, c in a_zs + b_zs:
        pl.when(cond)(c.wait_send)
    z_back_sent(a_fin, NECK_TILES, 0, 0)
    z_back_sent(b_fin, REST_TILES, NECK_TILES, 16)


def local(level_in, w_level, w_down, w_neck, cotangent):
    device_count = lax.axis_size("gy") * lax.axis_size("gx")
    level_count = level_in.shape[0] * level_in.shape[1] * device_count
    level_scale = 1.0 / math.sqrt(level_count)
    neck_scale = 1.0 / math.sqrt(level_count // 4)
    vmem = pl.BlockSpec(memory_space=pltpu.VMEM)
    hbm = pl.BlockSpec(memory_space=pl.ANY)
    dma = pltpu.SemaphoreType.DMA

    def v(*shape, dtype=BF16):
        return pltpu.VMEM(shape, dtype)

    def group(tiles, flat):
        whole = (16 * tiles, 16, 128) if flat else (16, tiles, 16, 128)
        return [
            v(*whole), v(*whole), v(*whole), v(16, tiles, 16, 128), v(tiles, 16, 128), v(16, 16, 128), v(tiles, 16, 128),
            v(2, 16, tiles, 16, 128),
        ]

    outs = pl.pallas_call(
        functools.partial(kernel, (neck_scale, level_scale)),
        out_shape=[
            jax.ShapeDtypeStruct((4, 16, 512), BF16),
            jax.ShapeDtypeStruct((8, 64, 128), BF16),
            jax.ShapeDtypeStruct((1152, 128), BF16),
            jax.ShapeDtypeStruct((512, 256), BF16),
            jax.ShapeDtypeStruct((2304, 256), BF16),
        ],
        in_specs=[vmem, hbm, hbm, hbm, vmem],
        out_specs=[vmem] * 5,
        scratch_shapes=[
            v(3, 384, 128), v(512, 256), v(3, 768, 256), v(3, 384, 128),
            v(18, WIDE, 128), v(16 + 18 * WIDE, 128, dtype=F32), v(18 * WIDE, 384),
            v(8 * WIDE, 128, dtype=F32), v(16 * WIDE, 128, dtype=F32), v(8 * NARROW, 512),
            v(16 + 8 * NARROW, 256, dtype=F32), v(8 * NARROW, 768),
            v(6 * NARROW, 256, dtype=F32), v(16 + 6 * NARROW, 256, dtype=F32), v(6 * NARROW, 768),
            v(4 * NARROW, 256), v(4 * NARROW, 256), v(8 * WIDE, 128, dtype=F32),
            v(10, WIDE, 128), v(16 + 10 * WIDE, 128, dtype=F32), v(10 * WIDE, 384),
            v(16, 16, 128), v(16, 16, 128), v(4, 32, 256), v(2, 1, 32, 256), v(2, 4, 16, 256), v(2, 2, 1, 16, 256),
            v(16, 16, 128), v(16, 16, 128),
            v(144, 16, 128, dtype=F32), v(1152, 128, dtype=F32), v(512, 256, dtype=F32),
            *group(NECK_TILES, True), *group(REST_TILES, False),
            dma((3,)), dma((2, 8)), dma((2, 16)), dma((2, 8)), dma((2, 16)), dma((2, 8)),
            dma((2, 4)), dma((2, 32)), dma((2, 32)), dma((2, 32)), dma((2, 32)),
        ],
        compiler_params=pltpu.CompilerParams(
            collective_id=0, has_side_effects=True, vmem_limit_bytes=56 * 1024 * 1024
        ),
    )(
        level_in,
        w_level.reshape(3, 384, 128),
        w_down.reshape(512, 256),
        w_neck.reshape(3, 768, 256),
        jnp.transpose(cotangent, (0, 2, 1)),
    )
    return (
        jnp.transpose(outs[0], (0, 2, 1)),
        outs[1],
        outs[2].reshape(w_level.shape),
        outs[3].reshape(w_down.shape),
        outs[4].reshape(w_neck.shape),
    )


def solution(mesh):
    return jax.shard_map(
        local,
        mesh=mesh,
        in_specs=(P("gy", "gx", None), P(), P(), P(), P("gy", None, "gx")),
        out_specs=(P("gy", None, "gx"), P("gy", "gx", None), P(), P(), P()),
        check_vma=False,
    )
```

```python
import functools
import math

import jax
import jax.numpy as jnp
from jax import lax
from jax.experimental import pallas as pl
from jax.experimental.pallas import tpu as pltpu
from jax.sharding import PartitionSpec as P

MESH = pl.DeviceIdType.MESH
BF16, F32 = jnp.bfloat16, jnp.float32

RIM = 5
WIDE = 96
NARROW = 48
SIDES = [(dy, dx) for dy in (-1, 0, 1) for dx in (-1, 0, 1) if (dy, dx) != (0, 0)]
NECK_TILES = 9
REST_TILES = 5
LEVEL_OWNERS = 12


def sigmoid(v):
    return 1.0 / (1.0 + jnp.exp(-v))


def slope_of(v):
    s = jax.nn.sigmoid(v)
    return s + v * s * (1.0 - s)


def dot(a, b):
    return jnp.dot(a, b, preferred_element_type=F32)


def dot_nt(a, b):
    return lax.dot_general(a, b, (((1,), (1,)), ((), ())), preferred_element_type=F32)


def dot_tn(a, b):
    return lax.dot_general(a, b, (((0,), (0,)), ((), ())), preferred_element_type=F32)


def kernel(
    scales,
    level_in, wl_hbm, wd_hbm, wn_hbm, cot_hbm,
    neck_out, grad_input, a_all, b_all,
    level_own, cot_in, wl, wd, wn, wlt,
    lp, lf, im_l, pre_l, act, dn, nf, im_n, cf, gf, im_g, gate_own, ng, lbf, gp, g2f, im_b,
    cot_send, cot_recv, ct, hr, hc, hx, no_send, no_recv,
    neck_own, level_acc, down_acc,
    a_pair_s, a_pair_r, a_work, a_xy, a_piece, a_z, a_fin,
    b_pair_s, b_pair_r, b_work, b_xy, b_piece, b_z, b_fin,
    w_sem, e1_sem, cot_sem, ch_sem, no_sem, e4_sem,
    pair_sem, xy_sem, z_sem, zb_sem, xyb_sem,
):
    gy, gx = lax.axis_index("gy"), lax.axis_index("gx")
    z, core = gy // 2, gy % 2
    other = 1 - core

    def side(dy, dx):
        return ((gy + dy + 32) % 32, (gx + dx + 16) % 16)

    pair_dev = (z * 2 + other, gx)
    plane = [None] + [(gy, (gx + k) % 16) for k in range(1, 16)]

    def column(zz):
        return (zz * 2 + core, gx)

    barrier = pltpu.get_barrier_semaphore()
    peers = plane[1:] + [column((z + k) % 16) for k in range(1, 16)] + [side(dy, dx) for dy, dx in SIDES if dy != 0]
    for peer in peers:
        pl.semaphore_signal(barrier, inc=1, device_id=peer, device_id_type=MESH)

    loads = [
        pltpu.make_async_copy(cot_hbm, cot_in, w_sem.at[3]),
        pltpu.make_async_copy(level_in, level_own, w_sem.at[4]),
        pltpu.make_async_copy(wl_hbm, wl, w_sem.at[0]),
        pltpu.make_async_copy(wd_hbm, wd, w_sem.at[1]),
        pltpu.make_async_copy(wn_hbm, wn, w_sem.at[2]),
    ]
    for load in loads:
        load.start()

    def copy(src, dst, sems, k, dev):
        return pltpu.make_async_remote_copy(
            src_ref=src, dst_ref=dst, send_sem=sems.at[0, k], recv_sem=sems.at[1, k],
            device_id=dev, device_id_type=MESH,
        )

    sent = []

    def go(copies):
        for c in copies:
            c.start()
        sent.extend(copies)
        return copies

    loads[0].wait()
    lane = lax.broadcasted_iota(jnp.int32, (16, 128), 1)
    for q in range(4):
        rows = [cot_in[r, :, 128 * q:128 * q + 128].astype(F32) for r in range(4)]
        for j in range(4):
            out = pltpu.roll(rows[3], (32 * (3 - j)) % 128, 1) if j != 3 else rows[3]
            for r in (2, 1, 0):
                part = pltpu.roll(rows[r], (32 * (r - j)) % 128, 1) if r != j else rows[r]
                out = jnp.where(lane < 32 * (r + 1), part, out)
            cot_send[4 * q + j] = out.astype(BF16)
    cot_recv[gx] = cot_send[gx]

    top_ok = jnp.where(gy > 0, 1.0, 0.0).astype(F32)
    bottom_ok = jnp.where(gy < 31, 1.0, 0.0).astype(F32)
    left_ok = jnp.where(gx > 0, 1.0, 0.0).astype(F32)
    right_ok = jnp.where(gx < 15, 1.0, 0.0).astype(F32)

    loads[1].wait()
    lf[0:8] = jnp.zeros((8, 128), F32)
    lf[8 + 18 * WIDE:] = jnp.zeros((8, 128), F32)
    for r in range(8):
        start = 8 + (r + RIM) * WIDE + 16
        lf[start:start + 64] = level_own[r].astype(F32)

    pl.semaphore_wait(barrier, len(peers))

    cot_copies = go([
        copy(cot_send.at[(gx + k) % 16], cot_recv.at[gx], cot_sem, k, plane[k]) for k in range(1, 16)
    ])
    src_rows = {-1: slice(0, RIM), 0: slice(0, 8), 1: slice(8 - RIM, 8)}
    src_cols = {-1: slice(0, 16), 0: slice(0, 64), 1: slice(48, 64)}
    dst_rows = {-1: slice(RIM + 8, RIM + 8 + RIM), 0: slice(RIM, RIM + 8), 1: slice(0, RIM)}
    dst_cols = {-1: slice(80, 96), 0: slice(16, 80), 1: slice(0, 16)}
    e1 = go([
        copy(level_in.at[src_rows[dy], src_cols[dx]], lp.at[dst_rows[dy], dst_cols[dx]], e1_sem, n, side(dy, dx))
        for n, (dy, dx) in enumerate(SIDES)
    ])

    loads[2].wait()
    for ky in range(3):
        for kx in range(3):
            w = wl[2 - ky, (2 - kx) * 128:(3 - kx) * 128, :].astype(F32)
            wlt[ky, kx * 128:(kx + 1) * 128, :] = w.T.astype(BF16)

    for c in cot_copies:
        c.wait_recv()
    ct[...] = cot_recv[...].reshape(256, 128).astype(F32).T.astype(BF16).reshape(4, 32, 256)
    one_row = {-1: slice(0, 1), 0: slice(0, 4), 1: slice(3, 4)}
    half_cols = {-1: slice(0, 16), 0: slice(0, 32), 1: slice(16, 32)}

    def rim_buffer(dy, dx):
        if dx == 0:
            return hr.at[(dy + 1) // 2]
        if dy == 0:
            return hc.at[(dx + 1) // 2]
        return hx.at[(dy + 1) // 2, (dx + 1) // 2]

    ch = go([
        copy(ct.at[one_row[dy], half_cols[dx]], rim_buffer(dy, dx), ch_sem, n, side(dy, dx))
        for n, (dy, dx) in enumerate(SIDES)
    ])

    for c in e1:
        c.wait_recv()
    for r in range(18):
        row_ok = top_ok if r < RIM else bottom_ok if r >= RIM + 8 else None
        base = 8 + r * WIDE
        left = lp[r, 0:16].astype(F32) * left_ok
        right = lp[r, 80:96].astype(F32) * right_ok
        if row_ok is not None:
            left, right = left * row_ok, right * row_ok
            lf[base + 16:base + 80] = lp[r, 16:80].astype(F32) * row_ok
        lf[base:base + 16] = left
        lf[base + 80:base + 96] = right
    for r in range(18):
        for kx in range(3):
            start = 7 + kx + r * WIDE
            im_l[r * WIDE:(r + 1) * WIDE, kx * 128:(kx + 1) * 128] = lf[start:start + WIDE].astype(BF16)

    for q in range(4):
        pre = dot(im_l[4 * q * WIDE:(4 * q + 4) * WIDE], wl[0])
        for ky in (1, 2):
            pre = pre + dot(im_l[(4 * q + ky) * WIDE:(4 * q + ky + 4) * WIDE], wl[ky])
        own = lf[8 + (4 * q + 1) * WIDE:8 + (4 * q + 5) * WIDE]
        act[4 * q * WIDE:(4 * q + 4) * WIDE] = own + pre * jax.nn.sigmoid(pre)
        if q in (1, 2):
            pre_l[(q - 1) * 4 * WIDE:q * 4 * WIDE] = pre

    for rr in range(16):
        for q in range(2):
            lanes = slice(128 * (2 * (rr % 2) + q), 128 * (2 * (rr % 2) + q) + 128)
            dn[(rr // 2) * NARROW:(rr // 2 + 1) * NARROW, lanes] = act[pl.ds(rr * WIDE + q, NARROW, stride=2), :].astype(BF16)
    loads[3].wait()
    col = lax.broadcasted_iota(jnp.int32, (NARROW, 256), 0)
    col_ok = jnp.where(col < 8, left_ok, jnp.where(col >= 40, right_ok, 1.0))
    col_own = jnp.where((col >= 8) & (col < 40), 1.0, 0.0)
    nf[0:8] = jnp.zeros((8, 256), F32)
    nf[8 + 8 * NARROW:] = jnp.zeros((8, 256), F32)
    neck_in = dot(dn[...], wd[...]).astype(BF16).astype(F32)
    for r in range(8):
        row = neck_in[r * NARROW:(r + 1) * NARROW] * col_ok
        if r < 2:
            row = row * top_ok
        if r >= 6:
            row = row * bottom_ok
        nf[8 + r * NARROW:8 + (r + 1) * NARROW] = row
    for kx in range(3):
        im_n[:, kx * 256:(kx + 1) * 256] = nf[7 + kx:7 + kx + 8 * NARROW].astype(BF16)
    loads[4].wait()
    neck_pre = dot(im_n[0:6 * NARROW], wn[0])
    for ky in (1, 2):
        neck_pre = neck_pre + dot(im_n[ky * NARROW:(ky + 6) * NARROW], wn[ky])

    for c in ch:
        c.wait_recv()
    for r in range(6):
        if 1 <= r <= 4:
            mid = ct[r - 1].astype(F32)
            left = hc[1, r - 1, 8:16].astype(F32) * left_ok
            right = hc[0, r - 1, 0:8].astype(F32) * right_ok
        else:
            n, ok = (1, top_ok) if r == 0 else (0, bottom_ok)
            mid = hr[n, 0].astype(F32) * ok
            left = hx[n, 1, 0, 8:16].astype(F32) * (left_ok * ok)
            right = hx[n, 0, 0, 0:8].astype(F32) * (right_ok * ok)
        base = r * NARROW
        cf[base:base + 8] = left
        cf[base + 8:base + 40] = mid
        cf[base + 40:base + 48] = right

    gate = (cf[...] * slope_of(neck_pre)).astype(BF16).astype(F32)
    gf[0:8] = jnp.zeros((8, 256), F32)
    gf[8 + 6 * NARROW:] = jnp.zeros((8, 256), F32)
    gf[8:8 + 6 * NARROW] = gate
    for r in range(4):
        gate_own[r * NARROW:(r + 1) * NARROW] = (gate[(r + 1) * NARROW:(r + 2) * NARROW] * col_own).astype(BF16)

    def half_lanes(half):
        return pl.ds(pl.multiple_of(half * 128, 128), 128)

    theirs = gate_own[:, half_lanes(other)]
    for ky in range(3):
        part = dot_tn(im_n[(1 + ky) * NARROW:(5 + ky) * NARROW], theirs)
        a_pair_s[48 * ky:48 * ky + 48] = part.astype(BF16).reshape(48, 16, 128)
    a_pair = go([copy(a_pair_s, a_pair_r, pair_sem, 0, pair_dev)])
    mine = gate_own[:, half_lanes(core)]
    for ky in range(3):
        neck_own[48 * ky:48 * ky + 48] = dot_tn(im_n[(1 + ky) * NARROW:(5 + ky) * NARROW], mine).reshape(48, 16, 128)

    rows = []
    for r in range(4):
        v = neck_pre[(r + 1) * NARROW + 8:(r + 1) * NARROW + 40]
        rows.append(nf[8 + (r + 2) * NARROW + 8:8 + (r + 2) * NARROW + 40] + v * jax.nn.sigmoid(v))
    no_send[...] = jnp.concatenate(rows, axis=0).T.astype(BF16).reshape(16, 16, 128)
    no_recv[gx] = no_send[gx]
    no_copies = go([copy(no_send.at[(gx + k) % 16], no_recv.at[gx], no_sem, k, plane[k]) for k in range(1, 16)])

    for kx in range(3):
        im_g[:, kx * 256:(kx + 1) * 256] = gf[7 + kx:7 + kx + 6 * NARROW].astype(BF16)
    back = None
    for ky in range(3):
        for kx in range(3):
            term = dot_nt(
                im_g[ky * NARROW:(ky + 4) * NARROW, kx * 256:(kx + 1) * 256],
                wn[2 - ky, (2 - kx) * 256:(3 - kx) * 256, :],
            )
            back = term if back is None else back + term
    for r in range(4):
        v = cf[(r + 1) * NARROW:(r + 2) * NARROW] + back[r * NARROW:(r + 1) * NARROW]
        ng[r * NARROW:(r + 1) * NARROW] = (v * col_own).astype(BF16)
    spread = dot_nt(ng[...], wd[...])
    for r in range(4):
        for p in range(2):
            for q in range(2):
                lanes = slice(128 * (2 * p + q), 128 * (2 * p + q) + 128)
                lbf[pl.ds((2 * r + p) * WIDE + q, NARROW, stride=2), :] = spread[r * NARROW:(r + 1) * NARROW, lanes]
    for r in range(8):
        rows_r = slice(r * WIDE + 16, r * WIDE + 80)
        gp[r + 1, 16:80] = (lbf[rows_r] * slope_of(pre_l[rows_r])).astype(BF16)
    e4_src = {-1: slice(1, 2), 0: slice(1, 9), 1: slice(8, 9)}
    e4_dst = {-1: slice(9, 10), 0: slice(1, 9), 1: slice(0, 1)}
    e4_scol = {-1: slice(16, 32), 0: slice(16, 80), 1: slice(64, 80)}
    e4 = go([
        copy(gp.at[e4_src[dy], e4_scol[dx]], gp.at[e4_dst[dy], dst_cols[dx]], e4_sem, n, side(dy, dx))
        for n, (dy, dx) in enumerate(SIDES)
    ])

    own_gate = gp[1:9, 16:80].reshape(512, 128)
    for ky in range(3):
        window = jnp.concatenate(
            [im_l[(4 + ky + r) * WIDE + 16:(4 + ky + r) * WIDE + 80] for r in range(8)], axis=0
        )
        level_acc[ky * 384:(ky + 1) * 384] = dot_tn(window, own_gate)
    down_acc[...] = dot_tn(dn[2 * NARROW:6 * NARROW], ng[...])

    def rest_terms(half):
        down = down_acc[:, half_lanes(half)].reshape(16, 2, 16, 128)
        level = level_acc[pl.ds(pl.multiple_of(half * 576, 576), 576), :].reshape(LEVEL_OWNERS, 3, 16, 128)
        return down, level

    down, level = rest_terms(other)
    nothing = jnp.zeros((16 - LEVEL_OWNERS, 3, 16, 128), BF16)
    b_pair_s[:, 0:2] = down.astype(BF16)
    b_pair_s[0:LEVEL_OWNERS, 2:5] = level.astype(BF16)
    b_pair_s[LEVEL_OWNERS:, 2:5] = nothing
    b_pair = go([copy(b_pair_s, b_pair_r, pair_sem, 1, pair_dev)])

    def plane_stage(work, buf, sems, first):
        return go([copy(work(( gx + k) % 16), buf.at[k], sems, first + k, plane[k]) for k in range(1, 16)])

    def a_piece_of(o):
        return a_work.at[pl.ds(o * NECK_TILES, NECK_TILES)]

    def b_piece_of(o):
        return b_work.at[o]

    a_pair[0].wait_recv()
    for n in range(16):
        part = slice(n * NECK_TILES, (n + 1) * NECK_TILES)
        a_work[part] = (neck_own[part] + a_pair_r[part].astype(F32)).astype(BF16)
    a_plane = plane_stage(a_piece_of, a_xy, xy_sem, 0)

    b_pair[0].wait_recv()
    down, level = rest_terms(core)
    b_work[:, 0:2] = (down + b_pair_r[:, 0:2].astype(F32)).astype(BF16)
    b_work[0:LEVEL_OWNERS, 2:5] = (level + b_pair_r[0:LEVEL_OWNERS, 2:5].astype(F32)).astype(BF16)
    b_work[LEVEL_OWNERS:, 2:5] = nothing
    b_plane = plane_stage(b_piece_of, b_xy, xy_sem, 16)

    for c in e4:
        c.wait_recv()
    g2f[0:8] = jnp.zeros((8, 128), F32)
    g2f[8 + 10 * WIDE:] = jnp.zeros((8, 128), F32)
    for r in range(10):
        row_ok = top_ok if r == 0 else bottom_ok if r == 9 else None
        base = 8 + r * WIDE
        left, mid, right = gp[r, 0:16].astype(F32) * left_ok, gp[r, 16:80].astype(F32), gp[r, 80:96].astype(F32) * right_ok
        if row_ok is not None:
            left, mid, right = left * row_ok, mid * row_ok, right * row_ok
        g2f[base:base + 16] = left
        g2f[base + 16:base + 80] = mid
        g2f[base + 80:base + 96] = right
    for r in range(10):
        for kx in range(3):
            start = 7 + kx + r * WIDE
            im_b[r * WIDE:(r + 1) * WIDE, kx * 128:(kx + 1) * 128] = g2f[start:start + WIDE].astype(BF16)
    for q in range(2):
        total = lbf[4 * q * WIDE:(4 * q + 4) * WIDE]
        for ky in range(3):
            total = total + dot(im_b[(4 * q + ky) * WIDE:(4 * q + ky + 4) * WIDE], wlt[ky])
        grad_input[4 * q:4 * q + 4] = total.reshape(4, WIDE, 128)[:, 16:80].astype(BF16)

    for c in no_copies:
        c.wait_recv()
    for q in range(4):
        pieces = [no_recv[4 * q + j].astype(F32) for j in range(4)]
        for r in range(4):
            out = pltpu.roll(pieces[3], (32 * (3 - r)) % 128, 1) if r != 3 else pieces[3]
            for j in (2, 1, 0):
                part = pltpu.roll(pieces[j], (32 * (j - r)) % 128, 1) if r != j else pieces[j]
                out = jnp.where(lane < 32 * (j + 1), part, out)
            neck_out[r, :, 128 * q:128 * q + 128] = out.astype(BF16)

    def z_send(piece, buf, tiles, first, sems, offset):
        copies = []
        for t in range(tiles):
            c = copy_z(piece.at[t], buf.at[z], sems, offset + t, offset + z, column(first + t))
            copies.append((z != first + t, c))
        return copies

    def copy_z(src, dst, sems, ks, kr, dev):
        return pltpu.make_async_remote_copy(
            src_ref=src, dst_ref=dst, send_sem=sems.at[0, ks], recv_sem=sems.at[1, kr],
            device_id=dev, device_id_type=MESH,
        )

    def start_all(copies):
        for cond, c in copies:
            pl.when(cond)(c.start)

    def plane_sum(piece_of, buf, own_ref, copies, out):
        for c in copies:
            c.wait_recv()
        total = own_ref[...].astype(F32)
        for k in range(1, 16):
            total = total + buf[k].astype(F32)
        out[...] = total.astype(BF16)

    def owns(first, tiles):
        return (z >= first) & (z < first + tiles)

    def z_sum(piece, buf, fin, tiles, first, sems, offset, scale):
        @pl.when(owns(first, tiles))
        def _():
            mine = z - first
            for s in range(16):
                @pl.when(z != s)
                def _(s=s):
                    copy_z(piece.at[0], buf.at[s], sems, offset, offset + s, column(s)).wait_recv()
            buf[z] = piece[mine]
            total = buf[0].astype(F32)
            for s in range(1, 16):
                total = total + buf[s].astype(F32)
            fin[mine] = (total * scale).astype(BF16)
            for s in range(16):
                @pl.when(z != s)
                def _(s=s):
                    copy_z(fin.at[mine], fin.at[mine], zb_sem, offset + s, offset + mine, column(s)).start()

    def z_back(fin, tiles, first, offset):
        for t in range(tiles):
            @pl.when(z != first + t)
            def _(t=t):
                copy_z(fin.at[t], fin.at[t], zb_sem, offset, offset + t, column(first + t)).wait_recv()

    def z_back_sent(fin, tiles, first, offset):
        @pl.when(owns(first, tiles))
        def _():
            for s in range(16):
                @pl.when(z != s)
                def _(s=s):
                    copy_z(fin.at[0], fin.at[0], zb_sem, offset + s, offset, column(s)).wait_send()

    plane_sum(a_piece_of, a_xy, a_piece_of(gx), a_plane, a_piece)
    a_zs = z_send(a_piece, a_z, NECK_TILES, 0, z_sem, 0)
    start_all(a_zs)
    plane_sum(b_piece_of, b_xy, b_piece_of(gx), b_plane, b_piece)
    b_zs = z_send(b_piece, b_z, REST_TILES, NECK_TILES, z_sem, 16)
    start_all(b_zs)
    z_sum(a_piece, a_z, a_fin, NECK_TILES, 0, z_sem, 0, scales[0])
    z_sum(b_piece, b_z, b_fin, REST_TILES, NECK_TILES, z_sem, 16, jnp.where(z < NECK_TILES + 2, scales[0], scales[1]))

    z_back(a_fin, NECK_TILES, 0, 0)
    def a_slot(o):
        return a_all.at[core, pl.ds(o * NECK_TILES, NECK_TILES)]

    def b_slot(o):
        return b_all.at[core, o]

    a_all[core, pl.ds(gx * NECK_TILES, NECK_TILES)] = a_fin[...]
    a_mine = a_slot(gx)
    a_back = go([copy(a_mine, a_mine, xyb_sem, k, plane[k]) for k in range(1, 16)])
    z_back(b_fin, REST_TILES, NECK_TILES, 16)
    b_all[core, gx] = b_fin[...]
    b_mine = b_all.at[core, gx]
    b_back = go([copy(b_mine, b_mine, xyb_sem, 16 + k, plane[k]) for k in range(1, 16)])

    def landed(slot_of, sems, first):
        for k in range(1, 16):
            slot = slot_of((gx + 16 - k) % 16)
            copy(slot, slot, sems, first + k, plane[k]).wait_recv()

    landed(a_slot, xyb_sem, 0)
    go([copy(a_all.at[core], a_all.at[core], pair_sem, 2, pair_dev)])
    landed(b_slot, xyb_sem, 16)
    go([copy(b_all.at[core], b_all.at[core], pair_sem, 3, pair_dev)])
    copy(a_all.at[other], a_all.at[other], pair_sem, 2, pair_dev).wait_recv()
    copy(b_all.at[other], b_all.at[other], pair_sem, 3, pair_dev).wait_recv()

    for c in sent:
        c.wait_send()
    for cond, c in a_zs + b_zs:
        pl.when(cond)(c.wait_send)
    z_back_sent(a_fin, NECK_TILES, 0, 0)
    z_back_sent(b_fin, REST_TILES, NECK_TILES, 16)


def results_kernel(strip, level, a_all, b_all, neck_out, grad_input, grad_level, grad_down, grad_neck, sems):
    copies = [(strip, neck_out), (level, grad_input)]
    for half in range(2):
        lanes = slice(128 * half, 128 * half + 128)
        copies.append((a_all.at[half], grad_neck.at[:, :, lanes]))
        copies.append((b_all.at[half, :, 0:2], grad_down.at[:, :, :, lanes]))
        copies.append((b_all.at[half, 0:LEVEL_OWNERS, 2:5], grad_level.at[half]))
    copies = [pltpu.make_async_copy(src, dst, sems.at[n]) for n, (src, dst) in enumerate(copies)]
    for c in copies:
        c.start()
    for c in copies:
        c.wait()


def local(level_in, w_level, w_down, w_neck, cotangent):
    device_count = lax.axis_size("gy") * lax.axis_size("gx")
    level_count = level_in.shape[0] * level_in.shape[1] * device_count
    level_scale = 1.0 / math.sqrt(level_count)
    neck_scale = 1.0 / math.sqrt(level_count // 4)
    vmem = pl.BlockSpec(memory_space=pltpu.VMEM)
    hbm = pl.BlockSpec(memory_space=pltpu.HBM)
    dma = pltpu.SemaphoreType.DMA

    def v(*shape, dtype=BF16):
        return pltpu.VMEM(shape, dtype)

    def group(tiles, flat):
        whole = (16 * tiles, 16, 128) if flat else (16, tiles, 16, 128)
        return [
            v(*whole), v(*whole), v(*whole), v(16, tiles, 16, 128), v(tiles, 16, 128), v(16, 16, 128), v(tiles, 16, 128),
        ]

    outs = pl.pallas_call(
        functools.partial(kernel, (neck_scale, level_scale)),
        out_shape=[
            jax.ShapeDtypeStruct((4, 16, 512), BF16),
            jax.ShapeDtypeStruct((8, 64, 128), BF16),
            jax.ShapeDtypeStruct((2, 16 * NECK_TILES, 16, 128), BF16),
            jax.ShapeDtypeStruct((2, 16, REST_TILES, 16, 128), BF16),
        ],
        in_specs=[hbm] * 5,
        out_specs=[vmem] * 4,
        scratch_shapes=[
            v(8, 64, 128), v(4, 16, 512),
            v(3, 384, 128), v(512, 256), v(3, 768, 256), v(3, 384, 128),
            v(18, WIDE, 128), v(16 + 18 * WIDE, 128, dtype=F32), v(18 * WIDE, 384),
            v(8 * WIDE, 128, dtype=F32), v(16 * WIDE, 128, dtype=F32), v(8 * NARROW, 512),
            v(16 + 8 * NARROW, 256, dtype=F32), v(8 * NARROW, 768),
            v(6 * NARROW, 256, dtype=F32), v(16 + 6 * NARROW, 256, dtype=F32), v(6 * NARROW, 768),
            v(4 * NARROW, 256), v(4 * NARROW, 256), v(8 * WIDE, 128, dtype=F32),
            v(10, WIDE, 128), v(16 + 10 * WIDE, 128, dtype=F32), v(10 * WIDE, 384),
            v(16, 16, 128), v(16, 16, 128), v(4, 32, 256), v(2, 1, 32, 256), v(2, 4, 16, 256), v(2, 2, 1, 16, 256),
            v(16, 16, 128), v(16, 16, 128),
            v(144, 16, 128, dtype=F32), v(1152, 128, dtype=F32), v(512, 256, dtype=F32),
            *group(NECK_TILES, True), *group(REST_TILES, False),
            dma((5,)), dma((2, 8)), dma((2, 16)), dma((2, 8)), dma((2, 16)), dma((2, 8)),
            dma((2, 4)), dma((2, 32)), dma((2, 32)), dma((2, 32)), dma((2, 32)),
        ],
        compiler_params=pltpu.CompilerParams(
            collective_id=0, has_side_effects=True, vmem_limit_bytes=24 * 1024 * 1024
        ),
    )(
        *(pltpu.with_memory_space_constraint(t, pltpu.HBM) for t in (
            level_in,
            w_level.reshape(3, 384, 128),
            w_down.reshape(512, 256),
            w_neck.reshape(3, 768, 256),
            jnp.transpose(cotangent, (0, 2, 1)),
        ))
    )
    outs = pl.pallas_call(
        results_kernel,
        out_shape=[
            jax.ShapeDtypeStruct((4, 16, 512), BF16),
            jax.ShapeDtypeStruct((8, 64, 128), BF16),
            jax.ShapeDtypeStruct((2, LEVEL_OWNERS, 3, 16, 128), BF16),
            jax.ShapeDtypeStruct((16, 2, 16, 256), BF16),
            jax.ShapeDtypeStruct((144, 16, 256), BF16),
        ],
        in_specs=[vmem] * 4,
        out_specs=[hbm] * 5,
        scratch_shapes=[dma((8,))],
        compiler_params=pltpu.CompilerParams(vmem_limit_bytes=1024 * 1024),
    )(*outs)
    return (
        jnp.transpose(outs[0], (0, 2, 1)),
        outs[1],
        outs[2].reshape(w_level.shape),
        outs[3].reshape(w_down.shape),
        outs[4].reshape(w_neck.shape),
    )


def solution(mesh):
    return jax.shard_map(
        local,
        mesh=mesh,
        in_specs=(P("gy", "gx", None), P(), P(), P(), P("gy", None, "gx")),
        out_specs=(P("gy", None, "gx"), P("gy", "gx", None), P(), P(), P()),
        check_vma=False,
    )
```

```python
import functools
import math

import jax
import jax.numpy as jnp
from jax import lax
from jax.experimental import pallas as pl
from jax.experimental.pallas import tpu as pltpu
from jax.sharding import PartitionSpec as P

MESH = pl.DeviceIdType.MESH
BF16, F32 = jnp.bfloat16, jnp.float32

RIM = 5
WIDE = 96
NARROW = 48
SIDES = [(dy, dx) for dy in (-1, 0, 1) for dx in (-1, 0, 1) if (dy, dx) != (0, 0)]
FAR_FIRST = sorted(range(1, 16), key=lambda k: -(min(k // 4, 4 - k // 4) + min(k % 4, 4 - k % 4)))
Z_FAR_FIRST = sorted(range(1, 16), key=lambda k: -min(k, 16 - k))
NECK_TILES = 9
REST_TILES = 5
LEVEL_OWNERS = 12


def slope_of(v):
    s = jax.nn.sigmoid(v)
    return s + v * s * (1.0 - s)


def dot(a, b):
    return jnp.dot(a, b, preferred_element_type=F32)


def dot_nt(a, b):
    return lax.dot_general(a, b, (((1,), (1,)), ((), ())), preferred_element_type=F32)


def dot_tn(a, b):
    return lax.dot_general(a, b, (((0,), (0,)), ((), ())), preferred_element_type=F32)


def kernel(
    scales,
    level_in, wl_hbm, wd_hbm, wn_hbm, cot_hbm,
    neck_out, grad_input, a_all, b_all,
    level_own, cot_in, wl, wd, wn, wlt,
    lp, lf, im_l, pre_l, act, dn, nf, im_n, cf, gf, im_g, gate_own, ng, lbf, gp, g2f, im_b,
    cot_send, cot_recv, ct, hr, no_send, no_recv,
    neck_own, level_acc, down_acc,
    a_pair_s, a_pair_r, a_work, a_xy, a_piece, a_z, a_fin,
    b_pair_s, b_pair_r, b_work, b_xy, b_piece, b_z, b_fin,
    w_sem, e1_sem, cot_sem, ch_sem, no_sem, e4_sem,
    pair_sem, xy_sem, z_sem, zb_sem, xyb_sem,
):
    gy, gx = lax.axis_index("gy"), lax.axis_index("gx")
    z, core = gy // 2, gy % 2
    other = 1 - core

    def side(dy, dx):
        return ((gy + dy + 32) % 32, (gx + dx + 16) % 16)

    pair_dev = (z * 2 + other, gx)
    x, y = gx // 4, gx % 4

    def in_plane(k, sign=1):
        return ((x + sign * (k // 4) + 4) % 4) * 4 + (y + sign * (k % 4) + 4) % 4

    plane = [None] + [(gy, in_plane(k)) for k in range(1, 16)]

    def column(zz):
        return (zz * 2 + core, gx)

    barrier = pltpu.get_barrier_semaphore()
    peers = plane[1:] + [column((z + k) % 16) for k in range(1, 16)] + [side(dy, dx) for dy, dx in SIDES if dy != 0]
    for peer in peers:
        pl.semaphore_signal(barrier, inc=1, device_id=peer, device_id_type=MESH)

    loads = [
        pltpu.make_async_copy(cot_hbm, cot_in, w_sem.at[3]),
        pltpu.make_async_copy(level_in, level_own, w_sem.at[4]),
        pltpu.make_async_copy(wl_hbm, wl, w_sem.at[0]),
        pltpu.make_async_copy(wd_hbm, wd, w_sem.at[1]),
        pltpu.make_async_copy(wn_hbm, wn, w_sem.at[2]),
    ]
    for load in loads[:2]:
        load.start()

    def copy(src, dst, sems, k, dev):
        return pltpu.make_async_remote_copy(
            src_ref=src, dst_ref=dst, send_sem=sems.at[0, k], recv_sem=sems.at[1, k],
            device_id=dev, device_id_type=MESH,
        )

    sent = []

    def go(copies):
        for c in copies:
            c.start()
        sent.extend(copies)
        return copies

    loads[0].wait()
    for load in loads[2:]:
        load.start()
    lane = lax.broadcasted_iota(jnp.int32, (16, 128), 1)
    for q in range(4):
        rows = [cot_in[r, :, 128 * q:128 * q + 128].astype(F32) for r in range(4)]
        for j in range(4):
            out = pltpu.roll(rows[3], (32 * (3 - j)) % 128, 1) if j != 3 else rows[3]
            for r in (2, 1, 0):
                part = pltpu.roll(rows[r], (32 * (r - j)) % 128, 1) if r != j else rows[r]
                out = jnp.where(lane < 32 * (r + 1), part, out)
            cot_send[4 * q + j, 0] = out.astype(BF16)
    for t in range(16):
        cot_send[t, 1] = jnp.where(lane % 32 < 16, cot_send[(t + 1) % 16, 0].astype(F32), cot_send[(t + 15) % 16, 0].astype(F32)).astype(BF16)
    cot_recv[gx] = cot_send[gx]

    top_ok = jnp.where(gy > 0, 1.0, 0.0).astype(F32)
    bottom_ok = jnp.where(gy < 31, 1.0, 0.0).astype(F32)
    left_ok = jnp.where(gx > 0, 1.0, 0.0).astype(F32)
    right_ok = jnp.where(gx < 15, 1.0, 0.0).astype(F32)

    loads[1].wait()
    lf[0:8] = jnp.zeros((8, 128), F32)
    lf[8 + 18 * WIDE:] = jnp.zeros((8, 128), F32)
    for r in range(8):
        start = 8 + (r + RIM) * WIDE + 16
        lf[start:start + 64] = level_own[r].astype(F32)

    pl.semaphore_wait(barrier, len(peers))

    cot_copies = go([
        copy(cot_send.at[in_plane(k)], cot_recv.at[gx], cot_sem, k, plane[k]) for k in FAR_FIRST
    ])
    src_rows = {-1: slice(0, RIM), 0: slice(0, 8), 1: slice(8 - RIM, 8)}
    src_cols = {-1: slice(0, 16), 0: slice(0, 64), 1: slice(48, 64)}
    dst_rows = {-1: slice(RIM + 8, RIM + 8 + RIM), 0: slice(RIM, RIM + 8), 1: slice(0, RIM)}
    dst_cols = {-1: slice(80, 96), 0: slice(16, 80), 1: slice(0, 16)}
    e1 = go([
        copy(level_own.at[src_rows[dy], src_cols[dx]], lp.at[dst_rows[dy], dst_cols[dx]], e1_sem, n, side(dy, dx))
        for n, (dy, dx) in enumerate(SIDES)
    ])

    loads[2].wait()
    for ky in range(3):
        for kx in range(3):
            w = wl[2 - ky, (2 - kx) * 128:(3 - kx) * 128, :].astype(F32)
            wlt[ky, kx * 128:(kx + 1) * 128, :] = w.T.astype(BF16)

    for c in cot_copies:
        c.wait_recv()
    cot_tile = cot_recv[:, 0].reshape(256, 128).astype(F32).T
    cot_beside = cot_recv[:, 1].reshape(256, 128).astype(F32).T
    for r in range(4):
        base = (r + 1) * NARROW
        cf[base:base + 8] = cot_beside[32 * r + 24:32 * r + 32] * left_ok
        cf[base + 8:base + 40] = cot_tile[32 * r:32 * r + 32]
        cf[base + 40:base + 48] = cot_beside[32 * r:32 * r + 8] * right_ok
    ct[0] = cf[NARROW:2 * NARROW].astype(BF16)
    ct[1] = cf[4 * NARROW:5 * NARROW].astype(BF16)
    ch = go([copy(ct.at[n], hr.at[n], ch_sem, n, side(2 * n - 1, 0)) for n in range(2)])

    for c in e1:
        c.wait_recv()
    for r in range(18):
        row_ok = top_ok if r < RIM else bottom_ok if r >= RIM + 8 else None
        base = 8 + r * WIDE
        left = lp[r, 0:16].astype(F32) * left_ok
        right = lp[r, 80:96].astype(F32) * right_ok
        if row_ok is not None:
            left, right = left * row_ok, right * row_ok
            lf[base + 16:base + 80] = lp[r, 16:80].astype(F32) * row_ok
        lf[base:base + 16] = left
        lf[base + 80:base + 96] = right
    for r in range(18):
        for kx in range(3):
            start = 7 + kx + r * WIDE
            im_l[r * WIDE:(r + 1) * WIDE, kx * 128:(kx + 1) * 128] = lf[start:start + WIDE].astype(BF16)

    for q in range(4):
        pre = dot(im_l[4 * q * WIDE:(4 * q + 4) * WIDE], wl[0])
        for ky in (1, 2):
            pre = pre + dot(im_l[(4 * q + ky) * WIDE:(4 * q + ky + 4) * WIDE], wl[ky])
        own = lf[8 + (4 * q + 1) * WIDE:8 + (4 * q + 5) * WIDE]
        act[4 * q * WIDE:(4 * q + 4) * WIDE] = own + pre * jax.nn.sigmoid(pre)
        if q in (1, 2):
            pre_l[(q - 1) * 4 * WIDE:q * 4 * WIDE] = pre

    for rr in range(16):
        for q in range(2):
            lanes = slice(128 * (2 * (rr % 2) + q), 128 * (2 * (rr % 2) + q) + 128)
            dn[(rr // 2) * NARROW:(rr // 2 + 1) * NARROW, lanes] = act[pl.ds(rr * WIDE + q, NARROW, stride=2), :].astype(BF16)
    loads[3].wait()
    col = lax.broadcasted_iota(jnp.int32, (NARROW, 256), 0)
    col_ok = jnp.where(col < 8, left_ok, jnp.where(col >= 40, right_ok, 1.0))
    col_own = jnp.where((col >= 8) & (col < 40), 1.0, 0.0)
    nf[0:8] = jnp.zeros((8, 256), F32)
    nf[8 + 8 * NARROW:] = jnp.zeros((8, 256), F32)
    neck_in = dot(dn[...], wd[...]).astype(BF16).astype(F32)
    for r in range(8):
        row = neck_in[r * NARROW:(r + 1) * NARROW] * col_ok
        if r < 2:
            row = row * top_ok
        if r >= 6:
            row = row * bottom_ok
        nf[8 + r * NARROW:8 + (r + 1) * NARROW] = row
    for kx in range(3):
        im_n[:, kx * 256:(kx + 1) * 256] = nf[7 + kx:7 + kx + 8 * NARROW].astype(BF16)
    loads[4].wait()
    neck_pre = dot(im_n[0:6 * NARROW], wn[0])
    for ky in (1, 2):
        neck_pre = neck_pre + dot(im_n[ky * NARROW:(ky + 6) * NARROW], wn[ky])

    own = slice(NARROW, 5 * NARROW)
    gf[0:8] = jnp.zeros((8, 256), F32)
    gf[8 + 6 * NARROW:] = jnp.zeros((8, 256), F32)
    gate = (cf[own] * slope_of(neck_pre[own])).astype(BF16).astype(F32)
    gf[8 + NARROW:8 + 5 * NARROW] = gate
    for r in range(4):
        gate_own[r * NARROW:(r + 1) * NARROW] = (gate[r * NARROW:(r + 1) * NARROW] * col_own).astype(BF16)

    def half_lanes(half):
        return pl.ds(pl.multiple_of(half * 128, 128), 128)

    theirs = gate_own[:, half_lanes(other)]
    for ky in range(3):
        part = dot_tn(im_n[(1 + ky) * NARROW:(5 + ky) * NARROW], theirs)
        a_pair_s[48 * ky:48 * ky + 48] = part.astype(BF16).reshape(48, 16, 128)
    a_pair = go([copy(a_pair_s, a_pair_r, pair_sem, 0, pair_dev)])
    mine = gate_own[:, half_lanes(core)]
    for ky in range(3):
        neck_own[48 * ky:48 * ky + 48] = dot_tn(im_n[(1 + ky) * NARROW:(5 + ky) * NARROW], mine).reshape(48, 16, 128)

    def plane_stage(work, buf, sems, first):
        return go([copy(work(in_plane(k)), buf.at[k], sems, first + k, plane[k]) for k in FAR_FIRST])

    def a_piece_of(o):
        return a_work.at[pl.ds(o * NECK_TILES, NECK_TILES)]

    def b_piece_of(o):
        return b_work.at[o]

    a_pair[0].wait_recv()
    for n in range(16):
        part = slice(n * NECK_TILES, (n + 1) * NECK_TILES)
        a_work[part] = (neck_own[part] + a_pair_r[part].astype(F32)).astype(BF16)
    a_plane = plane_stage(a_piece_of, a_xy, xy_sem, 0)

    rows = []
    for r in range(4):
        v = neck_pre[(r + 1) * NARROW + 8:(r + 1) * NARROW + 40]
        rows.append(nf[8 + (r + 2) * NARROW + 8:8 + (r + 2) * NARROW + 40] + v * jax.nn.sigmoid(v))
    no_send[...] = jnp.concatenate(rows, axis=0).T.astype(BF16).reshape(16, 16, 128)
    no_recv[gx] = no_send[gx]
    no_copies = go([copy(no_send.at[in_plane(k)], no_recv.at[gx], no_sem, k, plane[k]) for k in FAR_FIRST])

    for c in ch:
        c.wait_recv()
    for n, ok, rows in ((1, top_ok, slice(0, NARROW)), (0, bottom_ok, slice(5 * NARROW, 6 * NARROW))):
        v = hr[n].astype(F32) * ok * slope_of(neck_pre[rows])
        gf[8 + rows.start:8 + rows.stop] = v.astype(BF16).astype(F32)

    for kx in range(3):
        im_g[:, kx * 256:(kx + 1) * 256] = gf[7 + kx:7 + kx + 6 * NARROW].astype(BF16)
    back = None
    for ky in range(3):
        for kx in range(3):
            term = dot_nt(
                im_g[ky * NARROW:(ky + 4) * NARROW, kx * 256:(kx + 1) * 256],
                wn[2 - ky, (2 - kx) * 256:(3 - kx) * 256, :],
            )
            back = term if back is None else back + term
    for r in range(4):
        v = cf[(r + 1) * NARROW:(r + 2) * NARROW] + back[r * NARROW:(r + 1) * NARROW]
        ng[r * NARROW:(r + 1) * NARROW] = (v * col_own).astype(BF16)
    spread = dot_nt(ng[...], wd[...])
    for r in range(4):
        for p in range(2):
            for q in range(2):
                lanes = slice(128 * (2 * p + q), 128 * (2 * p + q) + 128)
                lbf[pl.ds((2 * r + p) * WIDE + q, NARROW, stride=2), :] = spread[r * NARROW:(r + 1) * NARROW, lanes]
    for r in range(8):
        rows_r = slice(r * WIDE + 16, r * WIDE + 80)
        gp[r + 1, 16:80] = (lbf[rows_r] * slope_of(pre_l[rows_r])).astype(BF16)
    e4_src = {-1: slice(1, 2), 0: slice(1, 9), 1: slice(8, 9)}
    e4_dst = {-1: slice(9, 10), 0: slice(1, 9), 1: slice(0, 1)}
    e4_scol = {-1: slice(16, 32), 0: slice(16, 80), 1: slice(64, 80)}
    e4 = go([
        copy(gp.at[e4_src[dy], e4_scol[dx]], gp.at[e4_dst[dy], dst_cols[dx]], e4_sem, n, side(dy, dx))
        for n, (dy, dx) in enumerate(SIDES)
    ])

    own_gate = gp[1:9, 16:80].reshape(512, 128)
    for ky in range(3):
        window = jnp.concatenate(
            [im_l[(4 + ky + r) * WIDE + 16:(4 + ky + r) * WIDE + 80] for r in range(8)], axis=0
        )
        level_acc[ky * 384:(ky + 1) * 384] = dot_tn(window, own_gate)
    down_acc[...] = dot_tn(dn[2 * NARROW:6 * NARROW], ng[...])

    def rest_terms(half):
        down = down_acc[:, half_lanes(half)].reshape(16, 2, 16, 128)
        level = level_acc[pl.ds(pl.multiple_of(half * 576, 576), 576), :].reshape(LEVEL_OWNERS, 3, 16, 128)
        return down, level

    down, level = rest_terms(other)
    nothing = jnp.zeros((16 - LEVEL_OWNERS, 3, 16, 128), BF16)
    b_pair_s[:, 0:2] = down.astype(BF16)
    b_pair_s[0:LEVEL_OWNERS, 2:5] = level.astype(BF16)
    b_pair_s[LEVEL_OWNERS:, 2:5] = nothing
    b_pair = go([copy(b_pair_s, b_pair_r, pair_sem, 1, pair_dev)])

    b_pair[0].wait_recv()
    down, level = rest_terms(core)
    b_work[:, 0:2] = (down + b_pair_r[:, 0:2].astype(F32)).astype(BF16)
    b_work[0:LEVEL_OWNERS, 2:5] = (level + b_pair_r[0:LEVEL_OWNERS, 2:5].astype(F32)).astype(BF16)
    b_work[LEVEL_OWNERS:, 2:5] = nothing
    b_plane = plane_stage(b_piece_of, b_xy, xy_sem, 16)

    for c in e4:
        c.wait_recv()
    g2f[0:8] = jnp.zeros((8, 128), F32)
    g2f[8 + 10 * WIDE:] = jnp.zeros((8, 128), F32)
    for r in range(10):
        row_ok = top_ok if r == 0 else bottom_ok if r == 9 else None
        base = 8 + r * WIDE
        left, mid, right = gp[r, 0:16].astype(F32) * left_ok, gp[r, 16:80].astype(F32), gp[r, 80:96].astype(F32) * right_ok
        if row_ok is not None:
            left, mid, right = left * row_ok, mid * row_ok, right * row_ok
        g2f[base:base + 16] = left
        g2f[base + 16:base + 80] = mid
        g2f[base + 80:base + 96] = right
    for r in range(10):
        for kx in range(3):
            start = 7 + kx + r * WIDE
            im_b[r * WIDE:(r + 1) * WIDE, kx * 128:(kx + 1) * 128] = g2f[start:start + WIDE].astype(BF16)
    for q in range(2):
        total = lbf[4 * q * WIDE:(4 * q + 4) * WIDE]
        for ky in range(3):
            total = total + dot(im_b[(4 * q + ky) * WIDE:(4 * q + ky + 4) * WIDE], wlt[ky])
        grad_input[4 * q:4 * q + 4] = total.reshape(4, WIDE, 128)[:, 16:80].astype(BF16)

    for c in no_copies:
        c.wait_recv()
    for q in range(4):
        pieces = [no_recv[4 * q + j].astype(F32) for j in range(4)]
        for r in range(4):
            out = pltpu.roll(pieces[3], (32 * (3 - r)) % 128, 1) if r != 3 else pieces[3]
            for j in (2, 1, 0):
                part = pltpu.roll(pieces[j], (32 * (j - r)) % 128, 1) if r != j else pieces[j]
                out = jnp.where(lane < 32 * (j + 1), part, out)
            neck_out[r, :, 128 * q:128 * q + 128] = out.astype(BF16)

    def z_send(piece, buf, tiles, first, sems, offset):
        copies = []
        for t in range(tiles):
            c = copy_z(piece.at[t], buf.at[z], sems, offset + t, offset + z, column(first + t))
            copies.append((z != first + t, c))
        return copies

    def copy_z(src, dst, sems, ks, kr, dev):
        return pltpu.make_async_remote_copy(
            src_ref=src, dst_ref=dst, send_sem=sems.at[0, ks], recv_sem=sems.at[1, kr],
            device_id=dev, device_id_type=MESH,
        )

    def start_all(copies):
        for cond, c in copies:
            pl.when(cond)(c.start)

    def plane_sum(piece_of, buf, own_ref, copies, out):
        for c in copies:
            c.wait_recv()
        total = own_ref[...].astype(F32)
        for k in range(1, 16):
            total = total + buf[k].astype(F32)
        out[...] = total.astype(BF16)

    def owns(first, tiles):
        return (z >= first) & (z < first + tiles)

    def z_sum(piece, buf, fin, tiles, first, sems, offset, scale):
        @pl.when(owns(first, tiles))
        def _():
            mine = z - first
            for s in range(16):
                @pl.when(z != s)
                def _(s=s):
                    copy_z(piece.at[0], buf.at[s], sems, offset, offset + s, column(s)).wait_recv()
            buf[z] = piece[mine]
            total = buf[0].astype(F32)
            for s in range(1, 16):
                total = total + buf[s].astype(F32)
            fin[mine] = (total * scale).astype(BF16)
            for k in Z_FAR_FIRST:
                copy_z(fin.at[mine], fin.at[mine], zb_sem, offset + k, offset + mine, column((z + k) % 16)).start()

    def z_back(fin, tiles, first, offset):
        for t in range(tiles):
            @pl.when(z != first + t)
            def _(t=t):
                copy_z(fin.at[t], fin.at[t], zb_sem, offset, offset + t, column(first + t)).wait_recv()

    def z_back_sent(fin, tiles, first, offset):
        @pl.when(owns(first, tiles))
        def _():
            for k in Z_FAR_FIRST:
                copy_z(fin.at[0], fin.at[0], zb_sem, offset + k, offset, column((z + k) % 16)).wait_send()

    plane_sum(a_piece_of, a_xy, a_piece_of(gx), a_plane, a_piece)
    a_zs = z_send(a_piece, a_z, NECK_TILES, 0, z_sem, 0)
    start_all(a_zs)
    plane_sum(b_piece_of, b_xy, b_piece_of(gx), b_plane, b_piece)
    b_zs = z_send(b_piece, b_z, REST_TILES, NECK_TILES, z_sem, 16)
    start_all(b_zs)
    z_sum(a_piece, a_z, a_fin, NECK_TILES, 0, z_sem, 0, scales[0])
    z_sum(b_piece, b_z, b_fin, REST_TILES, NECK_TILES, z_sem, 16, jnp.where(z < NECK_TILES + 2, scales[0], scales[1]))

    z_back(a_fin, NECK_TILES, 0, 0)
    def a_slot(o):
        return a_all.at[core, pl.ds(o * NECK_TILES, NECK_TILES)]

    def b_slot(o):
        return b_all.at[core, o]

    a_all[core, pl.ds(gx * NECK_TILES, NECK_TILES)] = a_fin[...]
    a_mine = a_slot(gx)
    a_back = go([copy(a_mine, a_mine, xyb_sem, k, plane[k]) for k in FAR_FIRST])
    z_back(b_fin, REST_TILES, NECK_TILES, 16)
    b_all[core, gx] = b_fin[...]
    b_mine = b_all.at[core, gx]
    b_back = go([copy(b_mine, b_mine, xyb_sem, 16 + k, plane[k]) for k in FAR_FIRST])

    def landed(slot_of, sems, first):
        for k in range(1, 16):
            slot = slot_of(in_plane(k, -1))
            copy(slot, slot, sems, first + k, plane[k]).wait_recv()

    landed(a_slot, xyb_sem, 0)
    go([copy(a_all.at[core], a_all.at[core], pair_sem, 2, pair_dev)])
    landed(b_slot, xyb_sem, 16)
    go([copy(b_all.at[core], b_all.at[core], pair_sem, 3, pair_dev)])
    copy(a_all.at[other], a_all.at[other], pair_sem, 2, pair_dev).wait_recv()
    copy(b_all.at[other], b_all.at[other], pair_sem, 3, pair_dev).wait_recv()

    for c in sent:
        c.wait_send()
    for cond, c in a_zs + b_zs:
        pl.when(cond)(c.wait_send)
    z_back_sent(a_fin, NECK_TILES, 0, 0)
    z_back_sent(b_fin, REST_TILES, NECK_TILES, 16)


def results_kernel(strip, level, a_all, b_all, neck_out, grad_input, grad_level, grad_down, grad_neck, sems):
    copies = [(strip, neck_out), (level, grad_input)]
    for half in range(2):
        lanes = slice(128 * half, 128 * half + 128)
        copies.append((a_all.at[half], grad_neck.at[:, :, lanes]))
        copies.append((b_all.at[half, :, 0:2], grad_down.at[:, :, :, lanes]))
        copies.append((b_all.at[half, 0:LEVEL_OWNERS, 2:5], grad_level.at[half]))
    copies = [pltpu.make_async_copy(src, dst, sems.at[n]) for n, (src, dst) in enumerate(copies)]
    for c in copies:
        c.start()
    for c in copies:
        c.wait()


def local(level_in, w_level, w_down, w_neck, cotangent):
    device_count = lax.axis_size("gy") * lax.axis_size("gx")
    level_count = level_in.shape[0] * level_in.shape[1] * device_count
    level_scale = 1.0 / math.sqrt(level_count)
    neck_scale = 1.0 / math.sqrt(level_count // 4)
    vmem = pl.BlockSpec(memory_space=pltpu.VMEM)
    hbm = pl.BlockSpec(memory_space=pltpu.HBM)
    dma = pltpu.SemaphoreType.DMA

    def v(*shape, dtype=BF16):
        return pltpu.VMEM(shape, dtype)

    def group(tiles, flat):
        whole = (16 * tiles, 16, 128) if flat else (16, tiles, 16, 128)
        return [
            v(*whole), v(*whole), v(*whole), v(16, tiles, 16, 128), v(tiles, 16, 128), v(16, 16, 128), v(tiles, 16, 128),
        ]

    outs = pl.pallas_call(
        functools.partial(kernel, (neck_scale, level_scale)),
        out_shape=[
            jax.ShapeDtypeStruct((4, 16, 512), BF16),
            jax.ShapeDtypeStruct((8, 64, 128), BF16),
            jax.ShapeDtypeStruct((2, 16 * NECK_TILES, 16, 128), BF16),
            jax.ShapeDtypeStruct((2, 16, REST_TILES, 16, 128), BF16),
        ],
        in_specs=[hbm] * 5,
        out_specs=[vmem] * 4,
        scratch_shapes=[
            v(8, 64, 128), v(4, 16, 512),
            v(3, 384, 128), v(512, 256), v(3, 768, 256), v(3, 384, 128),
            v(18, WIDE, 128), v(16 + 18 * WIDE, 128, dtype=F32), v(18 * WIDE, 384),
            v(8 * WIDE, 128, dtype=F32), v(16 * WIDE, 128, dtype=F32), v(8 * NARROW, 512),
            v(16 + 8 * NARROW, 256, dtype=F32), v(8 * NARROW, 768),
            v(6 * NARROW, 256, dtype=F32), v(16 + 6 * NARROW, 256, dtype=F32), v(6 * NARROW, 768),
            v(4 * NARROW, 256), v(4 * NARROW, 256), v(8 * WIDE, 128, dtype=F32),
            v(10, WIDE, 128), v(16 + 10 * WIDE, 128, dtype=F32), v(10 * WIDE, 384),
            v(16, 2, 16, 128), v(16, 2, 16, 128), v(2, NARROW, 256), v(2, NARROW, 256),
            v(16, 16, 128), v(16, 16, 128),
            v(144, 16, 128, dtype=F32), v(1152, 128, dtype=F32), v(512, 256, dtype=F32),
            *group(NECK_TILES, True), *group(REST_TILES, False),
            dma((5,)), dma((2, 8)), dma((2, 16)), dma((2, 8)), dma((2, 16)), dma((2, 8)),
            dma((2, 4)), dma((2, 32)), dma((2, 32)), dma((2, 32)), dma((2, 32)),
        ],
        compiler_params=pltpu.CompilerParams(
            collective_id=0, has_side_effects=True, vmem_limit_bytes=24 * 1024 * 1024
        ),
    )(
        *(pltpu.with_memory_space_constraint(t, pltpu.HBM) for t in (
            level_in,
            w_level.reshape(3, 384, 128),
            w_down.reshape(512, 256),
            w_neck.reshape(3, 768, 256),
            jnp.transpose(cotangent, (0, 2, 1)),
        ))
    )
    outs = pl.pallas_call(
        results_kernel,
        out_shape=[
            jax.ShapeDtypeStruct((4, 16, 512), BF16),
            jax.ShapeDtypeStruct((8, 64, 128), BF16),
            jax.ShapeDtypeStruct((2, LEVEL_OWNERS, 3, 16, 128), BF16),
            jax.ShapeDtypeStruct((16, 2, 16, 256), BF16),
            jax.ShapeDtypeStruct((144, 16, 256), BF16),
        ],
        in_specs=[vmem] * 4,
        out_specs=[hbm] * 5,
        scratch_shapes=[dma((8,))],
        compiler_params=pltpu.CompilerParams(vmem_limit_bytes=1024 * 1024),
    )(*outs)
    return (
        jnp.transpose(outs[0], (0, 2, 1)),
        outs[1],
        outs[2].reshape(w_level.shape),
        outs[3].reshape(w_down.shape),
        outs[4].reshape(w_neck.shape),
    )


def solution(mesh):
    return jax.shard_map(
        local,
        mesh=mesh,
        in_specs=(P("gy", "gx", None), P(), P(), P(), P("gy", None, "gx")),
        out_specs=(P("gy", None, "gx"), P("gy", "gx", None), P(), P(), P()),
        check_vma=False,
    )
```

```python
import functools
import math

import jax
import jax.numpy as jnp
from jax import lax
from jax.experimental import pallas as pl
from jax.experimental.pallas import tpu as pltpu
from jax.sharding import PartitionSpec as P

MESH = pl.DeviceIdType.MESH
BF16, F32 = jnp.bfloat16, jnp.float32

RIM = 5
WIDE = 96
NARROW = 48
SIDES = [(dy, dx) for dy in (-1, 0, 1) for dx in (-1, 0, 1) if (dy, dx) != (0, 0)]
FAR_FIRST = sorted(range(1, 16), key=lambda k: -(min(k // 4, 4 - k // 4) + min(k % 4, 4 - k % 4)))
Z_FAR_FIRST = sorted(range(1, 16), key=lambda k: -min(k, 16 - k))
NECK_TILES = 9
ROUTE = 5
REST_TILES = 5
LEVEL_OWNERS = 12


def slope_of(v):
    s = jax.nn.sigmoid(v)
    return s + v * s * (1.0 - s)


def dot(a, b):
    return jnp.dot(a, b, preferred_element_type=F32)


def dot_nt(a, b):
    return lax.dot_general(a, b, (((1,), (1,)), ((), ())), preferred_element_type=F32)


def dot_tn(a, b):
    return lax.dot_general(a, b, (((0,), (0,)), ((), ())), preferred_element_type=F32)


def kernel(
    scales,
    level_in, wl_hbm, wd_hbm, wn_hbm, cot_hbm,
    neck_out, grad_input, a_all, b_all,
    level_own, cot_in, wl, wd, wn, wlt,
    lp, lf, im_l, pre_l, act, dn, nf, im_n, cf, gf, im_g, gate_own, ng, lbf, gp, g2f, im_b,
    cot_send, cot_recv, ct, hr, no_send, no_recv,
    neck_own, level_acc, down_acc,
    a_pair_s, a_pair_r, a_work, near_a, near_b, far_a, far_b, a_piece, a_z, a_fin,
    b_pair_s, b_pair_r, b_work, b_xy, b_piece, b_z, b_fin,
    w_sem, e1_sem, cot_sem, ch_sem, no_sem, e4_sem,
    pair_sem, xy_sem, z_sem, zb_sem, xyb_sem, near_sem, far_sem, back1_sem, back2_sem,
):
    gy, gx = lax.axis_index("gy"), lax.axis_index("gx")
    z, core = gy // 2, gy % 2
    other = 1 - core

    def side(dy, dx):
        return ((gy + dy + 32) % 32, (gx + dx + 16) % 16)

    pair_dev = (z * 2 + other, gx)
    x, y = gx // 4, gx % 4

    def in_plane(k, sign=1):
        return ((x + sign * (k // 4) + 4) % 4) * 4 + (y + sign * (k % 4) + 4) % 4

    plane = [None] + [(gy, in_plane(k)) for k in range(1, 16)]

    def column(zz):
        return (zz * 2 + core, gx)

    loads = [
        pltpu.make_async_copy(cot_hbm, cot_in, w_sem.at[3]),
        pltpu.make_async_copy(level_in, level_own, w_sem.at[4]),
        pltpu.make_async_copy(wl_hbm, wl, w_sem.at[0]),
        pltpu.make_async_copy(wd_hbm, wd, w_sem.at[1]),
        pltpu.make_async_copy(wn_hbm, wn, w_sem.at[2]),
    ]
    for load in loads[:2]:
        load.start()
    barrier = pltpu.get_barrier_semaphore()
    peers = plane[1:] + [column((z + k) % 16) for k in range(1, 16)] + [side(dy, dx) for dy, dx in SIDES if dy != 0]
    for peer in peers:
        pl.semaphore_signal(barrier, inc=1, device_id=peer, device_id_type=MESH)

    def copy(src, dst, sems, k, dev):
        return pltpu.make_async_remote_copy(
            src_ref=src, dst_ref=dst, send_sem=sems.at[0, k], recv_sem=sems.at[1, k],
            device_id=dev, device_id_type=MESH,
        )

    sent = []

    def go(copies):
        for c in copies:
            c.start()
        sent.extend(copies)
        return copies

    pl.semaphore_wait(barrier, len(peers))
    src_rows = {-1: slice(0, RIM), 0: slice(0, 8), 1: slice(8 - RIM, 8)}
    src_cols = {-1: slice(0, 16), 0: slice(0, 64), 1: slice(48, 64)}
    dst_rows = {-1: slice(RIM + 8, RIM + 8 + RIM), 0: slice(RIM, RIM + 8), 1: slice(0, RIM)}
    dst_cols = {-1: slice(80, 96), 0: slice(16, 80), 1: slice(0, 16)}
    e1 = go([
        copy(level_in.at[src_rows[dy], src_cols[dx]], lp.at[dst_rows[dy], dst_cols[dx]], e1_sem, n, side(dy, dx))
        for n, (dy, dx) in enumerate(SIDES)
    ])

    loads[0].wait()
    for load in loads[2:]:
        load.start()
    lane = lax.broadcasted_iota(jnp.int32, (16, 128), 1)
    for q in range(4):
        rows = [cot_in[r, :, 128 * q:128 * q + 128].astype(F32) for r in range(4)]
        for j in range(4):
            out = pltpu.roll(rows[3], (32 * (3 - j)) % 128, 1) if j != 3 else rows[3]
            for r in (2, 1, 0):
                part = pltpu.roll(rows[r], (32 * (r - j)) % 128, 1) if r != j else rows[r]
                out = jnp.where(lane < 32 * (r + 1), part, out)
            cot_send[4 * q + j, 0] = out.astype(BF16)
    for t in range(16):
        cot_send[t, 1] = jnp.where(lane % 32 < 16, cot_send[(t + 1) % 16, 0].astype(F32), cot_send[(t + 15) % 16, 0].astype(F32)).astype(BF16)
    cot_recv[gx] = cot_send[gx]

    top_ok = jnp.where(gy > 0, 1.0, 0.0).astype(F32)
    bottom_ok = jnp.where(gy < 31, 1.0, 0.0).astype(F32)
    left_ok = jnp.where(gx > 0, 1.0, 0.0).astype(F32)
    right_ok = jnp.where(gx < 15, 1.0, 0.0).astype(F32)

    cot_copies = go([
        copy(cot_send.at[in_plane(k)], cot_recv.at[gx], cot_sem, k, plane[k]) for k in FAR_FIRST
    ])
    loads[1].wait()
    lf[0:8] = jnp.zeros((8, 128), F32)
    lf[8 + 18 * WIDE:] = jnp.zeros((8, 128), F32)
    for r in range(8):
        start = 8 + (r + RIM) * WIDE + 16
        lf[start:start + 64] = level_own[r].astype(F32)

    loads[2].wait()
    for ky in range(3):
        for kx in range(3):
            w = wl[2 - ky, (2 - kx) * 128:(3 - kx) * 128, :].astype(F32)
            wlt[ky, kx * 128:(kx + 1) * 128, :] = w.T.astype(BF16)

    for c in cot_copies:
        c.wait_recv()
    cot_tile = cot_recv[:, 0].reshape(256, 128).astype(F32).T
    cot_beside = cot_recv[:, 1].reshape(256, 128).astype(F32).T
    for r in range(4):
        base = (r + 1) * NARROW
        cf[base:base + 8] = cot_beside[32 * r + 24:32 * r + 32] * left_ok
        cf[base + 8:base + 40] = cot_tile[32 * r:32 * r + 32]
        cf[base + 40:base + 48] = cot_beside[32 * r:32 * r + 8] * right_ok
    ct[0] = cf[NARROW:2 * NARROW].astype(BF16)
    ct[1] = cf[4 * NARROW:5 * NARROW].astype(BF16)
    ch = go([copy(ct.at[n], hr.at[n], ch_sem, n, side(2 * n - 1, 0)) for n in range(2)])

    for c in e1:
        c.wait_recv()
    for r in range(18):
        row_ok = top_ok if r < RIM else bottom_ok if r >= RIM + 8 else None
        base = 8 + r * WIDE
        left = lp[r, 0:16].astype(F32) * left_ok
        right = lp[r, 80:96].astype(F32) * right_ok
        if row_ok is not None:
            left, right = left * row_ok, right * row_ok
            lf[base + 16:base + 80] = lp[r, 16:80].astype(F32) * row_ok
        lf[base:base + 16] = left
        lf[base + 80:base + 96] = right
    for r in range(18):
        for kx in range(3):
            start = 7 + kx + r * WIDE
            im_l[r * WIDE:(r + 1) * WIDE, kx * 128:(kx + 1) * 128] = lf[start:start + WIDE].astype(BF16)

    for q in range(4):
        pre = dot(im_l[4 * q * WIDE:(4 * q + 4) * WIDE], wl[0])
        for ky in (1, 2):
            pre = pre + dot(im_l[(4 * q + ky) * WIDE:(4 * q + ky + 4) * WIDE], wl[ky])
        own = lf[8 + (4 * q + 1) * WIDE:8 + (4 * q + 5) * WIDE]
        act[4 * q * WIDE:(4 * q + 4) * WIDE] = own + pre * jax.nn.sigmoid(pre)
        if q in (1, 2):
            pre_l[(q - 1) * 4 * WIDE:q * 4 * WIDE] = pre

    for rr in range(16):
        for q in range(2):
            lanes = slice(128 * (2 * (rr % 2) + q), 128 * (2 * (rr % 2) + q) + 128)
            dn[(rr // 2) * NARROW:(rr // 2 + 1) * NARROW, lanes] = act[pl.ds(rr * WIDE + q, NARROW, stride=2), :].astype(BF16)
    loads[3].wait()
    col = lax.broadcasted_iota(jnp.int32, (NARROW, 256), 0)
    col_ok = jnp.where(col < 8, left_ok, jnp.where(col >= 40, right_ok, 1.0))
    col_own = jnp.where((col >= 8) & (col < 40), 1.0, 0.0)
    nf[0:8] = jnp.zeros((8, 256), F32)
    nf[8 + 8 * NARROW:] = jnp.zeros((8, 256), F32)
    neck_in = dot(dn[...], wd[...]).astype(BF16).astype(F32)
    for r in range(8):
        row = neck_in[r * NARROW:(r + 1) * NARROW] * col_ok
        if r < 2:
            row = row * top_ok
        if r >= 6:
            row = row * bottom_ok
        nf[8 + r * NARROW:8 + (r + 1) * NARROW] = row
    for kx in range(3):
        im_n[:, kx * 256:(kx + 1) * 256] = nf[7 + kx:7 + kx + 8 * NARROW].astype(BF16)
    loads[4].wait()
    neck_pre = dot(im_n[0:6 * NARROW], wn[0])
    for ky in (1, 2):
        neck_pre = neck_pre + dot(im_n[ky * NARROW:(ky + 6) * NARROW], wn[ky])

    own = slice(NARROW, 5 * NARROW)
    gf[0:8] = jnp.zeros((8, 256), F32)
    gf[8 + 6 * NARROW:] = jnp.zeros((8, 256), F32)
    gate = (cf[own] * slope_of(neck_pre[own])).astype(BF16).astype(F32)
    gf[8 + NARROW:8 + 5 * NARROW] = gate
    for r in range(4):
        gate_own[r * NARROW:(r + 1) * NARROW] = (gate[r * NARROW:(r + 1) * NARROW] * col_own).astype(BF16)

    def half_lanes(half):
        return pl.ds(pl.multiple_of(half * 128, 128), 128)

    theirs = gate_own[:, half_lanes(other)]
    for ky in range(3):
        part = dot_tn(im_n[(1 + ky) * NARROW:(5 + ky) * NARROW], theirs)
        a_pair_s[48 * ky:48 * ky + 48] = part.astype(BF16).reshape(48, 16, 128)
    a_pair = go([copy(a_pair_s, a_pair_r, pair_sem, 0, pair_dev)])
    mine = gate_own[:, half_lanes(core)]
    for ky in range(3):
        neck_own[48 * ky:48 * ky + 48] = dot_tn(im_n[(1 + ky) * NARROW:(5 + ky) * NARROW], mine).reshape(48, 16, 128)

    def plane_stage(work, buf, sems, first):
        return go([copy(work(in_plane(k)), buf.at[k], sems, first + k, plane[k]) for k in FAR_FIRST])

    def b_piece_of(o):
        return b_work.at[o]

    a_pair[0].wait_recv()
    for n in range(16):
        part = slice(n * NECK_TILES, (n + 1) * NECK_TILES)
        a_work[n // 4, n % 4] = (neck_own[part] + a_pair_r[part].astype(F32)).astype(BF16)
    x_peer = [None] + [(gy, (x + k) % 4 * 4 + y) for k in range(1, 4)]
    y_peer = [None] + [(gy, x * 4 + (y + k) % 4) for k in range(1, 4)]
    near = []
    for k in (2, 1, 3):
        near.append(copy(a_work.at[(x + k) % 4, :, 0:ROUTE], near_a.at[k], near_sem, k, x_peer[k]))
        near.append(copy(a_work.at[:, (y + k) % 4, ROUTE:], near_b.at[k], near_sem, 4 + k, y_peer[k]))
    go(near)

    rows = []
    for r in range(4):
        v = neck_pre[(r + 1) * NARROW + 8:(r + 1) * NARROW + 40]
        rows.append(nf[8 + (r + 2) * NARROW + 8:8 + (r + 2) * NARROW + 40] + v * jax.nn.sigmoid(v))
    no_send[...] = jnp.concatenate(rows, axis=0).T.astype(BF16).reshape(16, 16, 128)
    no_recv[gx] = no_send[gx]
    no_copies = go([copy(no_send.at[in_plane(k)], no_recv.at[gx], no_sem, k, plane[k]) for k in FAR_FIRST])

    for c in ch:
        c.wait_recv()
    for n, ok, rows in ((1, top_ok, slice(0, NARROW)), (0, bottom_ok, slice(5 * NARROW, 6 * NARROW))):
        v = hr[n].astype(F32) * ok * slope_of(neck_pre[rows])
        gf[8 + rows.start:8 + rows.stop] = v.astype(BF16).astype(F32)

    for kx in range(3):
        im_g[:, kx * 256:(kx + 1) * 256] = gf[7 + kx:7 + kx + 6 * NARROW].astype(BF16)
    back = None
    for ky in range(3):
        for kx in range(3):
            term = dot_nt(
                im_g[ky * NARROW:(ky + 4) * NARROW, kx * 256:(kx + 1) * 256],
                wn[2 - ky, (2 - kx) * 256:(3 - kx) * 256, :],
            )
            back = term if back is None else back + term
    for r in range(4):
        v = cf[(r + 1) * NARROW:(r + 2) * NARROW] + back[r * NARROW:(r + 1) * NARROW]
        ng[r * NARROW:(r + 1) * NARROW] = (v * col_own).astype(BF16)
    spread = dot_nt(ng[...], wd[...])
    for r in range(4):
        for p in range(2):
            for q in range(2):
                lanes = slice(128 * (2 * p + q), 128 * (2 * p + q) + 128)
                lbf[pl.ds((2 * r + p) * WIDE + q, NARROW, stride=2), :] = spread[r * NARROW:(r + 1) * NARROW, lanes]
    for r in range(8):
        rows_r = slice(r * WIDE + 16, r * WIDE + 80)
        gp[r + 1, 16:80] = (lbf[rows_r] * slope_of(pre_l[rows_r])).astype(BF16)
    e4_src = {-1: slice(1, 2), 0: slice(1, 9), 1: slice(8, 9)}
    e4_dst = {-1: slice(9, 10), 0: slice(1, 9), 1: slice(0, 1)}
    e4_scol = {-1: slice(16, 32), 0: slice(16, 80), 1: slice(64, 80)}
    e4 = go([
        copy(gp.at[e4_src[dy], e4_scol[dx]], gp.at[e4_dst[dy], dst_cols[dx]], e4_sem, n, side(dy, dx))
        for n, (dy, dx) in enumerate(SIDES)
    ])

    own_gate = gp[1:9, 16:80].reshape(512, 128)
    for ky in range(3):
        window = jnp.concatenate(
            [im_l[(4 + ky + r) * WIDE + 16:(4 + ky + r) * WIDE + 80] for r in range(8)], axis=0
        )
        level_acc[ky * 384:(ky + 1) * 384] = dot_tn(window, own_gate)
    down_acc[...] = dot_tn(dn[2 * NARROW:6 * NARROW], ng[...])

    def rest_terms(half):
        down = down_acc[:, half_lanes(half)].reshape(16, 2, 16, 128)
        level = level_acc[pl.ds(pl.multiple_of(half * 576, 576), 576), :].reshape(LEVEL_OWNERS, 3, 16, 128)
        return down, level

    down, level = rest_terms(other)
    nothing = jnp.zeros((16 - LEVEL_OWNERS, 3, 16, 128), BF16)
    b_pair_s[:, 0:2] = down.astype(BF16)
    b_pair_s[0:LEVEL_OWNERS, 2:5] = level.astype(BF16)
    b_pair_s[LEVEL_OWNERS:, 2:5] = nothing
    b_pair = go([copy(b_pair_s, b_pair_r, pair_sem, 1, pair_dev)])

    b_pair[0].wait_recv()
    down, level = rest_terms(core)
    b_work[:, 0:2] = (down + b_pair_r[:, 0:2].astype(F32)).astype(BF16)
    b_work[0:LEVEL_OWNERS, 2:5] = (level + b_pair_r[0:LEVEL_OWNERS, 2:5].astype(F32)).astype(BF16)
    b_work[LEVEL_OWNERS:, 2:5] = nothing
    b_plane = plane_stage(b_piece_of, b_xy, xy_sem, 16)

    for c in e4:
        c.wait_recv()
    g2f[0:8] = jnp.zeros((8, 128), F32)
    g2f[8 + 10 * WIDE:] = jnp.zeros((8, 128), F32)
    for r in range(10):
        row_ok = top_ok if r == 0 else bottom_ok if r == 9 else None
        base = 8 + r * WIDE
        left, mid, right = gp[r, 0:16].astype(F32) * left_ok, gp[r, 16:80].astype(F32), gp[r, 80:96].astype(F32) * right_ok
        if row_ok is not None:
            left, mid, right = left * row_ok, mid * row_ok, right * row_ok
        g2f[base:base + 16] = left
        g2f[base + 16:base + 80] = mid
        g2f[base + 80:base + 96] = right
    for r in range(10):
        for kx in range(3):
            start = 7 + kx + r * WIDE
            im_b[r * WIDE:(r + 1) * WIDE, kx * 128:(kx + 1) * 128] = g2f[start:start + WIDE].astype(BF16)
    for q in range(2):
        total = lbf[4 * q * WIDE:(4 * q + 4) * WIDE]
        for ky in range(3):
            total = total + dot(im_b[(4 * q + ky) * WIDE:(4 * q + ky + 4) * WIDE], wlt[ky])
        grad_input[4 * q:4 * q + 4] = total.reshape(4, WIDE, 128)[:, 16:80].astype(BF16)

    for c in near:
        c.wait_recv()
    for p in range(4):
        via_x, via_y = a_work[x, p, 0:ROUTE].astype(F32), a_work[p, y, ROUTE:].astype(F32)
        for k in range(1, 4):
            via_x = via_x + near_a[k, p].astype(F32)
            via_y = via_y + near_b[k, p].astype(F32)
        near_a[0, p] = via_x.astype(BF16)
        near_b[0, p] = via_y.astype(BF16)
    far = []
    for k in (2, 1, 3):
        far.append(copy(near_a.at[0, (y + k) % 4], far_a.at[k], far_sem, k, y_peer[k]))
        far.append(copy(near_b.at[0, (x + k) % 4], far_b.at[k], far_sem, 4 + k, x_peer[k]))
    go(far)

    for c in no_copies:
        c.wait_recv()
    for q in range(4):
        pieces = [no_recv[4 * q + j].astype(F32) for j in range(4)]
        for r in range(4):
            out = pltpu.roll(pieces[3], (32 * (3 - r)) % 128, 1) if r != 3 else pieces[3]
            for j in (2, 1, 0):
                part = pltpu.roll(pieces[j], (32 * (j - r)) % 128, 1) if r != j else pieces[j]
                out = jnp.where(lane < 32 * (j + 1), part, out)
            neck_out[r, :, 128 * q:128 * q + 128] = out.astype(BF16)

    def z_send(piece, buf, tiles, first, sems, offset):
        copies = []
        for t in range(tiles):
            c = copy_z(piece.at[t], buf.at[z], sems, offset + t, offset + z, column(first + t))
            copies.append((z != first + t, c))
        return copies

    def copy_z(src, dst, sems, ks, kr, dev):
        return pltpu.make_async_remote_copy(
            src_ref=src, dst_ref=dst, send_sem=sems.at[0, ks], recv_sem=sems.at[1, kr],
            device_id=dev, device_id_type=MESH,
        )

    def start_all(copies):
        for cond, c in copies:
            pl.when(cond)(c.start)

    def plane_sum(piece_of, buf, own_ref, copies, out):
        for c in copies:
            c.wait_recv()
        total = own_ref[...].astype(F32)
        for k in range(1, 16):
            total = total + buf[k].astype(F32)
        out[...] = total.astype(BF16)

    def owns(first, tiles):
        return (z >= first) & (z < first + tiles)

    def z_sum(piece, buf, fin, tiles, first, sems, offset, scale):
        @pl.when(owns(first, tiles))
        def _():
            mine = z - first
            for s in range(16):
                @pl.when(z != s)
                def _(s=s):
                    copy_z(piece.at[0], buf.at[s], sems, offset, offset + s, column(s)).wait_recv()
            buf[z] = piece[mine]
            total = buf[0].astype(F32)
            for s in range(1, 16):
                total = total + buf[s].astype(F32)
            fin[mine] = (total * scale).astype(BF16)
            for k in Z_FAR_FIRST:
                copy_z(fin.at[mine], fin.at[mine], zb_sem, offset + k, offset + mine, column((z + k) % 16)).start()

    def z_back(fin, tiles, first, offset):
        for t in range(tiles):
            @pl.when(z != first + t)
            def _(t=t):
                copy_z(fin.at[t], fin.at[t], zb_sem, offset, offset + t, column(first + t)).wait_recv()

    def z_back_sent(fin, tiles, first, offset):
        @pl.when(owns(first, tiles))
        def _():
            for k in Z_FAR_FIRST:
                copy_z(fin.at[0], fin.at[0], zb_sem, offset + k, offset, column((z + k) % 16)).wait_send()

    for c in far:
        c.wait_recv()
    via_x, via_y = near_a[0, y].astype(F32), near_b[0, x].astype(F32)
    for k in range(1, 4):
        via_x = via_x + far_a[k].astype(F32)
        via_y = via_y + far_b[k].astype(F32)
    a_piece[0:ROUTE] = via_x.astype(BF16)
    a_piece[ROUTE:] = via_y.astype(BF16)
    a_zs = z_send(a_piece, a_z, NECK_TILES, 0, z_sem, 0)
    start_all(a_zs)
    plane_sum(b_piece_of, b_xy, b_piece_of(gx), b_plane, b_piece)
    b_zs = z_send(b_piece, b_z, REST_TILES, NECK_TILES, z_sem, 16)
    start_all(b_zs)
    z_sum(a_piece, a_z, a_fin, NECK_TILES, 0, z_sem, 0, scales[0])
    z_sum(b_piece, b_z, b_fin, REST_TILES, NECK_TILES, z_sem, 16, jnp.where(z < NECK_TILES + 2, scales[0], scales[1]))

    z_back(a_fin, NECK_TILES, 0, 0)
    def b_slot(o):
        return b_all.at[core, o]

    a_all[core, x, y] = a_fin[...]
    leg1 = []
    for k in (2, 1, 3):
        mine_x, mine_y = a_all.at[core, x, y, 0:ROUTE], a_all.at[core, x, y, ROUTE:]
        leg1.append(copy(mine_x, mine_x, back1_sem, k, y_peer[k]))
        leg1.append(copy(mine_y, mine_y, back1_sem, 4 + k, x_peer[k]))
    go(leg1)
    z_back(b_fin, REST_TILES, NECK_TILES, 16)
    b_all[core, gx] = b_fin[...]
    b_mine = b_slot(gx)
    go([copy(b_mine, b_mine, xyb_sem, 16 + k, plane[k]) for k in FAR_FIRST])
    for c in leg1:
        c.wait_recv()

    def block_x(c, xx):
        return a_all.at[c, xx, :, 0:ROUTE]

    def block_y(c, yy):
        return a_all.at[c, :, yy, ROUTE:]

    leg2 = []
    for k in (2, 1, 3):
        leg2.append(copy(block_x(core, x), block_x(core, x), back2_sem, k, x_peer[k]))
        leg2.append(copy(block_y(core, y), block_y(core, y), back2_sem, 4 + k, y_peer[k]))
    go(leg2)

    def swap(k):
        bx, by = block_x(core, (x - k + 4) % 4), block_y(core, (y - k + 4) % 4)
        go([copy(bx, bx, pair_sem, 4 + k, pair_dev), copy(by, by, pair_sem, 8 + k, pair_dev)])

    swap(0)
    for k in FAR_FIRST:
        slot = b_slot(in_plane(k, -1))
        copy(slot, slot, xyb_sem, 16 + k, plane[k]).wait_recv()
    go([copy(b_all.at[core], b_all.at[core], pair_sem, 3, pair_dev)])
    for k in (1, 3, 2):
        bx, by = block_x(core, (x - k + 4) % 4), block_y(core, (y - k + 4) % 4)
        copy(bx, bx, back2_sem, k, x_peer[k]).wait_recv()
        copy(by, by, back2_sem, 4 + k, y_peer[k]).wait_recv()
        swap(k)
    copy(b_all.at[other], b_all.at[other], pair_sem, 3, pair_dev).wait_recv()
    for k in range(4):
        bx, by = block_x(other, (x - k + 4) % 4), block_y(other, (y - k + 4) % 4)
        copy(bx, bx, pair_sem, 4 + k, pair_dev).wait_recv()
        copy(by, by, pair_sem, 8 + k, pair_dev).wait_recv()

    for c in sent:
        c.wait_send()
    for cond, c in a_zs + b_zs:
        pl.when(cond)(c.wait_send)
    z_back_sent(a_fin, NECK_TILES, 0, 0)
    z_back_sent(b_fin, REST_TILES, NECK_TILES, 16)


def results_kernel(strip, level, a_all, b_all, neck_out, grad_input, grad_level, grad_down, grad_neck, sems):
    copies = [(strip, neck_out), (level, grad_input)]
    for half in range(2):
        lanes = slice(128 * half, 128 * half + 128)
        copies.append((a_all.at[half], grad_neck.at[:, :, :, :, lanes]))
        copies.append((b_all.at[half, :, 0:2], grad_down.at[:, :, :, lanes]))
        copies.append((b_all.at[half, 0:LEVEL_OWNERS, 2:5], grad_level.at[half]))
    copies = [pltpu.make_async_copy(src, dst, sems.at[n]) for n, (src, dst) in enumerate(copies)]
    for c in copies:
        c.start()
    for c in copies:
        c.wait()


def local(level_in, w_level, w_down, w_neck, cotangent):
    device_count = lax.axis_size("gy") * lax.axis_size("gx")
    level_count = level_in.shape[0] * level_in.shape[1] * device_count
    level_scale = 1.0 / math.sqrt(level_count)
    neck_scale = 1.0 / math.sqrt(level_count // 4)
    vmem = pl.BlockSpec(memory_space=pltpu.VMEM)
    hbm = pl.BlockSpec(memory_space=pltpu.HBM)
    dma = pltpu.SemaphoreType.DMA

    def v(*shape, dtype=BF16):
        return pltpu.VMEM(shape, dtype)

    outs = pl.pallas_call(
        functools.partial(kernel, (neck_scale, level_scale)),
        out_shape=[
            jax.ShapeDtypeStruct((4, 16, 512), BF16),
            jax.ShapeDtypeStruct((8, 64, 128), BF16),
            jax.ShapeDtypeStruct((2, 4, 4, NECK_TILES, 16, 128), BF16),
            jax.ShapeDtypeStruct((2, 16, REST_TILES, 16, 128), BF16),
        ],
        in_specs=[hbm] * 5,
        out_specs=[vmem] * 4,
        scratch_shapes=[
            v(8, 64, 128), v(4, 16, 512),
            v(3, 384, 128), v(512, 256), v(3, 768, 256), v(3, 384, 128),
            v(18, WIDE, 128), v(16 + 18 * WIDE, 128, dtype=F32), v(18 * WIDE, 384),
            v(8 * WIDE, 128, dtype=F32), v(16 * WIDE, 128, dtype=F32), v(8 * NARROW, 512),
            v(16 + 8 * NARROW, 256, dtype=F32), v(8 * NARROW, 768),
            v(6 * NARROW, 256, dtype=F32), v(16 + 6 * NARROW, 256, dtype=F32), v(6 * NARROW, 768),
            v(4 * NARROW, 256), v(4 * NARROW, 256), v(8 * WIDE, 128, dtype=F32),
            v(10, WIDE, 128), v(16 + 10 * WIDE, 128, dtype=F32), v(10 * WIDE, 384),
            v(16, 2, 16, 128), v(16, 2, 16, 128), v(2, NARROW, 256), v(2, NARROW, 256),
            v(16, 16, 128), v(16, 16, 128),
            v(144, 16, 128, dtype=F32), v(1152, 128, dtype=F32), v(512, 256, dtype=F32),
            v(16 * NECK_TILES, 16, 128), v(16 * NECK_TILES, 16, 128), v(4, 4, NECK_TILES, 16, 128),
            v(4, 4, ROUTE, 16, 128), v(4, 4, NECK_TILES - ROUTE, 16, 128),
            v(4, ROUTE, 16, 128), v(4, NECK_TILES - ROUTE, 16, 128),
            v(NECK_TILES, 16, 128), v(16, 16, 128), v(NECK_TILES, 16, 128),
            v(16, REST_TILES, 16, 128), v(16, REST_TILES, 16, 128), v(16, REST_TILES, 16, 128), v(16, REST_TILES, 16, 128),
            v(REST_TILES, 16, 128), v(16, 16, 128), v(REST_TILES, 16, 128),
            dma((5,)), dma((2, 8)), dma((2, 16)), dma((2, 8)), dma((2, 16)), dma((2, 8)),
            dma((2, 12)), dma((2, 32)), dma((2, 32)), dma((2, 32)), dma((2, 32)), dma((2, 8)), dma((2, 8)), dma((2, 8)), dma((2, 8)),
        ],
        compiler_params=pltpu.CompilerParams(
            collective_id=0, has_side_effects=True, vmem_limit_bytes=24 * 1024 * 1024
        ),
    )(
        *(pltpu.with_memory_space_constraint(t, pltpu.HBM) for t in (
            level_in,
            w_level.reshape(3, 384, 128),
            w_down.reshape(512, 256),
            w_neck.reshape(3, 768, 256),
            jnp.transpose(cotangent, (0, 2, 1)),
        ))
    )
    outs = pl.pallas_call(
        results_kernel,
        out_shape=[
            jax.ShapeDtypeStruct((4, 16, 512), BF16),
            jax.ShapeDtypeStruct((8, 64, 128), BF16),
            jax.ShapeDtypeStruct((2, LEVEL_OWNERS, 3, 16, 128), BF16),
            jax.ShapeDtypeStruct((16, 2, 16, 256), BF16),
            jax.ShapeDtypeStruct((4, 4, NECK_TILES, 16, 256), BF16),
        ],
        in_specs=[vmem] * 4,
        out_specs=[hbm] * 5,
        scratch_shapes=[dma((8,))],
        compiler_params=pltpu.CompilerParams(vmem_limit_bytes=1024 * 1024),
    )(*outs)
    return (
        jnp.transpose(outs[0], (0, 2, 1)),
        outs[1],
        outs[2].reshape(w_level.shape),
        outs[3].reshape(w_down.shape),
        outs[4].reshape(w_neck.shape),
    )


def solution(mesh):
    return jax.shard_map(
        local,
        mesh=mesh,
        in_specs=(P("gy", "gx", None), P(), P(), P(), P("gy", None, "gx")),
        out_specs=(P("gy", None, "gx"), P("gy", "gx", None), P(), P(), P()),
        check_vma=False,
    )
```

```python
import functools
import math

import jax
import jax.numpy as jnp
from jax import lax
from jax.experimental import pallas as pl
from jax.experimental.pallas import tpu as pltpu
from jax.sharding import PartitionSpec as P

MESH = pl.DeviceIdType.MESH
BF16, F32 = jnp.bfloat16, jnp.float32

RIM = 5
WIDE = 96
NARROW = 48
SIDES = [(dy, dx) for dy in (-1, 0, 1) for dx in (-1, 0, 1) if (dy, dx) != (0, 0)]
FAR_FIRST = sorted(range(1, 16), key=lambda k: -(min(k // 4, 4 - k // 4) + min(k % 4, 4 - k % 4)))
Z_FAR_FIRST = sorted(range(1, 16), key=lambda k: -min(k, 16 - k))
NECK_TILES = 9
ROUTE = 5
REST_TILES = 5
LEVEL_OWNERS = 12


def slope_of(v):
    s = jax.nn.sigmoid(v)
    return s + v * s * (1.0 - s)


def dot(a, b):
    return jnp.dot(a, b, preferred_element_type=F32)


def dot_nt(a, b):
    return lax.dot_general(a, b, (((1,), (1,)), ((), ())), preferred_element_type=F32)


def dot_tn(a, b):
    return lax.dot_general(a, b, (((0,), (0,)), ((), ())), preferred_element_type=F32)


def kernel(
    scales,
    level_in, wl_hbm, wd_hbm, wn_hbm, cot_hbm,
    neck_out, grad_input, a_all, b_all,
    level_own, cot_in, wl, wd, wn, wlt,
    lp, lf, im_l, pre_l, act, dn, nf, im_n, cf, gf, im_g, gate_own, ng, lbf, gp, g2f, im_b,
    cot_send, cot_recv, ct, hr, no_send, no_recv,
    neck_own, level_acc, down_acc,
    a_pair_s, a_pair_r, a_work, near_a, near_b, far_a, far_b, a_piece, a_z, a_fin,
    b_pair_s, b_pair_r, b_work, b_xy, b_piece, b_z, b_fin,
    w_sem, e1_sem, cot_sem, ch_sem, no_sem, e4_sem,
    pair_sem, xy_sem, z_sem, zb_sem, xyb_sem, near_sem, far_sem, back1_sem, back2_sem, known,
):
    gy, gx = lax.axis_index("gy"), lax.axis_index("gx")
    z, core = gy // 2, gy % 2
    other = 1 - core

    def side(dy, dx):
        return ((gy + dy + 32) % 32, (gx + dx + 16) % 16)

    pair_dev = (z * 2 + other, gx)
    x, y = gx // 4, gx % 4

    def in_plane(k, sign=1):
        return ((x + sign * (k // 4) + 4) % 4) * 4 + (y + sign * (k % 4) + 4) % 4

    plane = [None] + [(gy, in_plane(k)) for k in range(1, 16)]

    def column(zz):
        return (zz * 2 + core, gx)

    loads = [
        pltpu.make_async_copy(cot_hbm, cot_in, w_sem.at[3]),
        pltpu.make_async_copy(level_in, level_own, w_sem.at[4]),
        pltpu.make_async_copy(wl_hbm, wl, w_sem.at[0]),
        pltpu.make_async_copy(wd_hbm, wd, w_sem.at[1]),
        pltpu.make_async_copy(wn_hbm, wn, w_sem.at[2]),
    ]
    for load in loads[:2]:
        load.start()
    barrier = pltpu.get_barrier_semaphore()
    x_peer = [None] + [(gy, (x + k) % 4 * 4 + y) for k in range(1, 4)]
    y_peer = [None] + [(gy, x * 4 + (y + k) % 4) for k in range(1, 4)]
    peers = x_peer[1:] + y_peer[1:] + [side(dy, dx) for dy, dx in SIDES]
    for peer in peers:
        pl.semaphore_signal(barrier, inc=1, device_id=peer, device_id_type=MESH)

    def copy(src, dst, sems, k, dev):
        return pltpu.make_async_remote_copy(
            src_ref=src, dst_ref=dst, send_sem=sems.at[0, k], recv_sem=sems.at[1, k],
            device_id=dev, device_id_type=MESH,
        )

    sent = []

    def go(copies):
        for c in copies:
            c.start()
        sent.extend(copies)
        return copies

    pl.semaphore_wait(barrier, len(peers))
    def tell(n):
        for dy in (-1, 1):
            pl.semaphore_signal(known.at[n], inc=1, device_id=side(dy * 2 ** n, 0), device_id_type=MESH)

    for k in range(1, 4):
        pl.semaphore_signal(known.at[4], inc=1, device_id=y_peer[k], device_id_type=MESH)
    src_rows = {-1: slice(0, RIM), 0: slice(0, 8), 1: slice(8 - RIM, 8)}
    src_cols = {-1: slice(0, 16), 0: slice(0, 64), 1: slice(48, 64)}
    dst_rows = {-1: slice(RIM + 8, RIM + 8 + RIM), 0: slice(RIM, RIM + 8), 1: slice(0, RIM)}
    dst_cols = {-1: slice(80, 96), 0: slice(16, 80), 1: slice(0, 16)}
    e1 = go([
        copy(level_in.at[src_rows[dy], src_cols[dx]], lp.at[dst_rows[dy], dst_cols[dx]], e1_sem, n, side(dy, dx))
        for n, (dy, dx) in enumerate(SIDES)
    ])

    tell(0)
    loads[0].wait()
    for load in loads[2:]:
        load.start()
    lane = lax.broadcasted_iota(jnp.int32, (16, 128), 1)
    for q in range(4):
        rows = [cot_in[r, :, 128 * q:128 * q + 128].astype(F32) for r in range(4)]
        for j in range(4):
            out = pltpu.roll(rows[3], (32 * (3 - j)) % 128, 1) if j != 3 else rows[3]
            for r in (2, 1, 0):
                part = pltpu.roll(rows[r], (32 * (r - j)) % 128, 1) if r != j else rows[r]
                out = jnp.where(lane < 32 * (r + 1), part, out)
            cot_send[4 * q + j, 0] = out.astype(BF16)
    for t in range(16):
        cot_send[t, 1] = jnp.where(lane % 32 < 16, cot_send[(t + 1) % 16, 0].astype(F32), cot_send[(t + 15) % 16, 0].astype(F32)).astype(BF16)
    cot_recv[gx] = cot_send[gx]

    top_ok = jnp.where(gy > 0, 1.0, 0.0).astype(F32)
    bottom_ok = jnp.where(gy < 31, 1.0, 0.0).astype(F32)
    left_ok = jnp.where(gx > 0, 1.0, 0.0).astype(F32)
    right_ok = jnp.where(gx < 15, 1.0, 0.0).astype(F32)

    pl.semaphore_wait(known.at[4], 3)
    cot_copies = go([
        copy(cot_send.at[in_plane(k)], cot_recv.at[gx], cot_sem, k, plane[k]) for k in FAR_FIRST
    ])
    loads[1].wait()
    lf[0:8] = jnp.zeros((8, 128), F32)
    lf[8 + 18 * WIDE:] = jnp.zeros((8, 128), F32)
    for r in range(8):
        start = 8 + (r + RIM) * WIDE + 16
        lf[start:start + 64] = level_own[r].astype(F32)

    pl.semaphore_wait(known.at[0], 2)
    tell(1)

    loads[2].wait()
    for ky in range(3):
        for kx in range(3):
            w = wl[2 - ky, (2 - kx) * 128:(3 - kx) * 128, :].astype(F32)
            wlt[ky, kx * 128:(kx + 1) * 128, :] = w.T.astype(BF16)

    for c in cot_copies:
        c.wait_recv()
    cot_tile = cot_recv[:, 0].reshape(256, 128).astype(F32).T
    cot_beside = cot_recv[:, 1].reshape(256, 128).astype(F32).T
    for r in range(4):
        base = (r + 1) * NARROW
        cf[base:base + 8] = cot_beside[32 * r + 24:32 * r + 32] * left_ok
        cf[base + 8:base + 40] = cot_tile[32 * r:32 * r + 32]
        cf[base + 40:base + 48] = cot_beside[32 * r:32 * r + 8] * right_ok
    ct[0] = cf[NARROW:2 * NARROW].astype(BF16)
    ct[1] = cf[4 * NARROW:5 * NARROW].astype(BF16)
    ch = go([copy(ct.at[n], hr.at[n], ch_sem, n, side(2 * n - 1, 0)) for n in range(2)])

    pl.semaphore_wait(known.at[1], 2)
    tell(2)

    for c in e1:
        c.wait_recv()
    for r in range(18):
        row_ok = top_ok if r < RIM else bottom_ok if r >= RIM + 8 else None
        base = 8 + r * WIDE
        left = lp[r, 0:16].astype(F32) * left_ok
        right = lp[r, 80:96].astype(F32) * right_ok
        if row_ok is not None:
            left, right = left * row_ok, right * row_ok
            lf[base + 16:base + 80] = lp[r, 16:80].astype(F32) * row_ok
        lf[base:base + 16] = left
        lf[base + 80:base + 96] = right
    for r in range(18):
        for kx in range(3):
            start = 7 + kx + r * WIDE
            im_l[r * WIDE:(r + 1) * WIDE, kx * 128:(kx + 1) * 128] = lf[start:start + WIDE].astype(BF16)

    for q in range(4):
        pre = dot(im_l[4 * q * WIDE:(4 * q + 4) * WIDE], wl[0])
        for ky in (1, 2):
            pre = pre + dot(im_l[(4 * q + ky) * WIDE:(4 * q + ky + 4) * WIDE], wl[ky])
        own = lf[8 + (4 * q + 1) * WIDE:8 + (4 * q + 5) * WIDE]
        act[4 * q * WIDE:(4 * q + 4) * WIDE] = own + pre * jax.nn.sigmoid(pre)
        if q in (1, 2):
            pre_l[(q - 1) * 4 * WIDE:q * 4 * WIDE] = pre

    for rr in range(16):
        for q in range(2):
            lanes = slice(128 * (2 * (rr % 2) + q), 128 * (2 * (rr % 2) + q) + 128)
            dn[(rr // 2) * NARROW:(rr // 2 + 1) * NARROW, lanes] = act[pl.ds(rr * WIDE + q, NARROW, stride=2), :].astype(BF16)
    loads[3].wait()
    col = lax.broadcasted_iota(jnp.int32, (NARROW, 256), 0)
    col_ok = jnp.where(col < 8, left_ok, jnp.where(col >= 40, right_ok, 1.0))
    col_own = jnp.where((col >= 8) & (col < 40), 1.0, 0.0)
    nf[0:8] = jnp.zeros((8, 256), F32)
    nf[8 + 8 * NARROW:] = jnp.zeros((8, 256), F32)
    neck_in = dot(dn[...], wd[...]).astype(BF16).astype(F32)
    for r in range(8):
        row = neck_in[r * NARROW:(r + 1) * NARROW] * col_ok
        if r < 2:
            row = row * top_ok
        if r >= 6:
            row = row * bottom_ok
        nf[8 + r * NARROW:8 + (r + 1) * NARROW] = row
    for kx in range(3):
        im_n[:, kx * 256:(kx + 1) * 256] = nf[7 + kx:7 + kx + 8 * NARROW].astype(BF16)
    loads[4].wait()
    neck_pre = dot(im_n[0:6 * NARROW], wn[0])
    for ky in (1, 2):
        neck_pre = neck_pre + dot(im_n[ky * NARROW:(ky + 6) * NARROW], wn[ky])

    own = slice(NARROW, 5 * NARROW)
    gf[0:8] = jnp.zeros((8, 256), F32)
    gf[8 + 6 * NARROW:] = jnp.zeros((8, 256), F32)
    gate = (cf[own] * slope_of(neck_pre[own])).astype(BF16).astype(F32)
    gf[8 + NARROW:8 + 5 * NARROW] = gate
    for r in range(4):
        gate_own[r * NARROW:(r + 1) * NARROW] = (gate[r * NARROW:(r + 1) * NARROW] * col_own).astype(BF16)

    def half_lanes(half):
        return pl.ds(pl.multiple_of(half * 128, 128), 128)

    theirs = gate_own[:, half_lanes(other)]
    for ky in range(3):
        part = dot_tn(im_n[(1 + ky) * NARROW:(5 + ky) * NARROW], theirs)
        a_pair_s[48 * ky:48 * ky + 48] = part.astype(BF16).reshape(48, 16, 128)
    a_pair = go([copy(a_pair_s, a_pair_r, pair_sem, 0, pair_dev)])
    pl.semaphore_wait(known.at[2], 2)
    tell(3)
    mine = gate_own[:, half_lanes(core)]
    for ky in range(3):
        neck_own[48 * ky:48 * ky + 48] = dot_tn(im_n[(1 + ky) * NARROW:(5 + ky) * NARROW], mine).reshape(48, 16, 128)

    def plane_stage(work, buf, sems, first):
        return go([copy(work(in_plane(k)), buf.at[k], sems, first + k, plane[k]) for k in FAR_FIRST])

    def b_piece_of(o):
        return b_work.at[o]

    a_pair[0].wait_recv()
    for n in range(16):
        part = slice(n * NECK_TILES, (n + 1) * NECK_TILES)
        a_work[n // 4, n % 4] = (neck_own[part] + a_pair_r[part].astype(F32)).astype(BF16)
    near = []
    for k in (2, 1, 3):
        near.append(copy(a_work.at[(x + k) % 4, :, 0:ROUTE], near_a.at[k], near_sem, k, x_peer[k]))
        near.append(copy(a_work.at[:, (y + k) % 4, ROUTE:], near_b.at[k], near_sem, 4 + k, y_peer[k]))
    go(near)

    rows = []
    for r in range(4):
        v = neck_pre[(r + 1) * NARROW + 8:(r + 1) * NARROW + 40]
        rows.append(nf[8 + (r + 2) * NARROW + 8:8 + (r + 2) * NARROW + 40] + v * jax.nn.sigmoid(v))
    no_send[...] = jnp.concatenate(rows, axis=0).T.astype(BF16).reshape(16, 16, 128)
    no_recv[gx] = no_send[gx]
    no_copies = go([copy(no_send.at[in_plane(k)], no_recv.at[gx], no_sem, k, plane[k]) for k in FAR_FIRST])

    for c in ch:
        c.wait_recv()
    for n, ok, rows in ((1, top_ok, slice(0, NARROW)), (0, bottom_ok, slice(5 * NARROW, 6 * NARROW))):
        v = hr[n].astype(F32) * ok * slope_of(neck_pre[rows])
        gf[8 + rows.start:8 + rows.stop] = v.astype(BF16).astype(F32)

    for kx in range(3):
        im_g[:, kx * 256:(kx + 1) * 256] = gf[7 + kx:7 + kx + 6 * NARROW].astype(BF16)
    back = None
    for ky in range(3):
        for kx in range(3):
            term = dot_nt(
                im_g[ky * NARROW:(ky + 4) * NARROW, kx * 256:(kx + 1) * 256],
                wn[2 - ky, (2 - kx) * 256:(3 - kx) * 256, :],
            )
            back = term if back is None else back + term
    for r in range(4):
        v = cf[(r + 1) * NARROW:(r + 2) * NARROW] + back[r * NARROW:(r + 1) * NARROW]
        ng[r * NARROW:(r + 1) * NARROW] = (v * col_own).astype(BF16)
    spread = dot_nt(ng[...], wd[...])
    for r in range(4):
        for p in range(2):
            for q in range(2):
                lanes = slice(128 * (2 * p + q), 128 * (2 * p + q) + 128)
                lbf[pl.ds((2 * r + p) * WIDE + q, NARROW, stride=2), :] = spread[r * NARROW:(r + 1) * NARROW, lanes]
    for r in range(8):
        rows_r = slice(r * WIDE + 16, r * WIDE + 80)
        gp[r + 1, 16:80] = (lbf[rows_r] * slope_of(pre_l[rows_r])).astype(BF16)
    e4_src = {-1: slice(1, 2), 0: slice(1, 9), 1: slice(8, 9)}
    e4_dst = {-1: slice(9, 10), 0: slice(1, 9), 1: slice(0, 1)}
    e4_scol = {-1: slice(16, 32), 0: slice(16, 80), 1: slice(64, 80)}
    e4 = go([
        copy(gp.at[e4_src[dy], e4_scol[dx]], gp.at[e4_dst[dy], dst_cols[dx]], e4_sem, n, side(dy, dx))
        for n, (dy, dx) in enumerate(SIDES)
    ])

    own_gate = gp[1:9, 16:80].reshape(512, 128)
    for ky in range(3):
        window = jnp.concatenate(
            [im_l[(4 + ky + r) * WIDE + 16:(4 + ky + r) * WIDE + 80] for r in range(8)], axis=0
        )
        level_acc[ky * 384:(ky + 1) * 384] = dot_tn(window, own_gate)
    down_acc[...] = dot_tn(dn[2 * NARROW:6 * NARROW], ng[...])

    def rest_terms(half):
        down = down_acc[:, half_lanes(half)].reshape(16, 2, 16, 128)
        level = level_acc[pl.ds(pl.multiple_of(half * 576, 576), 576), :].reshape(LEVEL_OWNERS, 3, 16, 128)
        return down, level

    down, level = rest_terms(other)
    nothing = jnp.zeros((16 - LEVEL_OWNERS, 3, 16, 128), BF16)
    b_pair_s[:, 0:2] = down.astype(BF16)
    b_pair_s[0:LEVEL_OWNERS, 2:5] = level.astype(BF16)
    b_pair_s[LEVEL_OWNERS:, 2:5] = nothing
    b_pair = go([copy(b_pair_s, b_pair_r, pair_sem, 1, pair_dev)])

    b_pair[0].wait_recv()
    down, level = rest_terms(core)
    b_work[:, 0:2] = (down + b_pair_r[:, 0:2].astype(F32)).astype(BF16)
    b_work[0:LEVEL_OWNERS, 2:5] = (level + b_pair_r[0:LEVEL_OWNERS, 2:5].astype(F32)).astype(BF16)
    b_work[LEVEL_OWNERS:, 2:5] = nothing
    b_plane = plane_stage(b_piece_of, b_xy, xy_sem, 16)

    for c in e4:
        c.wait_recv()
    g2f[0:8] = jnp.zeros((8, 128), F32)
    g2f[8 + 10 * WIDE:] = jnp.zeros((8, 128), F32)
    for r in range(10):
        row_ok = top_ok if r == 0 else bottom_ok if r == 9 else None
        base = 8 + r * WIDE
        left, mid, right = gp[r, 0:16].astype(F32) * left_ok, gp[r, 16:80].astype(F32), gp[r, 80:96].astype(F32) * right_ok
        if row_ok is not None:
            left, mid, right = left * row_ok, mid * row_ok, right * row_ok
        g2f[base:base + 16] = left
        g2f[base + 16:base + 80] = mid
        g2f[base + 80:base + 96] = right
    for r in range(10):
        for kx in range(3):
            start = 7 + kx + r * WIDE
            im_b[r * WIDE:(r + 1) * WIDE, kx * 128:(kx + 1) * 128] = g2f[start:start + WIDE].astype(BF16)
    for q in range(2):
        total = lbf[4 * q * WIDE:(4 * q + 4) * WIDE]
        for ky in range(3):
            total = total + dot(im_b[(4 * q + ky) * WIDE:(4 * q + ky + 4) * WIDE], wlt[ky])
        grad_input[4 * q:4 * q + 4] = total.reshape(4, WIDE, 128)[:, 16:80].astype(BF16)

    for c in near:
        c.wait_recv()
    for p in range(4):
        via_x, via_y = a_work[x, p, 0:ROUTE].astype(F32), a_work[p, y, ROUTE:].astype(F32)
        for k in range(1, 4):
            via_x = via_x + near_a[k, p].astype(F32)
            via_y = via_y + near_b[k, p].astype(F32)
        near_a[0, p] = via_x.astype(BF16)
        near_b[0, p] = via_y.astype(BF16)
    far = []
    for k in (2, 1, 3):
        far.append(copy(near_a.at[0, (y + k) % 4], far_a.at[k], far_sem, k, y_peer[k]))
        far.append(copy(near_b.at[0, (x + k) % 4], far_b.at[k], far_sem, 4 + k, x_peer[k]))
    go(far)

    for c in no_copies:
        c.wait_recv()
    for q in range(4):
        pieces = [no_recv[4 * q + j].astype(F32) for j in range(4)]
        for r in range(4):
            out = pltpu.roll(pieces[3], (32 * (3 - r)) % 128, 1) if r != 3 else pieces[3]
            for j in (2, 1, 0):
                part = pltpu.roll(pieces[j], (32 * (j - r)) % 128, 1) if r != j else pieces[j]
                out = jnp.where(lane < 32 * (j + 1), part, out)
            neck_out[r, :, 128 * q:128 * q + 128] = out.astype(BF16)

    pl.semaphore_wait(known.at[3], 2)

    def z_send(piece, buf, tiles, first, sems, offset):
        copies = []
        for t in range(tiles):
            c = copy_z(piece.at[t], buf.at[z], sems, offset + t, offset + z, column(first + t))
            copies.append((z != first + t, c))
        return copies

    def copy_z(src, dst, sems, ks, kr, dev):
        return pltpu.make_async_remote_copy(
            src_ref=src, dst_ref=dst, send_sem=sems.at[0, ks], recv_sem=sems.at[1, kr],
            device_id=dev, device_id_type=MESH,
        )

    def start_all(copies):
        for cond, c in copies:
            pl.when(cond)(c.start)

    def plane_sum(piece_of, buf, own_ref, copies, out):
        for c in copies:
            c.wait_recv()
        total = own_ref[...].astype(F32)
        for k in range(1, 16):
            total = total + buf[k].astype(F32)
        out[...] = total.astype(BF16)

    def owns(first, tiles):
        return (z >= first) & (z < first + tiles)

    def z_sum(piece, buf, fin, tiles, first, sems, offset, scale):
        @pl.when(owns(first, tiles))
        def _():
            mine = z - first
            for s in range(16):
                @pl.when(z != s)
                def _(s=s):
                    copy_z(piece.at[0], buf.at[s], sems, offset, offset + s, column(s)).wait_recv()
            buf[z] = piece[mine]
            total = buf[0].astype(F32)
            for s in range(1, 16):
                total = total + buf[s].astype(F32)
            fin[mine] = (total * scale).astype(BF16)
            for k in Z_FAR_FIRST:
                copy_z(fin.at[mine], fin.at[mine], zb_sem, offset + k, offset + mine, column((z + k) % 16)).start()

    def z_back(fin, tiles, first, offset):
        for t in range(tiles):
            @pl.when(z != first + t)
            def _(t=t):
                copy_z(fin.at[t], fin.at[t], zb_sem, offset, offset + t, column(first + t)).wait_recv()

    def z_back_sent(fin, tiles, first, offset):
        @pl.when(owns(first, tiles))
        def _():
            for k in Z_FAR_FIRST:
                copy_z(fin.at[0], fin.at[0], zb_sem, offset + k, offset, column((z + k) % 16)).wait_send()

    for c in far:
        c.wait_recv()
    via_x, via_y = near_a[0, y].astype(F32), near_b[0, x].astype(F32)
    for k in range(1, 4):
        via_x = via_x + far_a[k].astype(F32)
        via_y = via_y + far_b[k].astype(F32)
    a_piece[0:ROUTE] = via_x.astype(BF16)
    a_piece[ROUTE:] = via_y.astype(BF16)
    a_zs = z_send(a_piece, a_z, NECK_TILES, 0, z_sem, 0)
    start_all(a_zs)
    plane_sum(b_piece_of, b_xy, b_piece_of(gx), b_plane, b_piece)
    b_zs = z_send(b_piece, b_z, REST_TILES, NECK_TILES, z_sem, 16)
    start_all(b_zs)
    z_sum(a_piece, a_z, a_fin, NECK_TILES, 0, z_sem, 0, scales[0])
    z_sum(b_piece, b_z, b_fin, REST_TILES, NECK_TILES, z_sem, 16, jnp.where(z < NECK_TILES + 2, scales[0], scales[1]))

    z_back(a_fin, NECK_TILES, 0, 0)
    def b_slot(o):
        return b_all.at[core, o]

    a_all[core, x, y] = a_fin[...]
    leg1 = []
    for k in (2, 1, 3):
        mine_x, mine_y = a_all.at[core, x, y, 0:ROUTE], a_all.at[core, x, y, ROUTE:]
        leg1.append(copy(mine_x, mine_x, back1_sem, k, y_peer[k]))
        leg1.append(copy(mine_y, mine_y, back1_sem, 4 + k, x_peer[k]))
    go(leg1)
    z_back(b_fin, REST_TILES, NECK_TILES, 16)
    b_all[core, gx] = b_fin[...]
    b_mine = b_slot(gx)
    go([copy(b_mine, b_mine, xyb_sem, 16 + k, plane[k]) for k in FAR_FIRST])
    for c in leg1:
        c.wait_recv()

    def block_x(c, xx):
        return a_all.at[c, xx, :, 0:ROUTE]

    def block_y(c, yy):
        return a_all.at[c, :, yy, ROUTE:]

    leg2 = []
    for k in (2, 1, 3):
        leg2.append(copy(block_x(core, x), block_x(core, x), back2_sem, k, x_peer[k]))
        leg2.append(copy(block_y(core, y), block_y(core, y), back2_sem, 4 + k, y_peer[k]))
    go(leg2)

    def swap(k):
        bx, by = block_x(core, (x - k + 4) % 4), block_y(core, (y - k + 4) % 4)
        go([copy(bx, bx, pair_sem, 4 + k, pair_dev), copy(by, by, pair_sem, 8 + k, pair_dev)])

    swap(0)
    for k in FAR_FIRST:
        slot = b_slot(in_plane(k, -1))
        copy(slot, slot, xyb_sem, 16 + k, plane[k]).wait_recv()
    go([copy(b_all.at[core], b_all.at[core], pair_sem, 3, pair_dev)])
    for k in (1, 3, 2):
        bx, by = block_x(core, (x - k + 4) % 4), block_y(core, (y - k + 4) % 4)
        copy(bx, bx, back2_sem, k, x_peer[k]).wait_recv()
        copy(by, by, back2_sem, 4 + k, y_peer[k]).wait_recv()
        swap(k)
    copy(b_all.at[other], b_all.at[other], pair_sem, 3, pair_dev).wait_recv()
    for k in range(4):
        bx, by = block_x(other, (x - k + 4) % 4), block_y(other, (y - k + 4) % 4)
        copy(bx, bx, pair_sem, 4 + k, pair_dev).wait_recv()
        copy(by, by, pair_sem, 8 + k, pair_dev).wait_recv()

    for c in sent:
        c.wait_send()
    for cond, c in a_zs + b_zs:
        pl.when(cond)(c.wait_send)
    z_back_sent(a_fin, NECK_TILES, 0, 0)
    z_back_sent(b_fin, REST_TILES, NECK_TILES, 16)


def results_kernel(strip, level, a_all, b_all, neck_out, grad_input, grad_level, grad_down, grad_neck, sems):
    copies = [(strip, neck_out), (level, grad_input)]
    for half in range(2):
        lanes = slice(128 * half, 128 * half + 128)
        copies.append((a_all.at[half], grad_neck.at[:, :, :, :, lanes]))
        copies.append((b_all.at[half, :, 0:2], grad_down.at[:, :, :, lanes]))
        copies.append((b_all.at[half, 0:LEVEL_OWNERS, 2:5], grad_level.at[half]))
    copies = [pltpu.make_async_copy(src, dst, sems.at[n]) for n, (src, dst) in enumerate(copies)]
    for c in copies:
        c.start()
    for c in copies:
        c.wait()


def local(level_in, w_level, w_down, w_neck, cotangent):
    device_count = lax.axis_size("gy") * lax.axis_size("gx")
    level_count = level_in.shape[0] * level_in.shape[1] * device_count
    level_scale = 1.0 / math.sqrt(level_count)
    neck_scale = 1.0 / math.sqrt(level_count // 4)
    vmem = pl.BlockSpec(memory_space=pltpu.VMEM)
    hbm = pl.BlockSpec(memory_space=pltpu.HBM)
    dma = pltpu.SemaphoreType.DMA

    def v(*shape, dtype=BF16):
        return pltpu.VMEM(shape, dtype)

    outs = pl.pallas_call(
        functools.partial(kernel, (neck_scale, level_scale)),
        out_shape=[
            jax.ShapeDtypeStruct((4, 16, 512), BF16),
            jax.ShapeDtypeStruct((8, 64, 128), BF16),
            jax.ShapeDtypeStruct((2, 4, 4, NECK_TILES, 16, 128), BF16),
            jax.ShapeDtypeStruct((2, 16, REST_TILES, 16, 128), BF16),
        ],
        in_specs=[hbm] * 5,
        out_specs=[vmem] * 4,
        scratch_shapes=[
            v(8, 64, 128), v(4, 16, 512),
            v(3, 384, 128), v(512, 256), v(3, 768, 256), v(3, 384, 128),
            v(18, WIDE, 128), v(16 + 18 * WIDE, 128, dtype=F32), v(18 * WIDE, 384),
            v(8 * WIDE, 128, dtype=F32), v(16 * WIDE, 128, dtype=F32), v(8 * NARROW, 512),
            v(16 + 8 * NARROW, 256, dtype=F32), v(8 * NARROW, 768),
            v(6 * NARROW, 256, dtype=F32), v(16 + 6 * NARROW, 256, dtype=F32), v(6 * NARROW, 768),
            v(4 * NARROW, 256), v(4 * NARROW, 256), v(8 * WIDE, 128, dtype=F32),
            v(10, WIDE, 128), v(16 + 10 * WIDE, 128, dtype=F32), v(10 * WIDE, 384),
            v(16, 2, 16, 128), v(16, 2, 16, 128), v(2, NARROW, 256), v(2, NARROW, 256),
            v(16, 16, 128), v(16, 16, 128),
            v(144, 16, 128, dtype=F32), v(1152, 128, dtype=F32), v(512, 256, dtype=F32),
            v(16 * NECK_TILES, 16, 128), v(16 * NECK_TILES, 16, 128), v(4, 4, NECK_TILES, 16, 128),
            v(4, 4, ROUTE, 16, 128), v(4, 4, NECK_TILES - ROUTE, 16, 128),
            v(4, ROUTE, 16, 128), v(4, NECK_TILES - ROUTE, 16, 128),
            v(NECK_TILES, 16, 128), v(16, 16, 128), v(NECK_TILES, 16, 128),
            v(16, REST_TILES, 16, 128), v(16, REST_TILES, 16, 128), v(16, REST_TILES, 16, 128), v(16, REST_TILES, 16, 128),
            v(REST_TILES, 16, 128), v(16, 16, 128), v(REST_TILES, 16, 128),
            dma((5,)), dma((2, 8)), dma((2, 16)), dma((2, 8)), dma((2, 16)), dma((2, 8)),
            dma((2, 12)), dma((2, 32)), dma((2, 32)), dma((2, 32)), dma((2, 32)), dma((2, 8)), dma((2, 8)), dma((2, 8)), dma((2, 8)),
            pltpu.SemaphoreType.REGULAR((5,)),
        ],
        compiler_params=pltpu.CompilerParams(
            collective_id=0, has_side_effects=True, vmem_limit_bytes=24 * 1024 * 1024
        ),
    )(
        *(pltpu.with_memory_space_constraint(t, pltpu.HBM) for t in (
            level_in,
            w_level.reshape(3, 384, 128),
            w_down.reshape(512, 256),
            w_neck.reshape(3, 768, 256),
            jnp.transpose(cotangent, (0, 2, 1)),
        ))
    )
    outs = pl.pallas_call(
        results_kernel,
        out_shape=[
            jax.ShapeDtypeStruct((4, 16, 512), BF16),
            jax.ShapeDtypeStruct((8, 64, 128), BF16),
            jax.ShapeDtypeStruct((2, LEVEL_OWNERS, 3, 16, 128), BF16),
            jax.ShapeDtypeStruct((16, 2, 16, 256), BF16),
            jax.ShapeDtypeStruct((4, 4, NECK_TILES, 16, 256), BF16),
        ],
        in_specs=[vmem] * 4,
        out_specs=[hbm] * 5,
        scratch_shapes=[dma((8,))],
        compiler_params=pltpu.CompilerParams(vmem_limit_bytes=1024 * 1024),
    )(*outs)
    return (
        jnp.transpose(outs[0], (0, 2, 1)),
        outs[1],
        outs[2].reshape(w_level.shape),
        outs[3].reshape(w_down.shape),
        outs[4].reshape(w_neck.shape),
    )


def solution(mesh):
    return jax.shard_map(
        local,
        mesh=mesh,
        in_specs=(P("gy", "gx", None), P(), P(), P(), P("gy", None, "gx")),
        out_specs=(P("gy", None, "gx"), P("gy", "gx", None), P(), P(), P()),
        check_vma=False,
    )
```

```python
import functools
import math

import jax
import jax.numpy as jnp
from jax import lax
from jax.experimental import pallas as pl
from jax.experimental.pallas import tpu as pltpu
from jax.sharding import PartitionSpec as P

MESH = pl.DeviceIdType.MESH
BF16, F32 = jnp.bfloat16, jnp.float32

RIM = 5
WIDE = 96
NARROW = 48
SIDES = [(dy, dx) for dy in (-1, 0, 1) for dx in (-1, 0, 1) if (dy, dx) != (0, 0)]
FAR_FIRST = sorted(range(1, 16), key=lambda k: -(min(k // 4, 4 - k // 4) + min(k % 4, 4 - k % 4)))
Z_FAR_FIRST = sorted(range(1, 16), key=lambda k: -min(k, 16 - k))
NECK_TILES = 9
ROUTE = 5
REST_TILES = 5
LEVEL_OWNERS = 12


def slope_of(v):
    s = jax.nn.sigmoid(v)
    return s + v * s * (1.0 - s)


def dot(a, b):
    return jnp.dot(a, b, preferred_element_type=F32)


def dot_nt(a, b):
    return lax.dot_general(a, b, (((1,), (1,)), ((), ())), preferred_element_type=F32)


def dot_tn(a, b):
    return lax.dot_general(a, b, (((0,), (0,)), ((), ())), preferred_element_type=F32)


def kernel(
    scales,
    level_in, wl_hbm, wd_hbm, wn_hbm, cot_hbm,
    neck_out, grad_input, a_all, b_all,
    level_own, cot_in, wl, wd, wn, wlt,
    lp, lf, im_l, pre_l, act, dn, nf, im_n, cf, gf, im_g, gate_own, ng, lbf, gp, g2f, im_b,
    cot_send, cot_recv, ct, hr, no_send, no_recv,
    neck_own, level_acc, down_acc,
    a_pair_s, a_pair_r, a_work, near_a, near_b, far_a, far_b, a_piece, a_z, a_fin,
    b_pair_s, b_pair_r, b_work, b_xy, b_piece, b_z, b_fin,
    w_sem, e1_sem, cot_sem, ch_sem, no_sem, e4_sem,
    pair_sem, xy_sem, z_sem, zb_sem, xyb_sem, near_sem, far_sem, back1_sem, back2_sem, known,
):
    gy, gx = lax.axis_index("gy"), lax.axis_index("gx")
    z, core = gy // 2, gy % 2
    other = 1 - core

    def side(dy, dx):
        return ((gy + dy + 32) % 32, (gx + dx + 16) % 16)

    pair_dev = (z * 2 + other, gx)
    x, y = gx // 4, gx % 4

    def in_plane(k, sign=1):
        return ((x + sign * (k // 4) + 4) % 4) * 4 + (y + sign * (k % 4) + 4) % 4

    plane = [None] + [(gy, in_plane(k)) for k in range(1, 16)]

    def column(zz):
        return (zz * 2 + core, gx)

    loads = [
        pltpu.make_async_copy(cot_hbm, cot_in, w_sem.at[3]),
        pltpu.make_async_copy(level_in, level_own, w_sem.at[4]),
        pltpu.make_async_copy(wl_hbm, wl, w_sem.at[0]),
        pltpu.make_async_copy(wd_hbm, wd, w_sem.at[1]),
        pltpu.make_async_copy(wn_hbm, wn, w_sem.at[2]),
    ]
    for load in loads[:2]:
        load.start()
    barrier = pltpu.get_barrier_semaphore()
    x_peer = [None] + [(gy, (x + k) % 4 * 4 + y) for k in range(1, 4)]
    y_peer = [None] + [(gy, x * 4 + (y + k) % 4) for k in range(1, 4)]
    peers = x_peer[1:] + y_peer[1:] + [side(dy, dx) for dy, dx in SIDES]
    for peer in peers:
        pl.semaphore_signal(barrier, inc=1, device_id=peer, device_id_type=MESH)

    def copy(src, dst, sems, k, dev):
        return pltpu.make_async_remote_copy(
            src_ref=src, dst_ref=dst, send_sem=sems.at[0, k], recv_sem=sems.at[1, k],
            device_id=dev, device_id_type=MESH,
        )

    sent = []

    def go(copies):
        for c in copies:
            c.start()
        sent.extend(copies)
        return copies

    pl.semaphore_wait(barrier, len(peers))
    def tell(n):
        for dy in (-1, 1):
            pl.semaphore_signal(known.at[n], inc=1, device_id=side(dy * 2 ** n, 0), device_id_type=MESH)

    for k in range(1, 4):
        pl.semaphore_signal(known.at[4], inc=1, device_id=y_peer[k], device_id_type=MESH)
    src_rows = {-1: slice(0, RIM), 0: slice(0, 8), 1: slice(8 - RIM, 8)}
    src_cols = {-1: slice(0, 16), 0: slice(0, 64), 1: slice(48, 64)}
    dst_rows = {-1: slice(RIM + 8, RIM + 8 + RIM), 0: slice(RIM, RIM + 8), 1: slice(0, RIM)}
    dst_cols = {-1: slice(80, 96), 0: slice(16, 80), 1: slice(0, 16)}
    e1 = go([
        copy(level_in.at[src_rows[dy], src_cols[dx]], lp.at[dst_rows[dy], dst_cols[dx]], e1_sem, n, side(dy, dx))
        for n, (dy, dx) in enumerate(SIDES)
    ])

    tell(0)
    loads[0].wait()
    for load in loads[2:]:
        load.start()
    lane = lax.broadcasted_iota(jnp.int32, (16, 128), 1)
    for q in range(4):
        rows = [cot_in[r, :, 128 * q:128 * q + 128].astype(F32) for r in range(4)]
        for j in range(4):
            out = pltpu.roll(rows[3], (32 * (3 - j)) % 128, 1) if j != 3 else rows[3]
            for r in (2, 1, 0):
                part = pltpu.roll(rows[r], (32 * (r - j)) % 128, 1) if r != j else rows[r]
                out = jnp.where(lane < 32 * (r + 1), part, out)
            cot_send[4 * q + j, 0] = out.astype(BF16)
    for t in range(16):
        cot_send[t, 1] = jnp.where(lane % 32 < 16, cot_send[(t + 1) % 16, 0].astype(F32), cot_send[(t + 15) % 16, 0].astype(F32)).astype(BF16)
    cot_recv[gx] = cot_send[gx]

    top_ok = jnp.where(gy > 0, 1.0, 0.0).astype(F32)
    bottom_ok = jnp.where(gy < 31, 1.0, 0.0).astype(F32)
    left_ok = jnp.where(gx > 0, 1.0, 0.0).astype(F32)
    right_ok = jnp.where(gx < 15, 1.0, 0.0).astype(F32)

    pl.semaphore_wait(known.at[4], 3)
    cot_copies = go([
        copy(cot_send.at[in_plane(k)], cot_recv.at[gx], cot_sem, k, plane[k]) for k in FAR_FIRST
    ])
    loads[1].wait()
    lf[0:8] = jnp.zeros((8, 128), F32)
    lf[8 + 18 * WIDE:] = jnp.zeros((8, 128), F32)
    for r in range(8):
        start = 8 + (r + RIM) * WIDE + 16
        lf[start:start + 64] = level_own[r].astype(F32)

    pl.semaphore_wait(known.at[0], 2)
    tell(1)

    loads[2].wait()
    for ky in range(3):
        for kx in range(3):
            w = wl[2 - ky, (2 - kx) * 128:(3 - kx) * 128, :].astype(F32)
            wlt[ky, kx * 128:(kx + 1) * 128, :] = w.T.astype(BF16)

    for c in cot_copies:
        c.wait_recv()
    cot_tile = cot_recv[:, 0].reshape(256, 128).astype(F32).T
    cot_beside = cot_recv[:, 1].reshape(256, 128).astype(F32).T
    for r in range(4):
        base = (r + 1) * NARROW
        cf[base:base + 8] = cot_beside[32 * r + 24:32 * r + 32] * left_ok
        cf[base + 8:base + 40] = cot_tile[32 * r:32 * r + 32]
        cf[base + 40:base + 48] = cot_beside[32 * r:32 * r + 8] * right_ok
    ct[0] = cf[NARROW:2 * NARROW].astype(BF16)
    ct[1] = cf[4 * NARROW:5 * NARROW].astype(BF16)
    ch = go([copy(ct.at[n], hr.at[n], ch_sem, n, side(2 * n - 1, 0)) for n in range(2)])

    pl.semaphore_wait(known.at[1], 2)
    tell(2)

    for c in e1:
        c.wait_recv()
    for r in range(18):
        row_ok = top_ok if r < RIM else bottom_ok if r >= RIM + 8 else None
        base = 8 + r * WIDE
        left = lp[r, 0:16].astype(F32) * left_ok
        right = lp[r, 80:96].astype(F32) * right_ok
        if row_ok is not None:
            left, right = left * row_ok, right * row_ok
            lf[base + 16:base + 80] = lp[r, 16:80].astype(F32) * row_ok
        lf[base:base + 16] = left
        lf[base + 80:base + 96] = right
    for r in range(18):
        for kx in range(3):
            start = 7 + kx + r * WIDE
            im_l[r * WIDE:(r + 1) * WIDE, kx * 128:(kx + 1) * 128] = lf[start:start + WIDE].astype(BF16)

    for q in range(4):
        pre = dot(im_l[4 * q * WIDE:(4 * q + 4) * WIDE], wl[0])
        for ky in (1, 2):
            pre = pre + dot(im_l[(4 * q + ky) * WIDE:(4 * q + ky + 4) * WIDE], wl[ky])
        own = lf[8 + (4 * q + 1) * WIDE:8 + (4 * q + 5) * WIDE]
        act[4 * q * WIDE:(4 * q + 4) * WIDE] = own + pre * jax.nn.sigmoid(pre)
        if q in (1, 2):
            pre_l[(q - 1) * 4 * WIDE:q * 4 * WIDE] = pre

    for rr in range(16):
        for q in range(2):
            lanes = slice(128 * (2 * (rr % 2) + q), 128 * (2 * (rr % 2) + q) + 128)
            dn[(rr // 2) * NARROW:(rr // 2 + 1) * NARROW, lanes] = act[pl.ds(rr * WIDE + q, NARROW, stride=2), :].astype(BF16)
    loads[3].wait()
    col = lax.broadcasted_iota(jnp.int32, (NARROW, 256), 0)
    col_ok = jnp.where(col < 8, left_ok, jnp.where(col >= 40, right_ok, 1.0))
    col_own = jnp.where((col >= 8) & (col < 40), 1.0, 0.0)
    nf[0:8] = jnp.zeros((8, 256), F32)
    nf[8 + 8 * NARROW:] = jnp.zeros((8, 256), F32)
    neck_in = dot(dn[...], wd[...]).astype(BF16).astype(F32)
    for r in range(8):
        row = neck_in[r * NARROW:(r + 1) * NARROW] * col_ok
        if r < 2:
            row = row * top_ok
        if r >= 6:
            row = row * bottom_ok
        nf[8 + r * NARROW:8 + (r + 1) * NARROW] = row
    for kx in range(3):
        im_n[:, kx * 256:(kx + 1) * 256] = nf[7 + kx:7 + kx + 8 * NARROW].astype(BF16)
    loads[4].wait()
    neck_pre = dot(im_n[0:6 * NARROW], wn[0])
    for ky in (1, 2):
        neck_pre = neck_pre + dot(im_n[ky * NARROW:(ky + 6) * NARROW], wn[ky])

    own = slice(NARROW, 5 * NARROW)
    gf[0:8] = jnp.zeros((8, 256), F32)
    gf[8 + 6 * NARROW:] = jnp.zeros((8, 256), F32)
    gate = (cf[own] * slope_of(neck_pre[own])).astype(BF16).astype(F32)
    gf[8 + NARROW:8 + 5 * NARROW] = gate
    for r in range(4):
        gate_own[r * NARROW:(r + 1) * NARROW] = (gate[r * NARROW:(r + 1) * NARROW] * col_own).astype(BF16)

    def half_lanes(half):
        return pl.ds(pl.multiple_of(half * 128, 128), 128)

    theirs = gate_own[:, half_lanes(other)]
    for ky in range(3):
        part = dot_tn(im_n[(1 + ky) * NARROW:(5 + ky) * NARROW], theirs)
        a_pair_s[48 * ky:48 * ky + 48] = part.astype(BF16).reshape(48, 16, 128)
    a_pair = go([copy(a_pair_s, a_pair_r, pair_sem, 0, pair_dev)])
    pl.semaphore_wait(known.at[2], 2)
    tell(3)
    mine = gate_own[:, half_lanes(core)]
    for ky in range(3):
        neck_own[48 * ky:48 * ky + 48] = dot_tn(im_n[(1 + ky) * NARROW:(5 + ky) * NARROW], mine).reshape(48, 16, 128)

    def plane_stage(work, buf, sems, first):
        return go([copy(work(in_plane(k)), buf.at[k], sems, first + k, plane[k]) for k in FAR_FIRST])

    def b_piece_of(o):
        return b_work.at[o]

    a_pair[0].wait_recv()
    for n in range(16):
        part = slice(n * NECK_TILES, (n + 1) * NECK_TILES)
        a_work[n // 4, n % 4] = (neck_own[part] + a_pair_r[part].astype(F32)).astype(BF16)
    near = []
    for k in (2, 1, 3):
        near.append(copy(a_work.at[(x + k) % 4, :, 0:ROUTE], near_a.at[k], near_sem, k, x_peer[k]))
        near.append(copy(a_work.at[:, (y + k) % 4, ROUTE:], near_b.at[k], near_sem, 4 + k, y_peer[k]))
    go(near)

    for c in ch:
        c.wait_recv()
    for n, ok, rows in ((1, top_ok, slice(0, NARROW)), (0, bottom_ok, slice(5 * NARROW, 6 * NARROW))):
        v = hr[n].astype(F32) * ok * slope_of(neck_pre[rows])
        gf[8 + rows.start:8 + rows.stop] = v.astype(BF16).astype(F32)

    for kx in range(3):
        im_g[:, kx * 256:(kx + 1) * 256] = gf[7 + kx:7 + kx + 6 * NARROW].astype(BF16)
    back = None
    for ky in range(3):
        for kx in range(3):
            term = dot_nt(
                im_g[ky * NARROW:(ky + 4) * NARROW, kx * 256:(kx + 1) * 256],
                wn[2 - ky, (2 - kx) * 256:(3 - kx) * 256, :],
            )
            back = term if back is None else back + term
    for r in range(4):
        v = cf[(r + 1) * NARROW:(r + 2) * NARROW] + back[r * NARROW:(r + 1) * NARROW]
        ng[r * NARROW:(r + 1) * NARROW] = (v * col_own).astype(BF16)
    spread = dot_nt(ng[...], wd[...])
    for r in range(4):
        for p in range(2):
            for q in range(2):
                lanes = slice(128 * (2 * p + q), 128 * (2 * p + q) + 128)
                lbf[pl.ds((2 * r + p) * WIDE + q, NARROW, stride=2), :] = spread[r * NARROW:(r + 1) * NARROW, lanes]
    for r in range(8):
        rows_r = slice(r * WIDE + 16, r * WIDE + 80)
        gp[r + 1, 16:80] = (lbf[rows_r] * slope_of(pre_l[rows_r])).astype(BF16)
    own_gate = gp[1:9, 16:80].reshape(512, 128)
    for ky in range(3):
        window = jnp.concatenate(
            [im_l[(4 + ky + r) * WIDE + 16:(4 + ky + r) * WIDE + 80] for r in range(8)], axis=0
        )
        level_acc[ky * 384:(ky + 1) * 384] = dot_tn(window, own_gate)
    down_acc[...] = dot_tn(dn[2 * NARROW:6 * NARROW], ng[...])

    def rest_terms(half):
        down = down_acc[:, half_lanes(half)].reshape(16, 2, 16, 128)
        level = level_acc[pl.ds(pl.multiple_of(half * 576, 576), 576), :].reshape(LEVEL_OWNERS, 3, 16, 128)
        return down, level

    down, level = rest_terms(other)
    nothing = jnp.zeros((16 - LEVEL_OWNERS, 3, 16, 128), BF16)
    b_pair_s[:, 0:2] = down.astype(BF16)
    b_pair_s[0:LEVEL_OWNERS, 2:5] = level.astype(BF16)
    b_pair_s[LEVEL_OWNERS:, 2:5] = nothing
    b_pair = go([copy(b_pair_s, b_pair_r, pair_sem, 1, pair_dev)])

    b_pair[0].wait_recv()
    down, level = rest_terms(core)
    b_work[:, 0:2] = (down + b_pair_r[:, 0:2].astype(F32)).astype(BF16)
    b_work[0:LEVEL_OWNERS, 2:5] = (level + b_pair_r[0:LEVEL_OWNERS, 2:5].astype(F32)).astype(BF16)
    b_work[LEVEL_OWNERS:, 2:5] = nothing
    b_plane = plane_stage(b_piece_of, b_xy, xy_sem, 16)

    e4_src = {-1: slice(1, 2), 0: slice(1, 9), 1: slice(8, 9)}
    e4_dst = {-1: slice(9, 10), 0: slice(1, 9), 1: slice(0, 1)}
    e4_scol = {-1: slice(16, 32), 0: slice(16, 80), 1: slice(64, 80)}
    e4 = go([
        copy(gp.at[e4_src[dy], e4_scol[dx]], gp.at[e4_dst[dy], dst_cols[dx]], e4_sem, n, side(dy, dx))
        for n, (dy, dx) in enumerate(SIDES)
    ])

    for c in near:
        c.wait_recv()
    for p in range(4):
        via_x, via_y = a_work[x, p, 0:ROUTE].astype(F32), a_work[p, y, ROUTE:].astype(F32)
        for k in range(1, 4):
            via_x = via_x + near_a[k, p].astype(F32)
            via_y = via_y + near_b[k, p].astype(F32)
        near_a[0, p] = via_x.astype(BF16)
        near_b[0, p] = via_y.astype(BF16)
    far = []
    for k in (2, 1, 3):
        far.append(copy(near_a.at[0, (y + k) % 4], far_a.at[k], far_sem, k, y_peer[k]))
        far.append(copy(near_b.at[0, (x + k) % 4], far_b.at[k], far_sem, 4 + k, x_peer[k]))
    go(far)

    rows = []
    for r in range(4):
        v = neck_pre[(r + 1) * NARROW + 8:(r + 1) * NARROW + 40]
        rows.append(nf[8 + (r + 2) * NARROW + 8:8 + (r + 2) * NARROW + 40] + v * jax.nn.sigmoid(v))
    no_send[...] = jnp.concatenate(rows, axis=0).T.astype(BF16).reshape(16, 16, 128)
    no_recv[gx] = no_send[gx]
    no_copies = go([copy(no_send.at[in_plane(k)], no_recv.at[gx], no_sem, k, plane[k]) for k in FAR_FIRST])

    pl.semaphore_wait(known.at[3], 2)

    def z_send(piece, buf, tiles, first, sems, offset):
        copies = []
        for k in Z_FAR_FIRST:
            t = (z + k) % 16 - first
            c = copy_z(piece.at[t], buf.at[z], sems, offset + k, offset + z, column((z + k) % 16))
            copies.append(((t >= 0) & (t < tiles), c))
        return copies

    def copy_z(src, dst, sems, ks, kr, dev):
        return pltpu.make_async_remote_copy(
            src_ref=src, dst_ref=dst, send_sem=sems.at[0, ks], recv_sem=sems.at[1, kr],
            device_id=dev, device_id_type=MESH,
        )

    def start_all(copies):
        for cond, c in copies:
            pl.when(cond)(c.start)

    def plane_sum(piece_of, buf, own_ref, copies, out):
        for c in copies:
            c.wait_recv()
        total = own_ref[...].astype(F32)
        for k in range(1, 16):
            total = total + buf[k].astype(F32)
        out[...] = total.astype(BF16)

    def owns(first, tiles):
        return (z >= first) & (z < first + tiles)

    def z_sum(piece, buf, fin, tiles, first, sems, offset, scale):
        @pl.when(owns(first, tiles))
        def _():
            mine = z - first
            for s in range(16):
                @pl.when(z != s)
                def _(s=s):
                    copy_z(piece.at[0], buf.at[s], sems, offset, offset + s, column(s)).wait_recv()
            buf[z] = piece[mine]
            total = buf[0].astype(F32)
            for s in range(1, 16):
                total = total + buf[s].astype(F32)
            fin[mine] = (total * scale).astype(BF16)
            for k in Z_FAR_FIRST:
                copy_z(fin.at[mine], fin.at[mine], zb_sem, offset + k, offset + mine, column((z + k) % 16)).start()

    def z_back(fin, tiles, first, offset):
        for t in range(tiles):
            @pl.when(z != first + t)
            def _(t=t):
                copy_z(fin.at[t], fin.at[t], zb_sem, offset, offset + t, column(first + t)).wait_recv()

    def z_back_sent(fin, tiles, first, offset):
        @pl.when(owns(first, tiles))
        def _():
            for k in Z_FAR_FIRST:
                copy_z(fin.at[0], fin.at[0], zb_sem, offset + k, offset, column((z + k) % 16)).wait_send()

    for c in far:
        c.wait_recv()
    via_x, via_y = near_a[0, y].astype(F32), near_b[0, x].astype(F32)
    for k in range(1, 4):
        via_x = via_x + far_a[k].astype(F32)
        via_y = via_y + far_b[k].astype(F32)
    a_piece[0:ROUTE] = via_x.astype(BF16)
    a_piece[ROUTE:] = via_y.astype(BF16)
    a_zs = z_send(a_piece, a_z, NECK_TILES, 0, z_sem, 0)
    start_all(a_zs)
    plane_sum(b_piece_of, b_xy, b_piece_of(gx), b_plane, b_piece)
    b_zs = z_send(b_piece, b_z, REST_TILES, NECK_TILES, z_sem, 16)
    start_all(b_zs)
    for c in e4:
        c.wait_recv()
    g2f[0:8] = jnp.zeros((8, 128), F32)
    g2f[8 + 10 * WIDE:] = jnp.zeros((8, 128), F32)
    for r in range(10):
        row_ok = top_ok if r == 0 else bottom_ok if r == 9 else None
        base = 8 + r * WIDE
        left, mid, right = gp[r, 0:16].astype(F32) * left_ok, gp[r, 16:80].astype(F32), gp[r, 80:96].astype(F32) * right_ok
        if row_ok is not None:
            left, mid, right = left * row_ok, mid * row_ok, right * row_ok
        g2f[base:base + 16] = left
        g2f[base + 16:base + 80] = mid
        g2f[base + 80:base + 96] = right
    for r in range(10):
        for kx in range(3):
            start = 7 + kx + r * WIDE
            im_b[r * WIDE:(r + 1) * WIDE, kx * 128:(kx + 1) * 128] = g2f[start:start + WIDE].astype(BF16)
    for q in range(2):
        total = lbf[4 * q * WIDE:(4 * q + 4) * WIDE]
        for ky in range(3):
            total = total + dot(im_b[(4 * q + ky) * WIDE:(4 * q + ky + 4) * WIDE], wlt[ky])
        grad_input[4 * q:4 * q + 4] = total.reshape(4, WIDE, 128)[:, 16:80].astype(BF16)

    for c in no_copies:
        c.wait_recv()
    for q in range(4):
        pieces = [no_recv[4 * q + j].astype(F32) for j in range(4)]
        for r in range(4):
            out = pltpu.roll(pieces[3], (32 * (3 - r)) % 128, 1) if r != 3 else pieces[3]
            for j in (2, 1, 0):
                part = pltpu.roll(pieces[j], (32 * (j - r)) % 128, 1) if r != j else pieces[j]
                out = jnp.where(lane < 32 * (j + 1), part, out)
            neck_out[r, :, 128 * q:128 * q + 128] = out.astype(BF16)

    z_sum(a_piece, a_z, a_fin, NECK_TILES, 0, z_sem, 0, scales[0])
    z_sum(b_piece, b_z, b_fin, REST_TILES, NECK_TILES, z_sem, 16, jnp.where(z < NECK_TILES + 2, scales[0], scales[1]))

    z_back(a_fin, NECK_TILES, 0, 0)
    def b_slot(o):
        return b_all.at[core, o]

    a_all[core, x, y] = a_fin[...]
    leg1 = []
    for k in (2, 1, 3):
        mine_x, mine_y = a_all.at[core, x, y, 0:ROUTE], a_all.at[core, x, y, ROUTE:]
        leg1.append(copy(mine_x, mine_x, back1_sem, k, y_peer[k]))
        leg1.append(copy(mine_y, mine_y, back1_sem, 4 + k, x_peer[k]))
    go(leg1)
    z_back(b_fin, REST_TILES, NECK_TILES, 16)
    b_all[core, gx] = b_fin[...]
    b_mine = b_slot(gx)
    go([copy(b_mine, b_mine, xyb_sem, 16 + k, plane[k]) for k in FAR_FIRST])
    for c in leg1:
        c.wait_recv()

    def block_x(c, xx):
        return a_all.at[c, xx, :, 0:ROUTE]

    def block_y(c, yy):
        return a_all.at[c, :, yy, ROUTE:]

    leg2 = []
    for k in (2, 1, 3):
        leg2.append(copy(block_x(core, x), block_x(core, x), back2_sem, k, x_peer[k]))
        leg2.append(copy(block_y(core, y), block_y(core, y), back2_sem, 4 + k, y_peer[k]))
    go(leg2)

    def swap(k):
        bx, by = block_x(core, (x - k + 4) % 4), block_y(core, (y - k + 4) % 4)
        go([copy(bx, bx, pair_sem, 4 + k, pair_dev), copy(by, by, pair_sem, 8 + k, pair_dev)])

    swap(0)
    for k in FAR_FIRST:
        slot = b_slot(in_plane(k, -1))
        copy(slot, slot, xyb_sem, 16 + k, plane[k]).wait_recv()
    go([copy(b_all.at[core], b_all.at[core], pair_sem, 3, pair_dev)])
    for k in (1, 3, 2):
        bx, by = block_x(core, (x - k + 4) % 4), block_y(core, (y - k + 4) % 4)
        copy(bx, bx, back2_sem, k, x_peer[k]).wait_recv()
        copy(by, by, back2_sem, 4 + k, y_peer[k]).wait_recv()
        swap(k)
    copy(b_all.at[other], b_all.at[other], pair_sem, 3, pair_dev).wait_recv()
    for k in range(4):
        bx, by = block_x(other, (x - k + 4) % 4), block_y(other, (y - k + 4) % 4)
        copy(bx, bx, pair_sem, 4 + k, pair_dev).wait_recv()
        copy(by, by, pair_sem, 8 + k, pair_dev).wait_recv()

    for c in sent:
        c.wait_send()
    for cond, c in a_zs + b_zs:
        pl.when(cond)(c.wait_send)
    z_back_sent(a_fin, NECK_TILES, 0, 0)
    z_back_sent(b_fin, REST_TILES, NECK_TILES, 16)


def results_kernel(strip, level, a_all, b_all, neck_out, grad_input, grad_level, grad_down, grad_neck, sems):
    copies = [(strip, neck_out), (level, grad_input)]
    for half in range(2):
        lanes = slice(128 * half, 128 * half + 128)
        copies.append((a_all.at[half], grad_neck.at[:, :, :, :, lanes]))
        copies.append((b_all.at[half, :, 0:2], grad_down.at[:, :, :, lanes]))
        copies.append((b_all.at[half, 0:LEVEL_OWNERS, 2:5], grad_level.at[half]))
    copies = [pltpu.make_async_copy(src, dst, sems.at[n]) for n, (src, dst) in enumerate(copies)]
    for c in copies:
        c.start()
    for c in copies:
        c.wait()


def local(level_in, w_level, w_down, w_neck, cotangent):
    device_count = lax.axis_size("gy") * lax.axis_size("gx")
    level_count = level_in.shape[0] * level_in.shape[1] * device_count
    level_scale = 1.0 / math.sqrt(level_count)
    neck_scale = 1.0 / math.sqrt(level_count // 4)
    vmem = pl.BlockSpec(memory_space=pltpu.VMEM)
    hbm = pl.BlockSpec(memory_space=pltpu.HBM)
    dma = pltpu.SemaphoreType.DMA

    def v(*shape, dtype=BF16):
        return pltpu.VMEM(shape, dtype)

    outs = pl.pallas_call(
        functools.partial(kernel, (neck_scale, level_scale)),
        out_shape=[
            jax.ShapeDtypeStruct((4, 16, 512), BF16),
            jax.ShapeDtypeStruct((8, 64, 128), BF16),
            jax.ShapeDtypeStruct((2, 4, 4, NECK_TILES, 16, 128), BF16),
            jax.ShapeDtypeStruct((2, 16, REST_TILES, 16, 128), BF16),
        ],
        in_specs=[hbm] * 5,
        out_specs=[vmem] * 4,
        scratch_shapes=[
            v(8, 64, 128), v(4, 16, 512),
            v(3, 384, 128), v(512, 256), v(3, 768, 256), v(3, 384, 128),
            v(18, WIDE, 128), v(16 + 18 * WIDE, 128, dtype=F32), v(18 * WIDE, 384),
            v(8 * WIDE, 128, dtype=F32), v(16 * WIDE, 128, dtype=F32), v(8 * NARROW, 512),
            v(16 + 8 * NARROW, 256, dtype=F32), v(8 * NARROW, 768),
            v(6 * NARROW, 256, dtype=F32), v(16 + 6 * NARROW, 256, dtype=F32), v(6 * NARROW, 768),
            v(4 * NARROW, 256), v(4 * NARROW, 256), v(8 * WIDE, 128, dtype=F32),
            v(10, WIDE, 128), v(16 + 10 * WIDE, 128, dtype=F32), v(10 * WIDE, 384),
            v(16, 2, 16, 128), v(16, 2, 16, 128), v(2, NARROW, 256), v(2, NARROW, 256),
            v(16, 16, 128), v(16, 16, 128),
            v(144, 16, 128, dtype=F32), v(1152, 128, dtype=F32), v(512, 256, dtype=F32),
            v(16 * NECK_TILES, 16, 128), v(16 * NECK_TILES, 16, 128), v(4, 4, NECK_TILES, 16, 128),
            v(4, 4, ROUTE, 16, 128), v(4, 4, NECK_TILES - ROUTE, 16, 128),
            v(4, ROUTE, 16, 128), v(4, NECK_TILES - ROUTE, 16, 128),
            v(NECK_TILES, 16, 128), v(16, 16, 128), v(NECK_TILES, 16, 128),
            v(16, REST_TILES, 16, 128), v(16, REST_TILES, 16, 128), v(16, REST_TILES, 16, 128), v(16, REST_TILES, 16, 128),
            v(REST_TILES, 16, 128), v(16, 16, 128), v(REST_TILES, 16, 128),
            dma((5,)), dma((2, 8)), dma((2, 16)), dma((2, 8)), dma((2, 16)), dma((2, 8)),
            dma((2, 12)), dma((2, 32)), dma((2, 32)), dma((2, 32)), dma((2, 32)), dma((2, 8)), dma((2, 8)), dma((2, 8)), dma((2, 8)),
            pltpu.SemaphoreType.REGULAR((5,)),
        ],
        compiler_params=pltpu.CompilerParams(
            collective_id=0, has_side_effects=True, vmem_limit_bytes=24 * 1024 * 1024
        ),
    )(
        *(pltpu.with_memory_space_constraint(t, pltpu.HBM) for t in (
            level_in,
            w_level.reshape(3, 384, 128),
            w_down.reshape(512, 256),
            w_neck.reshape(3, 768, 256),
            jnp.transpose(cotangent, (0, 2, 1)),
        ))
    )
    outs = pl.pallas_call(
        results_kernel,
        out_shape=[
            jax.ShapeDtypeStruct((4, 16, 512), BF16),
            jax.ShapeDtypeStruct((8, 64, 128), BF16),
            jax.ShapeDtypeStruct((2, LEVEL_OWNERS, 3, 16, 128), BF16),
            jax.ShapeDtypeStruct((16, 2, 16, 256), BF16),
            jax.ShapeDtypeStruct((4, 4, NECK_TILES, 16, 256), BF16),
        ],
        in_specs=[vmem] * 4,
        out_specs=[hbm] * 5,
        scratch_shapes=[dma((8,))],
        compiler_params=pltpu.CompilerParams(vmem_limit_bytes=1024 * 1024),
    )(*outs)
    return (
        jnp.transpose(outs[0], (0, 2, 1)),
        outs[1],
        outs[2].reshape(w_level.shape),
        outs[3].reshape(w_down.shape),
        outs[4].reshape(w_neck.shape),
    )


def solution(mesh):
    return jax.shard_map(
        local,
        mesh=mesh,
        in_specs=(P("gy", "gx", None), P(), P(), P(), P("gy", None, "gx")),
        out_specs=(P("gy", None, "gx"), P("gy", "gx", None), P(), P(), P()),
        check_vma=False,
    )
```

```python
import functools
import math

import jax
import jax.numpy as jnp
from jax import lax
from jax.experimental import pallas as pl
from jax.experimental.pallas import tpu as pltpu
from jax.sharding import PartitionSpec as P

MESH = pl.DeviceIdType.MESH
BF16, F32 = jnp.bfloat16, jnp.float32

RIM = 5
WIDE = 96
NARROW = 48
SIDES = [(dy, dx) for dy in (-1, 0, 1) for dx in (-1, 0, 1) if (dy, dx) != (0, 0)]
FAR_FIRST = sorted(range(1, 16), key=lambda k: -(min(k // 4, 4 - k // 4) + min(k % 4, 4 - k % 4)))
Z_FAR_FIRST = sorted(range(1, 16), key=lambda k: -min(k, 16 - k))
NECK_TILES = 9
ROUTE = 5
REST_TILES = 5
LEVEL_OWNERS = 12


def slope_of(v):
    s = jax.nn.sigmoid(v)
    return s + v * s * (1.0 - s)


def dot(a, b):
    return jnp.dot(a, b, preferred_element_type=F32)


def dot_nt(a, b):
    return lax.dot_general(a, b, (((1,), (1,)), ((), ())), preferred_element_type=F32)


def dot_tn(a, b):
    return lax.dot_general(a, b, (((0,), (0,)), ((), ())), preferred_element_type=F32)


def kernel(
    scales,
    level_in, wl_hbm, wd_hbm, wn_hbm, cot_hbm,
    neck_out, grad_input, a_all, b_all,
    level_own, cot_in, wl, wd, wn, wlt,
    lp, lf, im_l, pre_l, act, dn, nf, im_n, cf, gf, im_g, gate_own, ng, lbf, gp, g2f, im_b,
    cot_send, cot_recv, ct, hr, no_send, no_recv,
    neck_own, level_acc, down_acc,
    a_pair_s, a_pair_r, a_work, near_a, near_b, far_a, far_b, a_piece, a_z, a_fin,
    b_pair_s, b_pair_r, b_work, b_xy, b_piece, b_z, b_fin,
    w_sem, e1_sem, cot_sem, ch_sem, no_sem, e4_sem,
    pair_sem, xy_sem, z_sem, zb_sem, xyb_sem, near_sem, far_sem, back1_sem, back2_sem, known,
):
    gy, gx = lax.axis_index("gy"), lax.axis_index("gx")
    z, core = gy // 2, gy % 2
    other = 1 - core

    def side(dy, dx):
        return ((gy + dy + 32) % 32, (gx + dx + 16) % 16)

    pair_dev = (z * 2 + other, gx)
    x, y = gx // 4, gx % 4

    def in_plane(k, sign=1):
        return ((x + sign * (k // 4) + 4) % 4) * 4 + (y + sign * (k % 4) + 4) % 4

    plane = [None] + [(gy, in_plane(k)) for k in range(1, 16)]

    def column(zz):
        return (zz * 2 + core, gx)

    loads = [
        pltpu.make_async_copy(cot_hbm, cot_in, w_sem.at[3]),
        pltpu.make_async_copy(level_in, level_own, w_sem.at[4]),
        pltpu.make_async_copy(wl_hbm, wl, w_sem.at[0]),
        pltpu.make_async_copy(wd_hbm, wd, w_sem.at[1]),
        pltpu.make_async_copy(wn_hbm, wn, w_sem.at[2]),
    ]
    for load in loads[:2]:
        load.start()
    barrier = pltpu.get_barrier_semaphore()
    x_peer = [None] + [(gy, (x + k) % 4 * 4 + y) for k in range(1, 4)]
    y_peer = [None] + [(gy, x * 4 + (y + k) % 4) for k in range(1, 4)]
    peers = x_peer[1:] + y_peer[1:] + [side(dy, dx) for dy, dx in SIDES]
    for peer in peers:
        pl.semaphore_signal(barrier, inc=1, device_id=peer, device_id_type=MESH)

    def copy(src, dst, sems, k, dev):
        return pltpu.make_async_remote_copy(
            src_ref=src, dst_ref=dst, send_sem=sems.at[0, k], recv_sem=sems.at[1, k],
            device_id=dev, device_id_type=MESH,
        )

    sent = []

    def go(copies):
        for c in copies:
            c.start()
        sent.extend(copies)
        return copies

    pl.semaphore_wait(barrier, len(peers))
    def tell(n):
        for dy in (-1, 1):
            pl.semaphore_signal(known.at[n], inc=1, device_id=side(dy * 2 ** n, 0), device_id_type=MESH)

    src_rows = {-1: slice(0, RIM), 0: slice(0, 8), 1: slice(8 - RIM, 8)}
    src_cols = {-1: slice(0, 16), 0: slice(0, 64), 1: slice(48, 64)}
    dst_rows = {-1: slice(RIM + 8, RIM + 8 + RIM), 0: slice(RIM, RIM + 8), 1: slice(0, RIM)}
    dst_cols = {-1: slice(80, 96), 0: slice(16, 80), 1: slice(0, 16)}
    e1 = go([
        copy(level_in.at[src_rows[dy], src_cols[dx]], lp.at[dst_rows[dy], dst_cols[dx]], e1_sem, n, side(dy, dx))
        for n, (dy, dx) in sorted(enumerate(SIDES), key=lambda e: -abs(e[1][0]) - abs(e[1][1]))
    ])
    for k in range(1, 4):
        pl.semaphore_signal(known.at[4], inc=1, device_id=y_peer[k], device_id_type=MESH)
    tell(0)
    loads[0].wait()
    for load in loads[2:]:
        load.start()
    lane = lax.broadcasted_iota(jnp.int32, (16, 128), 1)
    for q in range(4):
        rows = [cot_in[r, :, 128 * q:128 * q + 128].astype(F32) for r in range(4)]
        for j in range(4):
            out = pltpu.roll(rows[3], (32 * (3 - j)) % 128, 1) if j != 3 else rows[3]
            for r in (2, 1, 0):
                part = pltpu.roll(rows[r], (32 * (r - j)) % 128, 1) if r != j else rows[r]
                out = jnp.where(lane < 32 * (r + 1), part, out)
            cot_send[4 * q + j, 0] = out.astype(BF16)
    for t in range(16):
        cot_send[t, 1] = jnp.where(lane % 32 < 16, cot_send[(t + 1) % 16, 0].astype(F32), cot_send[(t + 15) % 16, 0].astype(F32)).astype(BF16)
    cot_recv[gx] = cot_send[gx]

    top_ok = jnp.where(gy > 0, 1.0, 0.0).astype(F32)
    bottom_ok = jnp.where(gy < 31, 1.0, 0.0).astype(F32)
    left_ok = jnp.where(gx > 0, 1.0, 0.0).astype(F32)
    right_ok = jnp.where(gx < 15, 1.0, 0.0).astype(F32)

    pl.semaphore_wait(known.at[4], 3)
    cot_copies = go([
        copy(cot_send.at[in_plane(k)], cot_recv.at[gx], cot_sem, k, plane[k]) for k in FAR_FIRST
    ])
    loads[1].wait()
    lf[0:8] = jnp.zeros((8, 128), F32)
    lf[8 + 18 * WIDE:] = jnp.zeros((8, 128), F32)
    for r in range(8):
        start = 8 + (r + RIM) * WIDE + 16
        lf[start:start + 64] = level_own[r].astype(F32)

    pl.semaphore_wait(known.at[0], 2)
    tell(1)

    loads[2].wait()
    for ky in range(3):
        for kx in range(3):
            w = wl[2 - ky, (2 - kx) * 128:(3 - kx) * 128, :].astype(F32)
            wlt[ky, kx * 128:(kx + 1) * 128, :] = w.T.astype(BF16)

    for c in e1:
        c.wait_recv()
    pl.semaphore_wait(known.at[1], 2)
    tell(2)
    for r in range(18):
        row_ok = top_ok if r < RIM else bottom_ok if r >= RIM + 8 else None
        base = 8 + r * WIDE
        left = lp[r, 0:16].astype(F32) * left_ok
        right = lp[r, 80:96].astype(F32) * right_ok
        if row_ok is not None:
            left, right = left * row_ok, right * row_ok
            lf[base + 16:base + 80] = lp[r, 16:80].astype(F32) * row_ok
        lf[base:base + 16] = left
        lf[base + 80:base + 96] = right
    for r in range(18):
        for kx in range(3):
            start = 7 + kx + r * WIDE
            im_l[r * WIDE:(r + 1) * WIDE, kx * 128:(kx + 1) * 128] = lf[start:start + WIDE].astype(BF16)

    for q in range(4):
        pre = dot(im_l[4 * q * WIDE:(4 * q + 4) * WIDE], wl[0])
        for ky in (1, 2):
            pre = pre + dot(im_l[(4 * q + ky) * WIDE:(4 * q + ky + 4) * WIDE], wl[ky])
        own = lf[8 + (4 * q + 1) * WIDE:8 + (4 * q + 5) * WIDE]
        act[4 * q * WIDE:(4 * q + 4) * WIDE] = own + pre * jax.nn.sigmoid(pre)
        if q in (1, 2):
            pre_l[(q - 1) * 4 * WIDE:q * 4 * WIDE] = pre

    for c in cot_copies:
        c.wait_recv()
    cot_tile = cot_recv[:, 0].reshape(256, 128).astype(F32).T
    cot_beside = cot_recv[:, 1].reshape(256, 128).astype(F32).T
    for r in range(4):
        base = (r + 1) * NARROW
        cf[base:base + 8] = cot_beside[32 * r + 24:32 * r + 32] * left_ok
        cf[base + 8:base + 40] = cot_tile[32 * r:32 * r + 32]
        cf[base + 40:base + 48] = cot_beside[32 * r:32 * r + 8] * right_ok
    ct[0] = cf[NARROW:2 * NARROW].astype(BF16)
    ct[1] = cf[4 * NARROW:5 * NARROW].astype(BF16)
    ch = go([copy(ct.at[n], hr.at[n], ch_sem, n, side(2 * n - 1, 0)) for n in range(2)])

    for rr in range(16):
        for q in range(2):
            lanes = slice(128 * (2 * (rr % 2) + q), 128 * (2 * (rr % 2) + q) + 128)
            dn[(rr // 2) * NARROW:(rr // 2 + 1) * NARROW, lanes] = act[pl.ds(rr * WIDE + q, NARROW, stride=2), :].astype(BF16)
    loads[3].wait()
    col = lax.broadcasted_iota(jnp.int32, (NARROW, 256), 0)
    col_ok = jnp.where(col < 8, left_ok, jnp.where(col >= 40, right_ok, 1.0))
    col_own = jnp.where((col >= 8) & (col < 40), 1.0, 0.0)
    nf[0:8] = jnp.zeros((8, 256), F32)
    nf[8 + 8 * NARROW:] = jnp.zeros((8, 256), F32)
    neck_in = dot(dn[...], wd[...]).astype(BF16).astype(F32)
    for r in range(8):
        row = neck_in[r * NARROW:(r + 1) * NARROW] * col_ok
        if r < 2:
            row = row * top_ok
        if r >= 6:
            row = row * bottom_ok
        nf[8 + r * NARROW:8 + (r + 1) * NARROW] = row
    for kx in range(3):
        im_n[:, kx * 256:(kx + 1) * 256] = nf[7 + kx:7 + kx + 8 * NARROW].astype(BF16)
    loads[4].wait()
    neck_pre = dot(im_n[0:6 * NARROW], wn[0])
    for ky in (1, 2):
        neck_pre = neck_pre + dot(im_n[ky * NARROW:(ky + 6) * NARROW], wn[ky])

    own = slice(NARROW, 5 * NARROW)
    gf[0:8] = jnp.zeros((8, 256), F32)
    gf[8 + 6 * NARROW:] = jnp.zeros((8, 256), F32)
    gate = (cf[own] * slope_of(neck_pre[own])).astype(BF16).astype(F32)
    gf[8 + NARROW:8 + 5 * NARROW] = gate
    for r in range(4):
        gate_own[r * NARROW:(r + 1) * NARROW] = (gate[r * NARROW:(r + 1) * NARROW] * col_own).astype(BF16)

    def half_lanes(half):
        return pl.ds(pl.multiple_of(half * 128, 128), 128)

    theirs = gate_own[:, half_lanes(other)]
    a_pair = []
    for ky in range(3):
        part = dot_tn(im_n[(1 + ky) * NARROW:(5 + ky) * NARROW], theirs)
        third = slice(48 * ky, 48 * ky + 48)
        a_pair_s[third] = part.astype(BF16).reshape(48, 16, 128)
        a_pair.extend(go([copy(a_pair_s.at[third], a_pair_r.at[third], pair_sem, (0, 2, 12)[ky], pair_dev)]))
    mine = gate_own[:, half_lanes(core)]
    for ky in range(3):
        neck_own[48 * ky:48 * ky + 48] = dot_tn(im_n[(1 + ky) * NARROW:(5 + ky) * NARROW], mine).reshape(48, 16, 128)

    def plane_stage(work, buf, sems, first):
        return go([copy(work(in_plane(k)), buf.at[k], sems, first + k, plane[k]) for k in FAR_FIRST])

    def b_piece_of(o):
        return b_work.at[o]

    for n in range(16):
        if n in (0, 5, 10):
            a_pair[n // 5].wait_recv()
        part = slice(n * NECK_TILES, (n + 1) * NECK_TILES)
        a_work[n // 4, n % 4] = (neck_own[part] + a_pair_r[part].astype(F32)).astype(BF16)
    near = []
    for k in (2, 1, 3):
        near.append(copy(a_work.at[(x + k) % 4, :, 0:ROUTE], near_a.at[k], near_sem, k, x_peer[k]))
        near.append(copy(a_work.at[:, (y + k) % 4, ROUTE:], near_b.at[k], near_sem, 4 + k, y_peer[k]))
    go(near)
    pl.semaphore_wait(known.at[2], 2)
    tell(3)

    for c in ch:
        c.wait_recv()
    for n, ok, rows in ((1, top_ok, slice(0, NARROW)), (0, bottom_ok, slice(5 * NARROW, 6 * NARROW))):
        v = hr[n].astype(F32) * ok * slope_of(neck_pre[rows])
        gf[8 + rows.start:8 + rows.stop] = v.astype(BF16).astype(F32)

    for kx in range(3):
        im_g[:, kx * 256:(kx + 1) * 256] = gf[7 + kx:7 + kx + 6 * NARROW].astype(BF16)
    back = None
    for ky in range(3):
        for kx in range(3):
            term = dot_nt(
                im_g[ky * NARROW:(ky + 4) * NARROW, kx * 256:(kx + 1) * 256],
                wn[2 - ky, (2 - kx) * 256:(3 - kx) * 256, :],
            )
            back = term if back is None else back + term
    for r in range(4):
        v = cf[(r + 1) * NARROW:(r + 2) * NARROW] + back[r * NARROW:(r + 1) * NARROW]
        ng[r * NARROW:(r + 1) * NARROW] = (v * col_own).astype(BF16)
    spread = dot_nt(ng[...], wd[...])
    for r in range(4):
        for p in range(2):
            for q in range(2):
                lanes = slice(128 * (2 * p + q), 128 * (2 * p + q) + 128)
                lbf[pl.ds((2 * r + p) * WIDE + q, NARROW, stride=2), :] = spread[r * NARROW:(r + 1) * NARROW, lanes]
    for r in range(8):
        rows_r = slice(r * WIDE + 16, r * WIDE + 80)
        gp[r + 1, 16:80] = (lbf[rows_r] * slope_of(pre_l[rows_r])).astype(BF16)
    own_gate = gp[1:9, 16:80].reshape(512, 128)
    for ky in range(3):
        window = jnp.concatenate(
            [im_l[(4 + ky + r) * WIDE + 16:(4 + ky + r) * WIDE + 80] for r in range(8)], axis=0
        )
        level_acc[ky * 384:(ky + 1) * 384] = dot_tn(window, own_gate)
    down_acc[...] = dot_tn(dn[2 * NARROW:6 * NARROW], ng[...])

    def rest_terms(half):
        down = down_acc[:, half_lanes(half)].reshape(16, 2, 16, 128)
        level = level_acc[pl.ds(pl.multiple_of(half * 576, 576), 576), :].reshape(LEVEL_OWNERS, 3, 16, 128)
        return down, level

    down, level = rest_terms(other)
    nothing = jnp.zeros((16 - LEVEL_OWNERS, 3, 16, 128), BF16)
    b_pair_s[:, 0:2] = down.astype(BF16)
    b_pair_s[0:LEVEL_OWNERS, 2:5] = level.astype(BF16)
    b_pair_s[LEVEL_OWNERS:, 2:5] = nothing
    b_pair = go([copy(b_pair_s, b_pair_r, pair_sem, 1, pair_dev)])

    b_pair[0].wait_recv()
    down, level = rest_terms(core)
    b_work[:, 0:2] = (down + b_pair_r[:, 0:2].astype(F32)).astype(BF16)
    b_work[0:LEVEL_OWNERS, 2:5] = (level + b_pair_r[0:LEVEL_OWNERS, 2:5].astype(F32)).astype(BF16)
    b_work[LEVEL_OWNERS:, 2:5] = nothing
    b_plane = plane_stage(b_piece_of, b_xy, xy_sem, 16)

    e4_src = {-1: slice(1, 2), 0: slice(1, 9), 1: slice(8, 9)}
    e4_dst = {-1: slice(9, 10), 0: slice(1, 9), 1: slice(0, 1)}
    e4_scol = {-1: slice(16, 32), 0: slice(16, 80), 1: slice(64, 80)}
    e4 = go([
        copy(gp.at[e4_src[dy], e4_scol[dx]], gp.at[e4_dst[dy], dst_cols[dx]], e4_sem, n, side(dy, dx))
        for n, (dy, dx) in enumerate(SIDES)
    ])

    for c in near:
        c.wait_recv()
    for p in range(4):
        via_x, via_y = a_work[x, p, 0:ROUTE].astype(F32), a_work[p, y, ROUTE:].astype(F32)
        for k in range(1, 4):
            via_x = via_x + near_a[k, p].astype(F32)
            via_y = via_y + near_b[k, p].astype(F32)
        near_a[0, p] = via_x.astype(BF16)
        near_b[0, p] = via_y.astype(BF16)
    far = []
    for k in (2, 1, 3):
        far.append(copy(near_a.at[0, (y + k) % 4], far_a.at[k], far_sem, k, y_peer[k]))
        far.append(copy(near_b.at[0, (x + k) % 4], far_b.at[k], far_sem, 4 + k, x_peer[k]))
    go(far)

    rows = []
    for r in range(4):
        v = neck_pre[(r + 1) * NARROW + 8:(r + 1) * NARROW + 40]
        rows.append(nf[8 + (r + 2) * NARROW + 8:8 + (r + 2) * NARROW + 40] + v * jax.nn.sigmoid(v))
    no_send[...] = jnp.concatenate(rows, axis=0).T.astype(BF16).reshape(16, 16, 128)
    no_recv[gx] = no_send[gx]
    no_copies = go([copy(no_send.at[in_plane(k)], no_recv.at[gx], no_sem, k, plane[k]) for k in FAR_FIRST])

    pl.semaphore_wait(known.at[3], 2)

    def z_send(piece, buf, tiles, first, sems, offset):
        copies = []
        for k in Z_FAR_FIRST:
            t = (z + k) % 16 - first
            c = copy_z(piece.at[t], buf.at[z], sems, offset + k, offset + z, column((z + k) % 16))
            copies.append(((t >= 0) & (t < tiles), c))
        return copies

    def copy_z(src, dst, sems, ks, kr, dev):
        return pltpu.make_async_remote_copy(
            src_ref=src, dst_ref=dst, send_sem=sems.at[0, ks], recv_sem=sems.at[1, kr],
            device_id=dev, device_id_type=MESH,
        )

    def start_all(copies):
        for cond, c in copies:
            pl.when(cond)(c.start)

    def plane_sum(piece_of, buf, own_ref, copies, out):
        for c in copies:
            c.wait_recv()
        total = own_ref[...].astype(F32)
        for k in range(1, 16):
            total = total + buf[k].astype(F32)
        out[...] = total.astype(BF16)

    def owns(first, tiles):
        return (z >= first) & (z < first + tiles)

    def z_sum(piece, buf, fin, tiles, first, sems, offset, scale):
        @pl.when(owns(first, tiles))
        def _():
            mine = z - first
            for s in range(16):
                @pl.when(z != s)
                def _(s=s):
                    copy_z(piece.at[0], buf.at[s], sems, offset, offset + s, column(s)).wait_recv()
            buf[z] = piece[mine]
            total = buf[0].astype(F32)
            for s in range(1, 16):
                total = total + buf[s].astype(F32)
            fin[mine] = (total * scale).astype(BF16)
            for k in Z_FAR_FIRST:
                copy_z(fin.at[mine], fin.at[mine], zb_sem, offset + k, offset + mine, column((z + k) % 16)).start()

    def z_back(fin, tiles, first, offset):
        for t in range(tiles):
            @pl.when(z != first + t)
            def _(t=t):
                copy_z(fin.at[t], fin.at[t], zb_sem, offset, offset + t, column(first + t)).wait_recv()

    def z_back_sent(fin, tiles, first, offset):
        @pl.when(owns(first, tiles))
        def _():
            for k in Z_FAR_FIRST:
                copy_z(fin.at[0], fin.at[0], zb_sem, offset + k, offset, column((z + k) % 16)).wait_send()

    for c in far:
        c.wait_recv()
    via_x, via_y = near_a[0, y].astype(F32), near_b[0, x].astype(F32)
    for k in range(1, 4):
        via_x = via_x + far_a[k].astype(F32)
        via_y = via_y + far_b[k].astype(F32)
    a_piece[0:ROUTE] = via_x.astype(BF16)
    a_piece[ROUTE:] = via_y.astype(BF16)
    a_zs = z_send(a_piece, a_z, NECK_TILES, 0, z_sem, 0)
    start_all(a_zs)
    plane_sum(b_piece_of, b_xy, b_piece_of(gx), b_plane, b_piece)
    b_zs = z_send(b_piece, b_z, REST_TILES, NECK_TILES, z_sem, 16)
    start_all(b_zs)
    for c in e4:
        c.wait_recv()
    g2f[0:8] = jnp.zeros((8, 128), F32)
    g2f[8 + 10 * WIDE:] = jnp.zeros((8, 128), F32)
    for r in range(10):
        row_ok = top_ok if r == 0 else bottom_ok if r == 9 else None
        base = 8 + r * WIDE
        left, mid, right = gp[r, 0:16].astype(F32) * left_ok, gp[r, 16:80].astype(F32), gp[r, 80:96].astype(F32) * right_ok
        if row_ok is not None:
            left, mid, right = left * row_ok, mid * row_ok, right * row_ok
        g2f[base:base + 16] = left
        g2f[base + 16:base + 80] = mid
        g2f[base + 80:base + 96] = right
    for r in range(10):
        for kx in range(3):
            start = 7 + kx + r * WIDE
            im_b[r * WIDE:(r + 1) * WIDE, kx * 128:(kx + 1) * 128] = g2f[start:start + WIDE].astype(BF16)
    for q in range(2):
        total = lbf[4 * q * WIDE:(4 * q + 4) * WIDE]
        for ky in range(3):
            total = total + dot(im_b[(4 * q + ky) * WIDE:(4 * q + ky + 4) * WIDE], wlt[ky])
        grad_input[4 * q:4 * q + 4] = total.reshape(4, WIDE, 128)[:, 16:80].astype(BF16)

    for c in no_copies:
        c.wait_recv()
    for q in range(4):
        pieces = [no_recv[4 * q + j].astype(F32) for j in range(4)]
        for r in range(4):
            out = pltpu.roll(pieces[3], (32 * (3 - r)) % 128, 1) if r != 3 else pieces[3]
            for j in (2, 1, 0):
                part = pltpu.roll(pieces[j], (32 * (j - r)) % 128, 1) if r != j else pieces[j]
                out = jnp.where(lane < 32 * (j + 1), part, out)
            neck_out[r, :, 128 * q:128 * q + 128] = out.astype(BF16)

    z_sum(a_piece, a_z, a_fin, NECK_TILES, 0, z_sem, 0, scales[0])
    z_sum(b_piece, b_z, b_fin, REST_TILES, NECK_TILES, z_sem, 16, jnp.where(z < NECK_TILES + 2, scales[0], scales[1]))

    z_back(a_fin, NECK_TILES, 0, 0)
    def b_slot(o):
        return b_all.at[core, o]

    a_all[core, x, y] = a_fin[...]
    leg1 = []
    for k in (2, 1, 3):
        mine_x, mine_y = a_all.at[core, x, y, 0:ROUTE], a_all.at[core, x, y, ROUTE:]
        leg1.append(copy(mine_x, mine_x, back1_sem, k, y_peer[k]))
        leg1.append(copy(mine_y, mine_y, back1_sem, 4 + k, x_peer[k]))
    go(leg1)
    z_back(b_fin, REST_TILES, NECK_TILES, 16)
    b_all[core, gx] = b_fin[...]
    b_mine = b_slot(gx)
    go([copy(b_mine, b_mine, xyb_sem, 16 + k, plane[k]) for k in FAR_FIRST])
    for c in leg1:
        c.wait_recv()

    def block_x(c, xx):
        return a_all.at[c, xx, :, 0:ROUTE]

    def block_y(c, yy):
        return a_all.at[c, :, yy, ROUTE:]

    leg2 = []
    for k in (2, 1, 3):
        leg2.append(copy(block_x(core, x), block_x(core, x), back2_sem, k, x_peer[k]))
        leg2.append(copy(block_y(core, y), block_y(core, y), back2_sem, 4 + k, y_peer[k]))
    go(leg2)

    def swap(k):
        bx, by = block_x(core, (x - k + 4) % 4), block_y(core, (y - k + 4) % 4)
        go([copy(bx, bx, pair_sem, 4 + k, pair_dev), copy(by, by, pair_sem, 8 + k, pair_dev)])

    swap(0)
    for k in FAR_FIRST:
        slot = b_slot(in_plane(k, -1))
        copy(slot, slot, xyb_sem, 16 + k, plane[k]).wait_recv()
    go([copy(b_all.at[core], b_all.at[core], pair_sem, 3, pair_dev)])
    for k in (1, 3, 2):
        bx, by = block_x(core, (x - k + 4) % 4), block_y(core, (y - k + 4) % 4)
        copy(bx, bx, back2_sem, k, x_peer[k]).wait_recv()
        copy(by, by, back2_sem, 4 + k, y_peer[k]).wait_recv()
        swap(k)
    copy(b_all.at[other], b_all.at[other], pair_sem, 3, pair_dev).wait_recv()
    for k in range(4):
        bx, by = block_x(other, (x - k + 4) % 4), block_y(other, (y - k + 4) % 4)
        copy(bx, bx, pair_sem, 4 + k, pair_dev).wait_recv()
        copy(by, by, pair_sem, 8 + k, pair_dev).wait_recv()

    for c in sent:
        c.wait_send()
    for cond, c in a_zs + b_zs:
        pl.when(cond)(c.wait_send)
    z_back_sent(a_fin, NECK_TILES, 0, 0)
    z_back_sent(b_fin, REST_TILES, NECK_TILES, 16)


def results_kernel(strip, level, a_all, b_all, neck_out, grad_input, grad_level, grad_down, grad_neck, sems):
    copies = [(strip, neck_out), (level, grad_input)]
    for half in range(2):
        lanes = slice(128 * half, 128 * half + 128)
        copies.append((a_all.at[half], grad_neck.at[:, :, :, :, lanes]))
        copies.append((b_all.at[half, :, 0:2], grad_down.at[:, :, :, lanes]))
        copies.append((b_all.at[half, 0:LEVEL_OWNERS, 2:5], grad_level.at[half]))
    copies = [pltpu.make_async_copy(src, dst, sems.at[n]) for n, (src, dst) in enumerate(copies)]
    for c in copies:
        c.start()
    for c in copies:
        c.wait()


def local(level_in, w_level, w_down, w_neck, cotangent):
    device_count = lax.axis_size("gy") * lax.axis_size("gx")
    level_count = level_in.shape[0] * level_in.shape[1] * device_count
    level_scale = 1.0 / math.sqrt(level_count)
    neck_scale = 1.0 / math.sqrt(level_count // 4)
    vmem = pl.BlockSpec(memory_space=pltpu.VMEM)
    hbm = pl.BlockSpec(memory_space=pltpu.HBM)
    dma = pltpu.SemaphoreType.DMA

    def v(*shape, dtype=BF16):
        return pltpu.VMEM(shape, dtype)

    outs = pl.pallas_call(
        functools.partial(kernel, (neck_scale, level_scale)),
        out_shape=[
            jax.ShapeDtypeStruct((4, 16, 512), BF16),
            jax.ShapeDtypeStruct((8, 64, 128), BF16),
            jax.ShapeDtypeStruct((2, 4, 4, NECK_TILES, 16, 128), BF16),
            jax.ShapeDtypeStruct((2, 16, REST_TILES, 16, 128), BF16),
        ],
        in_specs=[hbm] * 5,
        out_specs=[vmem] * 4,
        scratch_shapes=[
            v(8, 64, 128), v(4, 16, 512),
            v(3, 384, 128), v(512, 256), v(3, 768, 256), v(3, 384, 128),
            v(18, WIDE, 128), v(16 + 18 * WIDE, 128, dtype=F32), v(18 * WIDE, 384),
            v(8 * WIDE, 128, dtype=F32), v(16 * WIDE, 128, dtype=F32), v(8 * NARROW, 512),
            v(16 + 8 * NARROW, 256, dtype=F32), v(8 * NARROW, 768),
            v(6 * NARROW, 256, dtype=F32), v(16 + 6 * NARROW, 256, dtype=F32), v(6 * NARROW, 768),
            v(4 * NARROW, 256), v(4 * NARROW, 256), v(8 * WIDE, 128, dtype=F32),
            v(10, WIDE, 128), v(16 + 10 * WIDE, 128, dtype=F32), v(10 * WIDE, 384),
            v(16, 2, 16, 128), v(16, 2, 16, 128), v(2, NARROW, 256), v(2, NARROW, 256),
            v(16, 16, 128), v(16, 16, 128),
            v(144, 16, 128, dtype=F32), v(1152, 128, dtype=F32), v(512, 256, dtype=F32),
            v(16 * NECK_TILES, 16, 128), v(16 * NECK_TILES, 16, 128), v(4, 4, NECK_TILES, 16, 128),
            v(4, 4, ROUTE, 16, 128), v(4, 4, NECK_TILES - ROUTE, 16, 128),
            v(4, ROUTE, 16, 128), v(4, NECK_TILES - ROUTE, 16, 128),
            v(NECK_TILES, 16, 128), v(16, 16, 128), v(NECK_TILES, 16, 128),
            v(16, REST_TILES, 16, 128), v(16, REST_TILES, 16, 128), v(16, REST_TILES, 16, 128), v(16, REST_TILES, 16, 128),
            v(REST_TILES, 16, 128), v(16, 16, 128), v(REST_TILES, 16, 128),
            dma((5,)), dma((2, 8)), dma((2, 16)), dma((2, 8)), dma((2, 16)), dma((2, 8)),
            dma((2, 13)), dma((2, 32)), dma((2, 32)), dma((2, 32)), dma((2, 32)), dma((2, 8)), dma((2, 8)), dma((2, 8)), dma((2, 8)),
            pltpu.SemaphoreType.REGULAR((5,)),
        ],
        compiler_params=pltpu.CompilerParams(
            collective_id=0, has_side_effects=True, vmem_limit_bytes=24 * 1024 * 1024
        ),
    )(
        *(pltpu.with_memory_space_constraint(t, pltpu.HBM) for t in (
            level_in,
            w_level.reshape(3, 384, 128),
            w_down.reshape(512, 256),
            w_neck.reshape(3, 768, 256),
            jnp.transpose(cotangent, (0, 2, 1)),
        ))
    )
    outs = pl.pallas_call(
        results_kernel,
        out_shape=[
            jax.ShapeDtypeStruct((4, 16, 512), BF16),
            jax.ShapeDtypeStruct((8, 64, 128), BF16),
            jax.ShapeDtypeStruct((2, LEVEL_OWNERS, 3, 16, 128), BF16),
            jax.ShapeDtypeStruct((16, 2, 16, 256), BF16),
            jax.ShapeDtypeStruct((4, 4, NECK_TILES, 16, 256), BF16),
        ],
        in_specs=[vmem] * 4,
        out_specs=[hbm] * 5,
        scratch_shapes=[dma((8,))],
        compiler_params=pltpu.CompilerParams(vmem_limit_bytes=1024 * 1024),
    )(*outs)
    return (
        jnp.transpose(outs[0], (0, 2, 1)),
        outs[1],
        outs[2].reshape(w_level.shape),
        outs[3].reshape(w_down.shape),
        outs[4].reshape(w_neck.shape),
    )


def solution(mesh):
    return jax.shard_map(
        local,
        mesh=mesh,
        in_specs=(P("gy", "gx", None), P(), P(), P(), P("gy", None, "gx")),
        out_specs=(P("gy", None, "gx"), P("gy", "gx", None), P(), P(), P()),
        check_vma=False,
    )
```

```python
import functools
import math

import jax
import jax.numpy as jnp
from jax import lax
from jax.experimental import pallas as pl
from jax.experimental.pallas import tpu as pltpu
from jax.sharding import PartitionSpec as P

MESH = pl.DeviceIdType.MESH
BF16, F32 = jnp.bfloat16, jnp.float32

RIM = 5
WIDE = 96
NARROW = 48
SIDES = [(dy, dx) for dy in (-1, 0, 1) for dx in (-1, 0, 1) if (dy, dx) != (0, 0)]
FAR_FIRST = sorted(range(1, 16), key=lambda k: -(min(k // 4, 4 - k // 4) + min(k % 4, 4 - k % 4)))
Z_FAR_FIRST = sorted(range(1, 16), key=lambda k: -min(k, 16 - k))
NECK_TILES = 9
ROUTE = 5
REST_TILES = 5
LEVEL_OWNERS = 12


def slope_of(v):
    s = jax.nn.sigmoid(v)
    return s + v * s * (1.0 - s)


def dot(a, b):
    return jnp.dot(a, b, preferred_element_type=F32)


def dot_nt(a, b):
    return lax.dot_general(a, b, (((1,), (1,)), ((), ())), preferred_element_type=F32)


def dot_tn(a, b):
    return lax.dot_general(a, b, (((0,), (0,)), ((), ())), preferred_element_type=F32)


def kernel(
    scales,
    level_in, wl_hbm, wd_hbm, wn_hbm, cot_hbm,
    neck_out, grad_input, a_all, b_all,
    level_own, cot_in, wl, wd, wn, wlt,
    lp, lf, im_l, pre_l, act, dn, nf, im_n, cf, gf, im_g, gate_own, ng, lbf, gp, g2f, im_b,
    cot_send, cot_recv, ct, hr, no_send, no_recv,
    neck_own, level_acc, down_acc,
    a_pair_s, a_pair_r, a_work, near_a, near_b, far_a, far_b, a_piece, a_z, a_fin,
    b_pair_s, b_pair_r, b_work, b_xy, b_piece, b_z, b_fin,
    w_sem, e1_sem, cot_sem, ch_sem, no_sem, e4_sem,
    pair_sem, xy_sem, z_sem, zb_sem, xyb_sem, near_sem, far_sem, back1_sem, back2_sem, known,
):
    gy, gx = lax.axis_index("gy"), lax.axis_index("gx")
    z, core = gy // 2, gy % 2
    other = 1 - core

    def side(dy, dx):
        return ((gy + dy + 32) % 32, (gx + dx + 16) % 16)

    pair_dev = (z * 2 + other, gx)
    x, y = gx // 4, gx % 4

    def in_plane(k, sign=1):
        return ((x + sign * (k // 4) + 4) % 4) * 4 + (y + sign * (k % 4) + 4) % 4

    plane = [None] + [(gy, in_plane(k)) for k in range(1, 16)]

    def column(zz):
        return (zz * 2 + core, gx)

    loads = [
        pltpu.make_async_copy(cot_hbm, cot_in, w_sem.at[3]),
        pltpu.make_async_copy(level_in, level_own, w_sem.at[4]),
        pltpu.make_async_copy(wl_hbm, wl, w_sem.at[0]),
        pltpu.make_async_copy(wd_hbm, wd, w_sem.at[1]),
        pltpu.make_async_copy(wn_hbm, wn, w_sem.at[2]),
    ]
    for load in loads[:2]:
        load.start()
    barrier = pltpu.get_barrier_semaphore()
    x_peer = [None] + [(gy, (x + k) % 4 * 4 + y) for k in range(1, 4)]
    y_peer = [None] + [(gy, x * 4 + (y + k) % 4) for k in range(1, 4)]
    corners_first = sorted(SIDES, key=lambda e: -abs(e[0]) - abs(e[1]))
    peers = [side(dy, dx) for dy, dx in corners_first] + x_peer[1:] + y_peer[1:]
    for peer in peers:
        pl.semaphore_signal(barrier, inc=1, device_id=peer, device_id_type=MESH)

    def copy(src, dst, sems, k, dev):
        return pltpu.make_async_remote_copy(
            src_ref=src, dst_ref=dst, send_sem=sems.at[0, k], recv_sem=sems.at[1, k],
            device_id=dev, device_id_type=MESH,
        )

    sent = []

    def go(copies):
        for c in copies:
            c.start()
        sent.extend(copies)
        return copies

    pl.semaphore_wait(barrier, len(peers))
    def tell(n):
        for dy in (-1, 1):
            pl.semaphore_signal(known.at[n], inc=1, device_id=side(dy * 2 ** n, 0), device_id_type=MESH)

    src_rows = {-1: slice(0, RIM), 0: slice(0, 8), 1: slice(8 - RIM, 8)}
    src_cols = {-1: slice(0, 16), 0: slice(0, 64), 1: slice(48, 64)}
    dst_rows = {-1: slice(RIM + 8, RIM + 8 + RIM), 0: slice(RIM, RIM + 8), 1: slice(0, RIM)}
    dst_cols = {-1: slice(80, 96), 0: slice(16, 80), 1: slice(0, 16)}
    e1 = go([
        copy(level_in.at[src_rows[dy], src_cols[dx]], lp.at[dst_rows[dy], dst_cols[dx]], e1_sem, n, side(dy, dx))
        for n, (dy, dx) in sorted(enumerate(SIDES), key=lambda e: -abs(e[1][0]) - abs(e[1][1]))
    ])
    for k in range(1, 4):
        pl.semaphore_signal(known.at[4], inc=1, device_id=y_peer[k], device_id_type=MESH)
    tell(0)
    loads[0].wait()
    for load in loads[2:]:
        load.start()
    lane = lax.broadcasted_iota(jnp.int32, (16, 128), 1)
    for q in range(4):
        rows = [cot_in[r, :, 128 * q:128 * q + 128].astype(F32) for r in range(4)]
        for j in range(4):
            out = pltpu.roll(rows[3], (32 * (3 - j)) % 128, 1) if j != 3 else rows[3]
            for r in (2, 1, 0):
                part = pltpu.roll(rows[r], (32 * (r - j)) % 128, 1) if r != j else rows[r]
                out = jnp.where(lane < 32 * (r + 1), part, out)
            cot_send[4 * q + j, 0] = out.astype(BF16)
    for t in range(16):
        cot_send[t, 1] = jnp.where(lane % 32 < 16, cot_send[(t + 1) % 16, 0].astype(F32), cot_send[(t + 15) % 16, 0].astype(F32)).astype(BF16)
    cot_recv[gx] = cot_send[gx]

    top_ok = jnp.where(gy > 0, 1.0, 0.0).astype(F32)
    bottom_ok = jnp.where(gy < 31, 1.0, 0.0).astype(F32)
    left_ok = jnp.where(gx > 0, 1.0, 0.0).astype(F32)
    right_ok = jnp.where(gx < 15, 1.0, 0.0).astype(F32)

    pl.semaphore_wait(known.at[4], 3)
    cot_copies = go([
        copy(cot_send.at[in_plane(k)], cot_recv.at[gx], cot_sem, k, plane[k]) for k in FAR_FIRST
    ])
    loads[1].wait()
    lf[0:8] = jnp.zeros((8, 128), F32)
    lf[8 + 18 * WIDE:] = jnp.zeros((8, 128), F32)
    for r in range(8):
        start = 8 + (r + RIM) * WIDE + 16
        lf[start:start + 64] = level_own[r].astype(F32)

    pl.semaphore_wait(known.at[0], 2)
    tell(1)

    loads[2].wait()
    for ky in range(3):
        for kx in range(3):
            w = wl[2 - ky, (2 - kx) * 128:(3 - kx) * 128, :].astype(F32)
            wlt[ky, kx * 128:(kx + 1) * 128, :] = w.T.astype(BF16)

    for c in e1:
        c.wait_recv()
    pl.semaphore_wait(known.at[1], 2)
    tell(2)
    for r in range(18):
        row_ok = top_ok if r < RIM else bottom_ok if r >= RIM + 8 else None
        base = 8 + r * WIDE
        left = lp[r, 0:16].astype(F32) * left_ok
        right = lp[r, 80:96].astype(F32) * right_ok
        if row_ok is not None:
            left, right = left * row_ok, right * row_ok
            lf[base + 16:base + 80] = lp[r, 16:80].astype(F32) * row_ok
        lf[base:base + 16] = left
        lf[base + 80:base + 96] = right
    for r in range(18):
        for kx in range(3):
            start = 7 + kx + r * WIDE
            im_l[r * WIDE:(r + 1) * WIDE, kx * 128:(kx + 1) * 128] = lf[start:start + WIDE].astype(BF16)

    for q in range(4):
        pre = dot(im_l[4 * q * WIDE:(4 * q + 4) * WIDE], wl[0])
        for ky in (1, 2):
            pre = pre + dot(im_l[(4 * q + ky) * WIDE:(4 * q + ky + 4) * WIDE], wl[ky])
        own = lf[8 + (4 * q + 1) * WIDE:8 + (4 * q + 5) * WIDE]
        act[4 * q * WIDE:(4 * q + 4) * WIDE] = own + pre * jax.nn.sigmoid(pre)
        if q in (1, 2):
            pre_l[(q - 1) * 4 * WIDE:q * 4 * WIDE] = pre

    for c in cot_copies:
        c.wait_recv()
    cot_tile = cot_recv[:, 0].reshape(256, 128).astype(F32).T
    cot_beside = cot_recv[:, 1].reshape(256, 128).astype(F32).T
    for r in range(4):
        base = (r + 1) * NARROW
        cf[base:base + 8] = cot_beside[32 * r + 24:32 * r + 32] * left_ok
        cf[base + 8:base + 40] = cot_tile[32 * r:32 * r + 32]
        cf[base + 40:base + 48] = cot_beside[32 * r:32 * r + 8] * right_ok
    ct[0] = cf[NARROW:2 * NARROW].astype(BF16)
    ct[1] = cf[4 * NARROW:5 * NARROW].astype(BF16)
    ch = go([copy(ct.at[n], hr.at[n], ch_sem, n, side(2 * n - 1, 0)) for n in range(2)])

    for rr in range(16):
        for q in range(2):
            lanes = slice(128 * (2 * (rr % 2) + q), 128 * (2 * (rr % 2) + q) + 128)
            dn[(rr // 2) * NARROW:(rr // 2 + 1) * NARROW, lanes] = act[pl.ds(rr * WIDE + q, NARROW, stride=2), :].astype(BF16)
    loads[3].wait()
    col = lax.broadcasted_iota(jnp.int32, (NARROW, 256), 0)
    col_ok = jnp.where(col < 8, left_ok, jnp.where(col >= 40, right_ok, 1.0))
    col_own = jnp.where((col >= 8) & (col < 40), 1.0, 0.0)
    nf[0:8] = jnp.zeros((8, 256), F32)
    nf[8 + 8 * NARROW:] = jnp.zeros((8, 256), F32)
    neck_in = dot(dn[...], wd[...]).astype(BF16).astype(F32)
    for r in range(8):
        row = neck_in[r * NARROW:(r + 1) * NARROW] * col_ok
        if r < 2:
            row = row * top_ok
        if r >= 6:
            row = row * bottom_ok
        nf[8 + r * NARROW:8 + (r + 1) * NARROW] = row
    for kx in range(3):
        im_n[:, kx * 256:(kx + 1) * 256] = nf[7 + kx:7 + kx + 8 * NARROW].astype(BF16)
    loads[4].wait()
    neck_pre = dot(im_n[0:6 * NARROW], wn[0])
    for ky in (1, 2):
        neck_pre = neck_pre + dot(im_n[ky * NARROW:(ky + 6) * NARROW], wn[ky])

    own = slice(NARROW, 5 * NARROW)
    gf[0:8] = jnp.zeros((8, 256), F32)
    gf[8 + 6 * NARROW:] = jnp.zeros((8, 256), F32)
    gate = (cf[own] * slope_of(neck_pre[own])).astype(BF16).astype(F32)
    gf[8 + NARROW:8 + 5 * NARROW] = gate
    for r in range(4):
        gate_own[r * NARROW:(r + 1) * NARROW] = (gate[r * NARROW:(r + 1) * NARROW] * col_own).astype(BF16)

    def half_lanes(half):
        return pl.ds(pl.multiple_of(half * 128, 128), 128)

    theirs = gate_own[:, half_lanes(other)]
    a_pair = []
    for ky in range(3):
        part = dot_tn(im_n[(1 + ky) * NARROW:(5 + ky) * NARROW], theirs)
        third = slice(48 * ky, 48 * ky + 48)
        a_pair_s[third] = part.astype(BF16).reshape(48, 16, 128)
        a_pair.extend(go([copy(a_pair_s.at[third], a_pair_r.at[third], pair_sem, (0, 2, 12)[ky], pair_dev)]))
    mine = gate_own[:, half_lanes(core)]
    for ky in range(3):
        neck_own[48 * ky:48 * ky + 48] = dot_tn(im_n[(1 + ky) * NARROW:(5 + ky) * NARROW], mine).reshape(48, 16, 128)

    for n in range(16):
        if n in (0, 5, 10):
            a_pair[n // 5].wait_recv()
        part = slice(n * NECK_TILES, (n + 1) * NECK_TILES)
        a_work[n // 4, n % 4] = (neck_own[part] + a_pair_r[part].astype(F32)).astype(BF16)
    near = []
    for k in (2, 1, 3):
        near.append(copy(a_work.at[(x + k) % 4, :, 0:ROUTE], near_a.at[k], near_sem, k, x_peer[k]))
        near.append(copy(a_work.at[:, (y + k) % 4, ROUTE:], near_b.at[k], near_sem, 4 + k, y_peer[k]))
    go(near)
    pl.semaphore_wait(known.at[2], 2)
    tell(3)

    for c in ch:
        c.wait_recv()
    for n, ok, rows in ((1, top_ok, slice(0, NARROW)), (0, bottom_ok, slice(5 * NARROW, 6 * NARROW))):
        v = hr[n].astype(F32) * ok * slope_of(neck_pre[rows])
        gf[8 + rows.start:8 + rows.stop] = v.astype(BF16).astype(F32)

    for kx in range(3):
        im_g[:, kx * 256:(kx + 1) * 256] = gf[7 + kx:7 + kx + 6 * NARROW].astype(BF16)
    back = None
    for ky in range(3):
        for kx in range(3):
            term = dot_nt(
                im_g[ky * NARROW:(ky + 4) * NARROW, kx * 256:(kx + 1) * 256],
                wn[2 - ky, (2 - kx) * 256:(3 - kx) * 256, :],
            )
            back = term if back is None else back + term
    for r in range(4):
        v = cf[(r + 1) * NARROW:(r + 2) * NARROW] + back[r * NARROW:(r + 1) * NARROW]
        ng[r * NARROW:(r + 1) * NARROW] = (v * col_own).astype(BF16)
    spread = dot_nt(ng[...], wd[...])
    for r in range(4):
        for p in range(2):
            for q in range(2):
                lanes = slice(128 * (2 * p + q), 128 * (2 * p + q) + 128)
                lbf[pl.ds((2 * r + p) * WIDE + q, NARROW, stride=2), :] = spread[r * NARROW:(r + 1) * NARROW, lanes]
    for r in range(8):
        rows_r = slice(r * WIDE + 16, r * WIDE + 80)
        gp[r + 1, 16:80] = (lbf[rows_r] * slope_of(pre_l[rows_r])).astype(BF16)
    own_gate = gp[1:9, 16:80].reshape(512, 128)
    for ky in range(3):
        window = jnp.concatenate(
            [im_l[(4 + ky + r) * WIDE + 16:(4 + ky + r) * WIDE + 80] for r in range(8)], axis=0
        )
        level_acc[ky * 384:(ky + 1) * 384] = dot_tn(window, own_gate)
    down_acc[...] = dot_tn(dn[2 * NARROW:6 * NARROW], ng[...])

    def rest_terms(half):
        down = down_acc[:, half_lanes(half)].reshape(16, 2, 16, 128)
        level = level_acc[pl.ds(pl.multiple_of(half * 576, 576), 576), :].reshape(LEVEL_OWNERS, 3, 16, 128)
        return down, level

    down, level = rest_terms(other)
    nothing = jnp.zeros((16 - LEVEL_OWNERS, 3, 16, 128), BF16)
    b_pair_s[:, 0:2] = down.astype(BF16)
    b_pair_s[0:LEVEL_OWNERS, 2:5] = level.astype(BF16)
    b_pair_s[LEVEL_OWNERS:, 2:5] = nothing
    b_pair = go([copy(b_pair_s, b_pair_r, pair_sem, 1, pair_dev)])

    b_pair[0].wait_recv()
    down, level = rest_terms(core)
    b_work[:, 0:2] = (down + b_pair_r[:, 0:2].astype(F32)).astype(BF16)
    b_work[0:LEVEL_OWNERS, 2:5] = (level + b_pair_r[0:LEVEL_OWNERS, 2:5].astype(F32)).astype(BF16)
    b_work[LEVEL_OWNERS:, 2:5] = nothing
    me_level = gx < LEVEL_OWNERS
    b_plane = []
    for k in FAR_FIRST:
        o = in_plane(k)
        full = copy(b_work.at[o], b_xy.at[k], xy_sem, 16 + k, plane[k])
        short = copy(b_work.at[o, 0:2], b_xy.at[k, 0:2], xy_sem, 16 + k, plane[k])
        b_plane.append((o < LEVEL_OWNERS, full, short))

    def either(cond, one, two):
        pl.when(cond)(one)
        pl.when(jnp.logical_not(cond))(two)

    for cond, full, short in b_plane:
        either(cond, full.start, short.start)

    e4_src = {-1: slice(1, 2), 0: slice(1, 9), 1: slice(8, 9)}
    e4_dst = {-1: slice(9, 10), 0: slice(1, 9), 1: slice(0, 1)}
    e4_scol = {-1: slice(16, 32), 0: slice(16, 80), 1: slice(64, 80)}
    e4 = go([
        copy(gp.at[e4_src[dy], e4_scol[dx]], gp.at[e4_dst[dy], dst_cols[dx]], e4_sem, n, side(dy, dx))
        for n, (dy, dx) in enumerate(SIDES)
    ])

    for c in near:
        c.wait_recv()
    for p in range(4):
        via_x, via_y = a_work[x, p, 0:ROUTE].astype(F32), a_work[p, y, ROUTE:].astype(F32)
        for k in range(1, 4):
            via_x = via_x + near_a[k, p].astype(F32)
            via_y = via_y + near_b[k, p].astype(F32)
        near_a[0, p] = via_x.astype(BF16)
        near_b[0, p] = via_y.astype(BF16)
    far = []
    for k in (2, 1, 3):
        far.append(copy(near_a.at[0, (y + k) % 4], far_a.at[k], far_sem, k, y_peer[k]))
        far.append(copy(near_b.at[0, (x + k) % 4], far_b.at[k], far_sem, 4 + k, x_peer[k]))
    go(far)

    rows = []
    for r in range(4):
        v = neck_pre[(r + 1) * NARROW + 8:(r + 1) * NARROW + 40]
        rows.append(nf[8 + (r + 2) * NARROW + 8:8 + (r + 2) * NARROW + 40] + v * jax.nn.sigmoid(v))
    no_send[...] = jnp.concatenate(rows, axis=0).T.astype(BF16).reshape(16, 16, 128)
    no_recv[gx] = no_send[gx]
    no_copies = go([copy(no_send.at[in_plane(k)], no_recv.at[gx], no_sem, k, plane[k]) for k in FAR_FIRST])

    pl.semaphore_wait(known.at[3], 2)

    def z_send(piece, buf, tiles, first, sems, offset):
        copies = []
        for k in Z_FAR_FIRST:
            t = (z + k) % 16 - first
            c = copy_z(piece.at[t], buf.at[z], sems, offset + k, offset + z, column((z + k) % 16))
            copies.append(((t >= 0) & (t < tiles), c))
        return copies

    def copy_z(src, dst, sems, ks, kr, dev):
        return pltpu.make_async_remote_copy(
            src_ref=src, dst_ref=dst, send_sem=sems.at[0, ks], recv_sem=sems.at[1, kr],
            device_id=dev, device_id_type=MESH,
        )

    def start_all(copies):
        for cond, c in copies:
            pl.when(cond)(c.start)

    def b_sum(tiles):
        total = b_work[gx, tiles].astype(F32)
        for k in range(1, 16):
            total = total + b_xy[k, tiles].astype(F32)
        b_piece[tiles] = total.astype(BF16)

    def owns(first, tiles):
        return (z >= first) & (z < first + tiles)

    def z_sum(piece, buf, fin, tiles, first, sems, offset, scale):
        @pl.when(owns(first, tiles))
        def _():
            mine = z - first
            for s in range(16):
                @pl.when(z != s)
                def _(s=s):
                    copy_z(piece.at[0], buf.at[s], sems, offset, offset + s, column(s)).wait_recv()
            buf[z] = piece[mine]
            total = buf[0].astype(F32)
            for s in range(1, 16):
                total = total + buf[s].astype(F32)
            fin[mine] = (total * scale).astype(BF16)
            for k in Z_FAR_FIRST:
                copy_z(fin.at[mine], fin.at[mine], zb_sem, offset + k, offset + mine, column((z + k) % 16)).start()

    def z_back(fin, tiles, first, offset):
        for t in range(tiles):
            @pl.when(z != first + t)
            def _(t=t):
                copy_z(fin.at[t], fin.at[t], zb_sem, offset, offset + t, column(first + t)).wait_recv()

    def z_back_sent(fin, tiles, first, offset):
        @pl.when(owns(first, tiles))
        def _():
            for k in Z_FAR_FIRST:
                copy_z(fin.at[0], fin.at[0], zb_sem, offset + k, offset, column((z + k) % 16)).wait_send()

    for c in far:
        c.wait_recv()
    via_x, via_y = near_a[0, y].astype(F32), near_b[0, x].astype(F32)
    for k in range(1, 4):
        via_x = via_x + far_a[k].astype(F32)
        via_y = via_y + far_b[k].astype(F32)
    a_piece[0:ROUTE] = via_x.astype(BF16)
    a_piece[ROUTE:] = via_y.astype(BF16)
    a_zs = z_send(a_piece, a_z, NECK_TILES, 0, z_sem, 0)
    start_all(a_zs)
    @pl.when(me_level)
    def _():
        for _, full, _ in b_plane:
            full.wait_recv()
        b_sum(slice(2, REST_TILES))

    @pl.when(jnp.logical_not(me_level))
    def _():
        for _, _, short in b_plane:
            short.wait_recv()
        b_piece[2:] = nothing[0]

    b_sum(slice(0, 2))
    b_zs = z_send(b_piece, b_z, REST_TILES, NECK_TILES, z_sem, 16)
    start_all(b_zs)
    for c in e4:
        c.wait_recv()
    g2f[0:8] = jnp.zeros((8, 128), F32)
    g2f[8 + 10 * WIDE:] = jnp.zeros((8, 128), F32)
    for r in range(10):
        row_ok = top_ok if r == 0 else bottom_ok if r == 9 else None
        base = 8 + r * WIDE
        left, mid, right = gp[r, 0:16].astype(F32) * left_ok, gp[r, 16:80].astype(F32), gp[r, 80:96].astype(F32) * right_ok
        if row_ok is not None:
            left, mid, right = left * row_ok, mid * row_ok, right * row_ok
        g2f[base:base + 16] = left
        g2f[base + 16:base + 80] = mid
        g2f[base + 80:base + 96] = right
    for r in range(10):
        for kx in range(3):
            start = 7 + kx + r * WIDE
            im_b[r * WIDE:(r + 1) * WIDE, kx * 128:(kx + 1) * 128] = g2f[start:start + WIDE].astype(BF16)
    for q in range(2):
        total = lbf[4 * q * WIDE:(4 * q + 4) * WIDE]
        for ky in range(3):
            total = total + dot(im_b[(4 * q + ky) * WIDE:(4 * q + ky + 4) * WIDE], wlt[ky])
        grad_input[4 * q:4 * q + 4] = total.reshape(4, WIDE, 128)[:, 16:80].astype(BF16)

    for c in no_copies:
        c.wait_recv()
    for q in range(4):
        pieces = [no_recv[4 * q + j].astype(F32) for j in range(4)]
        for r in range(4):
            out = pltpu.roll(pieces[3], (32 * (3 - r)) % 128, 1) if r != 3 else pieces[3]
            for j in (2, 1, 0):
                part = pltpu.roll(pieces[j], (32 * (j - r)) % 128, 1) if r != j else pieces[j]
                out = jnp.where(lane < 32 * (j + 1), part, out)
            neck_out[r, :, 128 * q:128 * q + 128] = out.astype(BF16)

    z_sum(a_piece, a_z, a_fin, NECK_TILES, 0, z_sem, 0, scales[0])
    z_sum(b_piece, b_z, b_fin, REST_TILES, NECK_TILES, z_sem, 16, jnp.where(z < NECK_TILES + 2, scales[0], scales[1]))

    z_back(a_fin, NECK_TILES, 0, 0)
    def b_slot(o):
        return b_all.at[core, o]

    a_all[core, x, y] = a_fin[...]
    leg1 = []
    for k in (2, 1, 3):
        mine_x, mine_y = a_all.at[core, x, y, 0:ROUTE], a_all.at[core, x, y, ROUTE:]
        leg1.append(copy(mine_x, mine_x, back1_sem, k, y_peer[k]))
        leg1.append(copy(mine_y, mine_y, back1_sem, 4 + k, x_peer[k]))
    go(leg1)
    z_back(b_fin, REST_TILES, NECK_TILES, 16)
    b_all[core, gx] = b_fin[...]
    b_back = []
    for k in FAR_FIRST:
        full, short = b_slot(gx), b_all.at[core, gx, 0:2]
        b_back.append((copy(full, full, xyb_sem, 16 + k, plane[k]), copy(short, short, xyb_sem, 16 + k, plane[k])))

    @pl.when(me_level)
    def _():
        for full, _ in b_back:
            full.start()

    @pl.when(jnp.logical_not(me_level))
    def _():
        for _, short in b_back:
            short.start()

    for c in leg1:
        c.wait_recv()

    def block_x(c, xx):
        return a_all.at[c, xx, :, 0:ROUTE]

    def block_y(c, yy):
        return a_all.at[c, :, yy, ROUTE:]

    leg2 = []
    for k in (2, 1, 3):
        leg2.append(copy(block_x(core, x), block_x(core, x), back2_sem, k, x_peer[k]))
        leg2.append(copy(block_y(core, y), block_y(core, y), back2_sem, 4 + k, y_peer[k]))
    go(leg2)

    def swap(k):
        bx, by = block_x(core, (x - k + 4) % 4), block_y(core, (y - k + 4) % 4)
        go([copy(bx, bx, pair_sem, 4 + k, pair_dev), copy(by, by, pair_sem, 8 + k, pair_dev)])

    swap(0)
    for k in FAR_FIRST:
        o = in_plane(k, -1)
        full, short = b_slot(o), b_all.at[core, o, 0:2]
        full, short = copy(full, full, xyb_sem, 16 + k, plane[k]), copy(short, short, xyb_sem, 16 + k, plane[k])
        either(o < LEVEL_OWNERS, full.wait_recv, short.wait_recv)

    def b_parts(c):
        return b_all.at[c, 0:LEVEL_OWNERS], b_all.at[c, LEVEL_OWNERS:, 0:2]

    go([copy(part, part, pair_sem, (3, 13)[n], pair_dev) for n, part in enumerate(b_parts(core))])
    for k in (1, 3, 2):
        bx, by = block_x(core, (x - k + 4) % 4), block_y(core, (y - k + 4) % 4)
        copy(bx, bx, back2_sem, k, x_peer[k]).wait_recv()
        copy(by, by, back2_sem, 4 + k, y_peer[k]).wait_recv()
        swap(k)
    for n, part in enumerate(b_parts(other)):
        copy(part, part, pair_sem, (3, 13)[n], pair_dev).wait_recv()
    for k in range(4):
        bx, by = block_x(other, (x - k + 4) % 4), block_y(other, (y - k + 4) % 4)
        copy(bx, bx, pair_sem, 4 + k, pair_dev).wait_recv()
        copy(by, by, pair_sem, 8 + k, pair_dev).wait_recv()

    for c in sent:
        c.wait_send()
    for (cond, full, short), (back, back_short) in zip(b_plane, b_back):
        either(cond, full.wait_send, short.wait_send)
        either(me_level, back.wait_send, back_short.wait_send)
    for cond, c in a_zs + b_zs:
        pl.when(cond)(c.wait_send)
    z_back_sent(a_fin, NECK_TILES, 0, 0)
    z_back_sent(b_fin, REST_TILES, NECK_TILES, 16)


def results_kernel(strip, level, a_all, b_all, neck_out, grad_input, grad_level, grad_down, grad_neck, sems):
    copies = [(strip, neck_out), (level, grad_input)]
    for half in range(2):
        lanes = slice(128 * half, 128 * half + 128)
        copies.append((a_all.at[half], grad_neck.at[:, :, :, :, lanes]))
        copies.append((b_all.at[half, :, 0:2], grad_down.at[:, :, :, lanes]))
        copies.append((b_all.at[half, 0:LEVEL_OWNERS, 2:5], grad_level.at[half]))
    copies = [pltpu.make_async_copy(src, dst, sems.at[n]) for n, (src, dst) in enumerate(copies)]
    for c in copies:
        c.start()
    for c in copies:
        c.wait()


def local(level_in, w_level, w_down, w_neck, cotangent):
    device_count = lax.axis_size("gy") * lax.axis_size("gx")
    level_count = level_in.shape[0] * level_in.shape[1] * device_count
    level_scale = 1.0 / math.sqrt(level_count)
    neck_scale = 1.0 / math.sqrt(level_count // 4)
    vmem = pl.BlockSpec(memory_space=pltpu.VMEM)
    hbm = pl.BlockSpec(memory_space=pltpu.HBM)
    dma = pltpu.SemaphoreType.DMA

    def v(*shape, dtype=BF16):
        return pltpu.VMEM(shape, dtype)

    outs = pl.pallas_call(
        functools.partial(kernel, (neck_scale, level_scale)),
        out_shape=[
            jax.ShapeDtypeStruct((4, 16, 512), BF16),
            jax.ShapeDtypeStruct((8, 64, 128), BF16),
            jax.ShapeDtypeStruct((2, 4, 4, NECK_TILES, 16, 128), BF16),
            jax.ShapeDtypeStruct((2, 16, REST_TILES, 16, 128), BF16),
        ],
        in_specs=[hbm] * 5,
        out_specs=[vmem] * 4,
        scratch_shapes=[
            v(8, 64, 128), v(4, 16, 512),
            v(3, 384, 128), v(512, 256), v(3, 768, 256), v(3, 384, 128),
            v(18, WIDE, 128), v(16 + 18 * WIDE, 128, dtype=F32), v(18 * WIDE, 384),
            v(8 * WIDE, 128, dtype=F32), v(16 * WIDE, 128, dtype=F32), v(8 * NARROW, 512),
            v(16 + 8 * NARROW, 256, dtype=F32), v(8 * NARROW, 768),
            v(6 * NARROW, 256, dtype=F32), v(16 + 6 * NARROW, 256, dtype=F32), v(6 * NARROW, 768),
            v(4 * NARROW, 256), v(4 * NARROW, 256), v(8 * WIDE, 128, dtype=F32),
            v(10, WIDE, 128), v(16 + 10 * WIDE, 128, dtype=F32), v(10 * WIDE, 384),
            v(16, 2, 16, 128), v(16, 2, 16, 128), v(2, NARROW, 256), v(2, NARROW, 256),
            v(16, 16, 128), v(16, 16, 128),
            v(144, 16, 128, dtype=F32), v(1152, 128, dtype=F32), v(512, 256, dtype=F32),
            v(16 * NECK_TILES, 16, 128), v(16 * NECK_TILES, 16, 128), v(4, 4, NECK_TILES, 16, 128),
            v(4, 4, ROUTE, 16, 128), v(4, 4, NECK_TILES - ROUTE, 16, 128),
            v(4, ROUTE, 16, 128), v(4, NECK_TILES - ROUTE, 16, 128),
            v(NECK_TILES, 16, 128), v(16, 16, 128), v(NECK_TILES, 16, 128),
            v(16, REST_TILES, 16, 128), v(16, REST_TILES, 16, 128), v(16, REST_TILES, 16, 128), v(16, REST_TILES, 16, 128),
            v(REST_TILES, 16, 128), v(16, 16, 128), v(REST_TILES, 16, 128),
            dma((5,)), dma((2, 8)), dma((2, 16)), dma((2, 8)), dma((2, 16)), dma((2, 8)),
            dma((2, 14)), dma((2, 32)), dma((2, 32)), dma((2, 32)), dma((2, 32)), dma((2, 8)), dma((2, 8)), dma((2, 8)), dma((2, 8)),
            pltpu.SemaphoreType.REGULAR((5,)),
        ],
        compiler_params=pltpu.CompilerParams(
            collective_id=0, has_side_effects=True, vmem_limit_bytes=24 * 1024 * 1024
        ),
    )(
        *(pltpu.with_memory_space_constraint(t, pltpu.HBM) for t in (
            level_in,
            w_level.reshape(3, 384, 128),
            w_down.reshape(512, 256),
            w_neck.reshape(3, 768, 256),
            jnp.transpose(cotangent, (0, 2, 1)),
        ))
    )
    outs = pl.pallas_call(
        results_kernel,
        out_shape=[
            jax.ShapeDtypeStruct((4, 16, 512), BF16),
            jax.ShapeDtypeStruct((8, 64, 128), BF16),
            jax.ShapeDtypeStruct((2, LEVEL_OWNERS, 3, 16, 128), BF16),
            jax.ShapeDtypeStruct((16, 2, 16, 256), BF16),
            jax.ShapeDtypeStruct((4, 4, NECK_TILES, 16, 256), BF16),
        ],
        in_specs=[vmem] * 4,
        out_specs=[hbm] * 5,
        scratch_shapes=[dma((8,))],
        compiler_params=pltpu.CompilerParams(vmem_limit_bytes=1024 * 1024),
    )(*outs)
    return (
        jnp.transpose(outs[0], (0, 2, 1)),
        outs[1],
        outs[2].reshape(w_level.shape),
        outs[3].reshape(w_down.shape),
        outs[4].reshape(w_neck.shape),
    )


def solution(mesh):
    return jax.shard_map(
        local,
        mesh=mesh,
        in_specs=(P("gy", "gx", None), P(), P(), P(), P("gy", None, "gx")),
        out_specs=(P("gy", None, "gx"), P("gy", "gx", None), P(), P(), P()),
        check_vma=False,
    )
```

```python
import functools
import math

import jax
import jax.numpy as jnp
from jax import lax
from jax.experimental import pallas as pl
from jax.experimental.pallas import tpu as pltpu
from jax.sharding import PartitionSpec as P

MESH = pl.DeviceIdType.MESH
BF16, F32 = jnp.bfloat16, jnp.float32

RIM = 5
WIDE = 96
NARROW = 48
SIDES = [(dy, dx) for dy in (-1, 0, 1) for dx in (-1, 0, 1) if (dy, dx) != (0, 0)]
FAR_FIRST = sorted(range(1, 16), key=lambda k: -(min(k // 4, 4 - k // 4) + min(k % 4, 4 - k % 4)))
Z_FAR_FIRST = sorted(range(1, 16), key=lambda k: -min(k, 16 - k))
NECK_TILES = 9
ROUTE = 5
REST_TILES = 5
LEVEL_OWNERS = 12


def slope_of(v):
    s = jax.nn.sigmoid(v)
    return s + v * s * (1.0 - s)


def dot(a, b):
    return jnp.dot(a, b, preferred_element_type=F32)


def dot_nt(a, b):
    return lax.dot_general(a, b, (((1,), (1,)), ((), ())), preferred_element_type=F32)


def dot_tn(a, b):
    return lax.dot_general(a, b, (((0,), (0,)), ((), ())), preferred_element_type=F32)


def kernel(
    scales,
    level_in, wl_hbm, wd_hbm, wn_hbm, cot_hbm,
    neck_out, grad_input, a_all, b_all,
    level_own, cot_in, wl, wd, wn, wlt,
    lp, lf, im_l, pre_l, act, dn, nf, im_n, cf, gf, im_g, gate_own, ng, lbf, gp, g2f, im_b,
    cot_send, cot_recv, ct, hr, no_send, no_recv,
    neck_own, level_acc, down_acc,
    a_pair_s, a_pair_r, a_work, near_a, near_b, far_a, far_b, a_piece, a_z, a_fin,
    b_pair_s, b_pair_r, b_work, b_xy, b_piece, b_z, b_fin,
    w_sem, e1_sem, cot_sem, ch_sem, no_sem, e4_sem,
    pair_sem, xy_sem, z_sem, zb_sem, xyb_sem, near_sem, far_sem, back1_sem, back2_sem, known,
):
    gy, gx = lax.axis_index("gy"), lax.axis_index("gx")
    z, core = gy // 2, gy % 2
    other = 1 - core

    def side(dy, dx):
        return ((gy + dy + 32) % 32, (gx + dx + 16) % 16)

    pair_dev = (z * 2 + other, gx)
    x, y = gx // 4, gx % 4

    def in_plane(k, sign=1):
        return ((x + sign * (k // 4) + 4) % 4) * 4 + (y + sign * (k % 4) + 4) % 4

    plane = [None] + [(gy, in_plane(k)) for k in range(1, 16)]

    def column(zz):
        return (zz * 2 + core, gx)

    loads = [
        pltpu.make_async_copy(cot_hbm, cot_in, w_sem.at[3]),
        pltpu.make_async_copy(level_in, level_own, w_sem.at[4]),
        pltpu.make_async_copy(wl_hbm, wl, w_sem.at[0]),
        pltpu.make_async_copy(wd_hbm, wd, w_sem.at[1]),
        pltpu.make_async_copy(wn_hbm, wn, w_sem.at[2]),
    ]
    for load in loads[:2]:
        load.start()
    barrier = pltpu.get_barrier_semaphore()
    x_peer = [None] + [(gy, (x + k) % 4 * 4 + y) for k in range(1, 4)]
    y_peer = [None] + [(gy, x * 4 + (y + k) % 4) for k in range(1, 4)]
    corners_first = sorted(SIDES, key=lambda e: -abs(e[0]) - abs(e[1]))
    peers = [side(dy, dx) for dy, dx in corners_first] + x_peer[1:] + y_peer[1:]
    for peer in peers:
        pl.semaphore_signal(barrier, inc=1, device_id=peer, device_id_type=MESH)

    def copy(src, dst, sems, k, dev):
        return pltpu.make_async_remote_copy(
            src_ref=src, dst_ref=dst, send_sem=sems.at[0, k], recv_sem=sems.at[1, k],
            device_id=dev, device_id_type=MESH,
        )

    sent = []

    def go(copies):
        for c in copies:
            c.start()
        sent.extend(copies)
        return copies

    pl.semaphore_wait(barrier, len(peers))
    def tell(n):
        for dy in (-1, 1):
            pl.semaphore_signal(known.at[n], inc=1, device_id=side(dy * 2 ** n, 0), device_id_type=MESH)

    src_rows = {-1: slice(0, RIM), 0: slice(0, 8), 1: slice(8 - RIM, 8)}
    src_cols = {-1: slice(0, 16), 0: slice(0, 64), 1: slice(48, 64)}
    dst_rows = {-1: slice(RIM + 8, RIM + 8 + RIM), 0: slice(RIM, RIM + 8), 1: slice(0, RIM)}
    dst_cols = {-1: slice(80, 96), 0: slice(16, 80), 1: slice(0, 16)}
    e1 = go([
        copy(level_in.at[src_rows[dy], src_cols[dx]], lp.at[dst_rows[dy], dst_cols[dx]], e1_sem, n, side(dy, dx))
        for n, (dy, dx) in sorted(enumerate(SIDES), key=lambda e: -abs(e[1][0]) - abs(e[1][1]))
    ])
    for k in range(1, 4):
        pl.semaphore_signal(known.at[4], inc=1, device_id=y_peer[k], device_id_type=MESH)
    tell(0)
    loads[0].wait()
    for load in loads[2:]:
        load.start()
    lane = lax.broadcasted_iota(jnp.int32, (16, 128), 1)
    for q in range(4):
        rows = [cot_in[r, :, 128 * q:128 * q + 128].astype(F32) for r in range(4)]
        for j in range(4):
            out = pltpu.roll(rows[3], (32 * (3 - j)) % 128, 1) if j != 3 else rows[3]
            for r in (2, 1, 0):
                part = pltpu.roll(rows[r], (32 * (r - j)) % 128, 1) if r != j else rows[r]
                out = jnp.where(lane < 32 * (r + 1), part, out)
            cot_send[4 * q + j, 0] = out.astype(BF16)
    for t in range(16):
        cot_send[t, 1] = jnp.where(lane % 32 < 16, cot_send[(t + 1) % 16, 0].astype(F32), cot_send[(t + 15) % 16, 0].astype(F32)).astype(BF16)
    cot_recv[gx] = cot_send[gx]

    top_ok = jnp.where(gy > 0, 1.0, 0.0).astype(F32)
    bottom_ok = jnp.where(gy < 31, 1.0, 0.0).astype(F32)
    left_ok = jnp.where(gx > 0, 1.0, 0.0).astype(F32)
    right_ok = jnp.where(gx < 15, 1.0, 0.0).astype(F32)

    pl.semaphore_wait(known.at[4], 3)
    cot_copies = go([
        copy(cot_send.at[in_plane(k)], cot_recv.at[gx], cot_sem, k, plane[k]) for k in FAR_FIRST
    ])
    loads[1].wait()
    lf[0:8] = jnp.zeros((8, 128), F32)
    lf[8 + 18 * WIDE:] = jnp.zeros((8, 128), F32)
    for r in range(8):
        start = 8 + (r + RIM) * WIDE + 16
        lf[start:start + 64] = level_own[r].astype(F32)

    pl.semaphore_wait(known.at[0], 2)
    tell(1)

    loads[2].wait()
    for ky in range(3):
        for kx in range(3):
            w = wl[2 - ky, (2 - kx) * 128:(3 - kx) * 128, :].astype(F32)
            wlt[ky, kx * 128:(kx + 1) * 128, :] = w.T.astype(BF16)

    for c in e1:
        c.wait_recv()
    pl.semaphore_wait(known.at[1], 2)
    tell(2)
    for r in range(18):
        row_ok = top_ok if r < RIM else bottom_ok if r >= RIM + 8 else None
        base = 8 + r * WIDE
        left = lp[r, 0:16].astype(F32) * left_ok
        right = lp[r, 80:96].astype(F32) * right_ok
        if row_ok is not None:
            left, right = left * row_ok, right * row_ok
            lf[base + 16:base + 80] = lp[r, 16:80].astype(F32) * row_ok
        lf[base:base + 16] = left
        lf[base + 80:base + 96] = right
    for r in range(18):
        for kx in range(3):
            start = 7 + kx + r * WIDE
            im_l[r * WIDE:(r + 1) * WIDE, kx * 128:(kx + 1) * 128] = lf[start:start + WIDE].astype(BF16)

    for q in range(4):
        pre = dot(im_l[4 * q * WIDE:(4 * q + 4) * WIDE], wl[0])
        for ky in (1, 2):
            pre = pre + dot(im_l[(4 * q + ky) * WIDE:(4 * q + ky + 4) * WIDE], wl[ky])
        own = lf[8 + (4 * q + 1) * WIDE:8 + (4 * q + 5) * WIDE]
        act[4 * q * WIDE:(4 * q + 4) * WIDE] = own + pre * jax.nn.sigmoid(pre)
        if q in (1, 2):
            pre_l[(q - 1) * 4 * WIDE:q * 4 * WIDE] = pre

    for c in cot_copies:
        c.wait_recv()
    cot_tile = cot_recv[:, 0].reshape(256, 128).astype(F32).T
    cot_beside = cot_recv[:, 1].reshape(256, 128).astype(F32).T
    for r in range(4):
        base = (r + 1) * NARROW
        cf[base:base + 8] = cot_beside[32 * r + 24:32 * r + 32] * left_ok
        cf[base + 8:base + 40] = cot_tile[32 * r:32 * r + 32]
        cf[base + 40:base + 48] = cot_beside[32 * r:32 * r + 8] * right_ok
    ct[0] = cf[NARROW:2 * NARROW].astype(BF16)
    ct[1] = cf[4 * NARROW:5 * NARROW].astype(BF16)
    ch = go([copy(ct.at[n], hr.at[n], ch_sem, n, side(2 * n - 1, 0)) for n in range(2)])

    for rr in range(16):
        for q in range(2):
            lanes = slice(128 * (2 * (rr % 2) + q), 128 * (2 * (rr % 2) + q) + 128)
            dn[(rr // 2) * NARROW:(rr // 2 + 1) * NARROW, lanes] = act[pl.ds(rr * WIDE + q, NARROW, stride=2), :].astype(BF16)
    loads[3].wait()
    col = lax.broadcasted_iota(jnp.int32, (NARROW, 256), 0)
    col_ok = jnp.where(col < 8, left_ok, jnp.where(col >= 40, right_ok, 1.0))
    col_own = jnp.where((col >= 8) & (col < 40), 1.0, 0.0)
    nf[0:8] = jnp.zeros((8, 256), F32)
    nf[8 + 8 * NARROW:] = jnp.zeros((8, 256), F32)
    neck_in = dot(dn[...], wd[...]).astype(BF16).astype(F32)
    for r in range(8):
        row = neck_in[r * NARROW:(r + 1) * NARROW] * col_ok
        if r < 2:
            row = row * top_ok
        if r >= 6:
            row = row * bottom_ok
        nf[8 + r * NARROW:8 + (r + 1) * NARROW] = row
    for kx in range(3):
        im_n[:, kx * 256:(kx + 1) * 256] = nf[7 + kx:7 + kx + 8 * NARROW].astype(BF16)
    loads[4].wait()
    neck_pre = dot(im_n[0:6 * NARROW], wn[0])
    for ky in (1, 2):
        neck_pre = neck_pre + dot(im_n[ky * NARROW:(ky + 6) * NARROW], wn[ky])

    own = slice(NARROW, 5 * NARROW)
    gf[0:8] = jnp.zeros((8, 256), F32)
    gf[8 + 6 * NARROW:] = jnp.zeros((8, 256), F32)
    gate = (cf[own] * slope_of(neck_pre[own])).astype(BF16).astype(F32)
    gf[8 + NARROW:8 + 5 * NARROW] = gate
    for r in range(4):
        gate_own[r * NARROW:(r + 1) * NARROW] = (gate[r * NARROW:(r + 1) * NARROW] * col_own).astype(BF16)

    def half_lanes(half):
        return pl.ds(pl.multiple_of(half * 128, 128), 128)

    theirs = gate_own[:, half_lanes(other)]
    a_pair = []
    for ky in range(3):
        part = dot_tn(im_n[(1 + ky) * NARROW:(5 + ky) * NARROW], theirs)
        third = slice(48 * ky, 48 * ky + 48)
        a_pair_s[third] = part.astype(BF16).reshape(48, 16, 128)
        a_pair.extend(go([copy(a_pair_s.at[third], a_pair_r.at[third], pair_sem, (0, 2, 12)[ky], pair_dev)]))
    mine = gate_own[:, half_lanes(core)]
    for ky in range(3):
        neck_own[48 * ky:48 * ky + 48] = dot_tn(im_n[(1 + ky) * NARROW:(5 + ky) * NARROW], mine).reshape(48, 16, 128)

    for n in range(16):
        if n in (0, 5, 10):
            a_pair[n // 5].wait_recv()
        part = slice(n * NECK_TILES, (n + 1) * NECK_TILES)
        a_work[n // 4, n % 4] = (neck_own[part] + a_pair_r[part].astype(F32)).astype(BF16)
    near = []
    for k in (2, 1, 3):
        near.append(copy(a_work.at[(x + k) % 4, :, 0:ROUTE], near_a.at[k], near_sem, k, x_peer[k]))
        near.append(copy(a_work.at[:, (y + k) % 4, ROUTE:], near_b.at[k], near_sem, 4 + k, y_peer[k]))
    go(near)
    pl.semaphore_wait(known.at[2], 2)
    tell(3)

    for c in ch:
        c.wait_recv()
    for n, ok, rows in ((1, top_ok, slice(0, NARROW)), (0, bottom_ok, slice(5 * NARROW, 6 * NARROW))):
        v = hr[n].astype(F32) * ok * slope_of(neck_pre[rows])
        gf[8 + rows.start:8 + rows.stop] = v.astype(BF16).astype(F32)

    for kx in range(3):
        im_g[:, kx * 256:(kx + 1) * 256] = gf[7 + kx:7 + kx + 6 * NARROW].astype(BF16)
    back = None
    for ky in range(3):
        for kx in range(3):
            term = dot_nt(
                im_g[ky * NARROW:(ky + 4) * NARROW, kx * 256:(kx + 1) * 256],
                wn[2 - ky, (2 - kx) * 256:(3 - kx) * 256, :],
            )
            back = term if back is None else back + term
    for r in range(4):
        v = cf[(r + 1) * NARROW:(r + 2) * NARROW] + back[r * NARROW:(r + 1) * NARROW]
        ng[r * NARROW:(r + 1) * NARROW] = (v * col_own).astype(BF16)
    spread = dot_nt(ng[...], wd[...])
    for r in range(4):
        for p in range(2):
            for q in range(2):
                lanes = slice(128 * (2 * p + q), 128 * (2 * p + q) + 128)
                lbf[pl.ds((2 * r + p) * WIDE + q, NARROW, stride=2), :] = spread[r * NARROW:(r + 1) * NARROW, lanes]
    for r in range(8):
        rows_r = slice(r * WIDE + 16, r * WIDE + 80)
        gp[r + 1, 16:80] = (lbf[rows_r] * slope_of(pre_l[rows_r])).astype(BF16)
    def down_terms(half):
        return down_acc[:, half_lanes(half)].reshape(16, 2, 16, 128)

    def level_terms(half):
        return level_acc[pl.ds(pl.multiple_of(half * 576, 576), 576), :].reshape(LEVEL_OWNERS, 3, 16, 128)

    down_acc[...] = dot_tn(dn[2 * NARROW:6 * NARROW], ng[...])
    b_pair_s[:, 0:2] = down_terms(other).astype(BF16)
    b_pair = go([copy(b_pair_s.at[:, 0:2], b_pair_r.at[:, 0:2], pair_sem, 1, pair_dev)])
    own_gate = gp[1:9, 16:80].reshape(512, 128)
    for ky in range(3):
        window = jnp.concatenate(
            [im_l[(4 + ky + r) * WIDE + 16:(4 + ky + r) * WIDE + 80] for r in range(8)], axis=0
        )
        level_acc[ky * 384:(ky + 1) * 384] = dot_tn(window, own_gate)
    nothing = jnp.zeros((16 - LEVEL_OWNERS, 3, 16, 128), BF16)
    b_pair_s[0:LEVEL_OWNERS, 2:5] = level_terms(other).astype(BF16)
    with_level = b_pair_s.at[0:LEVEL_OWNERS, 2:5]
    b_pair.extend(go([copy(with_level, b_pair_r.at[0:LEVEL_OWNERS, 2:5], pair_sem, 14, pair_dev)]))

    for c in b_pair:
        c.wait_recv()
    down, level = down_terms(core), level_terms(core)
    b_work[:, 0:2] = (down + b_pair_r[:, 0:2].astype(F32)).astype(BF16)
    b_work[0:LEVEL_OWNERS, 2:5] = (level + b_pair_r[0:LEVEL_OWNERS, 2:5].astype(F32)).astype(BF16)
    b_work[LEVEL_OWNERS:, 2:5] = nothing
    me_level = gx < LEVEL_OWNERS
    b_plane = []
    for k in FAR_FIRST:
        o = in_plane(k)
        full = copy(b_work.at[o], b_xy.at[k], xy_sem, 16 + k, plane[k])
        short = copy(b_work.at[o, 0:2], b_xy.at[k, 0:2], xy_sem, 16 + k, plane[k])
        b_plane.append((o < LEVEL_OWNERS, full, short))

    def either(cond, one, two):
        pl.when(cond)(one)
        pl.when(jnp.logical_not(cond))(two)

    for cond, full, short in b_plane:
        either(cond, full.start, short.start)

    e4_src = {-1: slice(1, 2), 0: slice(1, 9), 1: slice(8, 9)}
    e4_dst = {-1: slice(9, 10), 0: slice(1, 9), 1: slice(0, 1)}
    e4_scol = {-1: slice(16, 32), 0: slice(16, 80), 1: slice(64, 80)}
    e4 = go([
        copy(gp.at[e4_src[dy], e4_scol[dx]], gp.at[e4_dst[dy], dst_cols[dx]], e4_sem, n, side(dy, dx))
        for n, (dy, dx) in enumerate(SIDES)
    ])

    for c in near:
        c.wait_recv()
    for p in range(4):
        via_x, via_y = a_work[x, p, 0:ROUTE].astype(F32), a_work[p, y, ROUTE:].astype(F32)
        for k in range(1, 4):
            via_x = via_x + near_a[k, p].astype(F32)
            via_y = via_y + near_b[k, p].astype(F32)
        near_a[0, p] = via_x.astype(BF16)
        near_b[0, p] = via_y.astype(BF16)
    far = []
    for k in (2, 1, 3):
        far.append(copy(near_a.at[0, (y + k) % 4], far_a.at[k], far_sem, k, y_peer[k]))
        far.append(copy(near_b.at[0, (x + k) % 4], far_b.at[k], far_sem, 4 + k, x_peer[k]))
    go(far)

    rows = []
    for r in range(4):
        v = neck_pre[(r + 1) * NARROW + 8:(r + 1) * NARROW + 40]
        rows.append(nf[8 + (r + 2) * NARROW + 8:8 + (r + 2) * NARROW + 40] + v * jax.nn.sigmoid(v))
    no_send[...] = jnp.concatenate(rows, axis=0).T.astype(BF16).reshape(16, 16, 128)
    no_recv[gx] = no_send[gx]
    no_copies = go([copy(no_send.at[in_plane(k)], no_recv.at[gx], no_sem, k, plane[k]) for k in FAR_FIRST])

    pl.semaphore_wait(known.at[3], 2)

    def z_send(piece, buf, tiles, first, sems, offset):
        copies = []
        for k in Z_FAR_FIRST:
            t = (z + k) % 16 - first
            c = copy_z(piece.at[t], buf.at[z], sems, offset + k, offset + z, column((z + k) % 16))
            copies.append(((t >= 0) & (t < tiles), c))
        return copies

    def copy_z(src, dst, sems, ks, kr, dev):
        return pltpu.make_async_remote_copy(
            src_ref=src, dst_ref=dst, send_sem=sems.at[0, ks], recv_sem=sems.at[1, kr],
            device_id=dev, device_id_type=MESH,
        )

    def start_all(copies):
        for cond, c in copies:
            pl.when(cond)(c.start)

    def b_sum(tiles):
        total = b_work[gx, tiles].astype(F32)
        for k in range(1, 16):
            total = total + b_xy[k, tiles].astype(F32)
        b_piece[tiles] = total.astype(BF16)

    def owns(first, tiles):
        return (z >= first) & (z < first + tiles)

    def z_sum(piece, buf, fin, tiles, first, sems, offset, scale):
        @pl.when(owns(first, tiles))
        def _():
            mine = z - first
            for s in range(16):
                @pl.when(z != s)
                def _(s=s):
                    copy_z(piece.at[0], buf.at[s], sems, offset, offset + s, column(s)).wait_recv()
            buf[z] = piece[mine]
            total = buf[0].astype(F32)
            for s in range(1, 16):
                total = total + buf[s].astype(F32)
            fin[mine] = (total * scale).astype(BF16)
            for k in Z_FAR_FIRST:
                copy_z(fin.at[mine], fin.at[mine], zb_sem, offset + k, offset + mine, column((z + k) % 16)).start()

    def z_back(fin, tiles, first, offset):
        for t in range(tiles):
            @pl.when(z != first + t)
            def _(t=t):
                copy_z(fin.at[t], fin.at[t], zb_sem, offset, offset + t, column(first + t)).wait_recv()

    def z_back_sent(fin, tiles, first, offset):
        @pl.when(owns(first, tiles))
        def _():
            for k in Z_FAR_FIRST:
                copy_z(fin.at[0], fin.at[0], zb_sem, offset + k, offset, column((z + k) % 16)).wait_send()

    for c in far:
        c.wait_recv()
    via_x, via_y = near_a[0, y].astype(F32), near_b[0, x].astype(F32)
    for k in range(1, 4):
        via_x = via_x + far_a[k].astype(F32)
        via_y = via_y + far_b[k].astype(F32)
    a_piece[0:ROUTE] = via_x.astype(BF16)
    a_piece[ROUTE:] = via_y.astype(BF16)
    a_zs = z_send(a_piece, a_z, NECK_TILES, 0, z_sem, 0)
    start_all(a_zs)
    @pl.when(me_level)
    def _():
        for _, full, _ in b_plane:
            full.wait_recv()
        b_sum(slice(2, REST_TILES))

    @pl.when(jnp.logical_not(me_level))
    def _():
        for _, _, short in b_plane:
            short.wait_recv()
        b_piece[2:] = nothing[0]

    b_sum(slice(0, 2))
    b_zs = z_send(b_piece, b_z, REST_TILES, NECK_TILES, z_sem, 16)
    start_all(b_zs)
    for c in e4:
        c.wait_recv()
    g2f[0:8] = jnp.zeros((8, 128), F32)
    g2f[8 + 10 * WIDE:] = jnp.zeros((8, 128), F32)
    for r in range(10):
        row_ok = top_ok if r == 0 else bottom_ok if r == 9 else None
        base = 8 + r * WIDE
        left, mid, right = gp[r, 0:16].astype(F32) * left_ok, gp[r, 16:80].astype(F32), gp[r, 80:96].astype(F32) * right_ok
        if row_ok is not None:
            left, mid, right = left * row_ok, mid * row_ok, right * row_ok
        g2f[base:base + 16] = left
        g2f[base + 16:base + 80] = mid
        g2f[base + 80:base + 96] = right
    for r in range(10):
        for kx in range(3):
            start = 7 + kx + r * WIDE
            im_b[r * WIDE:(r + 1) * WIDE, kx * 128:(kx + 1) * 128] = g2f[start:start + WIDE].astype(BF16)
    for q in range(2):
        total = lbf[4 * q * WIDE:(4 * q + 4) * WIDE]
        for ky in range(3):
            total = total + dot(im_b[(4 * q + ky) * WIDE:(4 * q + ky + 4) * WIDE], wlt[ky])
        grad_input[4 * q:4 * q + 4] = total.reshape(4, WIDE, 128)[:, 16:80].astype(BF16)

    for c in no_copies:
        c.wait_recv()
    for q in range(4):
        pieces = [no_recv[4 * q + j].astype(F32) for j in range(4)]
        for r in range(4):
            out = pltpu.roll(pieces[3], (32 * (3 - r)) % 128, 1) if r != 3 else pieces[3]
            for j in (2, 1, 0):
                part = pltpu.roll(pieces[j], (32 * (j - r)) % 128, 1) if r != j else pieces[j]
                out = jnp.where(lane < 32 * (j + 1), part, out)
            neck_out[r, :, 128 * q:128 * q + 128] = out.astype(BF16)

    z_sum(a_piece, a_z, a_fin, NECK_TILES, 0, z_sem, 0, scales[0])
    z_sum(b_piece, b_z, b_fin, REST_TILES, NECK_TILES, z_sem, 16, jnp.where(z < NECK_TILES + 2, scales[0], scales[1]))

    z_back(a_fin, NECK_TILES, 0, 0)
    def b_slot(o):
        return b_all.at[core, o]

    a_all[core, x, y] = a_fin[...]
    leg1 = []
    for k in (2, 1, 3):
        mine_x, mine_y = a_all.at[core, x, y, 0:ROUTE], a_all.at[core, x, y, ROUTE:]
        leg1.append(copy(mine_x, mine_x, back1_sem, k, y_peer[k]))
        leg1.append(copy(mine_y, mine_y, back1_sem, 4 + k, x_peer[k]))
    go(leg1)
    z_back(b_fin, REST_TILES, NECK_TILES, 16)
    b_all[core, gx] = b_fin[...]
    b_back = []
    for k in FAR_FIRST:
        full, short = b_slot(gx), b_all.at[core, gx, 0:2]
        b_back.append((copy(full, full, xyb_sem, 16 + k, plane[k]), copy(short, short, xyb_sem, 16 + k, plane[k])))

    @pl.when(me_level)
    def _():
        for full, _ in b_back:
            full.start()

    @pl.when(jnp.logical_not(me_level))
    def _():
        for _, short in b_back:
            short.start()

    for c in leg1:
        c.wait_recv()

    def block_x(c, xx):
        return a_all.at[c, xx, :, 0:ROUTE]

    def block_y(c, yy):
        return a_all.at[c, :, yy, ROUTE:]

    leg2 = []
    for k in (2, 1, 3):
        leg2.append(copy(block_x(core, x), block_x(core, x), back2_sem, k, x_peer[k]))
        leg2.append(copy(block_y(core, y), block_y(core, y), back2_sem, 4 + k, y_peer[k]))
    go(leg2)

    def swap(k):
        bx, by = block_x(core, (x - k + 4) % 4), block_y(core, (y - k + 4) % 4)
        go([copy(bx, bx, pair_sem, 4 + k, pair_dev), copy(by, by, pair_sem, 8 + k, pair_dev)])

    swap(0)
    for k in FAR_FIRST:
        o = in_plane(k, -1)
        full, short = b_slot(o), b_all.at[core, o, 0:2]
        full, short = copy(full, full, xyb_sem, 16 + k, plane[k]), copy(short, short, xyb_sem, 16 + k, plane[k])
        either(o < LEVEL_OWNERS, full.wait_recv, short.wait_recv)

    def b_parts(c):
        return b_all.at[c, 0:LEVEL_OWNERS], b_all.at[c, LEVEL_OWNERS:, 0:2]

    go([copy(part, part, pair_sem, (3, 13)[n], pair_dev) for n, part in enumerate(b_parts(core))])
    for k in (1, 3, 2):
        bx, by = block_x(core, (x - k + 4) % 4), block_y(core, (y - k + 4) % 4)
        copy(bx, bx, back2_sem, k, x_peer[k]).wait_recv()
        copy(by, by, back2_sem, 4 + k, y_peer[k]).wait_recv()
        swap(k)
    for n, part in enumerate(b_parts(other)):
        copy(part, part, pair_sem, (3, 13)[n], pair_dev).wait_recv()
    for k in range(4):
        bx, by = block_x(other, (x - k + 4) % 4), block_y(other, (y - k + 4) % 4)
        copy(bx, bx, pair_sem, 4 + k, pair_dev).wait_recv()
        copy(by, by, pair_sem, 8 + k, pair_dev).wait_recv()

    for c in sent:
        c.wait_send()
    for (cond, full, short), (back, back_short) in zip(b_plane, b_back):
        either(cond, full.wait_send, short.wait_send)
        either(me_level, back.wait_send, back_short.wait_send)
    for cond, c in a_zs + b_zs:
        pl.when(cond)(c.wait_send)
    z_back_sent(a_fin, NECK_TILES, 0, 0)
    z_back_sent(b_fin, REST_TILES, NECK_TILES, 16)


def results_kernel(strip, level, a_all, b_all, neck_out, grad_input, grad_level, grad_down, grad_neck, sems):
    copies = [(strip, neck_out), (level, grad_input)]
    for half in range(2):
        lanes = slice(128 * half, 128 * half + 128)
        copies.append((a_all.at[half], grad_neck.at[:, :, :, :, lanes]))
        copies.append((b_all.at[half, :, 0:2], grad_down.at[:, :, :, lanes]))
        copies.append((b_all.at[half, 0:LEVEL_OWNERS, 2:5], grad_level.at[half]))
    copies = [pltpu.make_async_copy(src, dst, sems.at[n]) for n, (src, dst) in enumerate(copies)]
    for c in copies:
        c.start()
    for c in copies:
        c.wait()


def local(level_in, w_level, w_down, w_neck, cotangent):
    device_count = lax.axis_size("gy") * lax.axis_size("gx")
    level_count = level_in.shape[0] * level_in.shape[1] * device_count
    level_scale = 1.0 / math.sqrt(level_count)
    neck_scale = 1.0 / math.sqrt(level_count // 4)
    vmem = pl.BlockSpec(memory_space=pltpu.VMEM)
    hbm = pl.BlockSpec(memory_space=pltpu.HBM)
    dma = pltpu.SemaphoreType.DMA

    def v(*shape, dtype=BF16):
        return pltpu.VMEM(shape, dtype)

    outs = pl.pallas_call(
        functools.partial(kernel, (neck_scale, level_scale)),
        out_shape=[
            jax.ShapeDtypeStruct((4, 16, 512), BF16),
            jax.ShapeDtypeStruct((8, 64, 128), BF16),
            jax.ShapeDtypeStruct((2, 4, 4, NECK_TILES, 16, 128), BF16),
            jax.ShapeDtypeStruct((2, 16, REST_TILES, 16, 128), BF16),
        ],
        in_specs=[hbm] * 5,
        out_specs=[vmem] * 4,
        scratch_shapes=[
            v(8, 64, 128), v(4, 16, 512),
            v(3, 384, 128), v(512, 256), v(3, 768, 256), v(3, 384, 128),
            v(18, WIDE, 128), v(16 + 18 * WIDE, 128, dtype=F32), v(18 * WIDE, 384),
            v(8 * WIDE, 128, dtype=F32), v(16 * WIDE, 128, dtype=F32), v(8 * NARROW, 512),
            v(16 + 8 * NARROW, 256, dtype=F32), v(8 * NARROW, 768),
            v(6 * NARROW, 256, dtype=F32), v(16 + 6 * NARROW, 256, dtype=F32), v(6 * NARROW, 768),
            v(4 * NARROW, 256), v(4 * NARROW, 256), v(8 * WIDE, 128, dtype=F32),
            v(10, WIDE, 128), v(16 + 10 * WIDE, 128, dtype=F32), v(10 * WIDE, 384),
            v(16, 2, 16, 128), v(16, 2, 16, 128), v(2, NARROW, 256), v(2, NARROW, 256),
            v(16, 16, 128), v(16, 16, 128),
            v(144, 16, 128, dtype=F32), v(1152, 128, dtype=F32), v(512, 256, dtype=F32),
            v(16 * NECK_TILES, 16, 128), v(16 * NECK_TILES, 16, 128), v(4, 4, NECK_TILES, 16, 128),
            v(4, 4, ROUTE, 16, 128), v(4, 4, NECK_TILES - ROUTE, 16, 128),
            v(4, ROUTE, 16, 128), v(4, NECK_TILES - ROUTE, 16, 128),
            v(NECK_TILES, 16, 128), v(16, 16, 128), v(NECK_TILES, 16, 128),
            v(16, REST_TILES, 16, 128), v(16, REST_TILES, 16, 128), v(16, REST_TILES, 16, 128), v(16, REST_TILES, 16, 128),
            v(REST_TILES, 16, 128), v(16, 16, 128), v(REST_TILES, 16, 128),
            dma((5,)), dma((2, 8)), dma((2, 16)), dma((2, 8)), dma((2, 16)), dma((2, 8)),
            dma((2, 15)), dma((2, 32)), dma((2, 32)), dma((2, 32)), dma((2, 32)), dma((2, 8)), dma((2, 8)), dma((2, 8)), dma((2, 8)),
            pltpu.SemaphoreType.REGULAR((5,)),
        ],
        compiler_params=pltpu.CompilerParams(
            collective_id=0, has_side_effects=True, vmem_limit_bytes=24 * 1024 * 1024
        ),
    )(
        *(pltpu.with_memory_space_constraint(t, pltpu.HBM) for t in (
            level_in,
            w_level.reshape(3, 384, 128),
            w_down.reshape(512, 256),
            w_neck.reshape(3, 768, 256),
            jnp.transpose(cotangent, (0, 2, 1)),
        ))
    )
    outs = pl.pallas_call(
        results_kernel,
        out_shape=[
            jax.ShapeDtypeStruct((4, 16, 512), BF16),
            jax.ShapeDtypeStruct((8, 64, 128), BF16),
            jax.ShapeDtypeStruct((2, LEVEL_OWNERS, 3, 16, 128), BF16),
            jax.ShapeDtypeStruct((16, 2, 16, 256), BF16),
            jax.ShapeDtypeStruct((4, 4, NECK_TILES, 16, 256), BF16),
        ],
        in_specs=[vmem] * 4,
        out_specs=[hbm] * 5,
        scratch_shapes=[dma((8,))],
        compiler_params=pltpu.CompilerParams(vmem_limit_bytes=1024 * 1024),
    )(*outs)
    return (
        jnp.transpose(outs[0], (0, 2, 1)),
        outs[1],
        outs[2].reshape(w_level.shape),
        outs[3].reshape(w_down.shape),
        outs[4].reshape(w_neck.shape),
    )


def solution(mesh):
    return jax.shard_map(
        local,
        mesh=mesh,
        in_specs=(P("gy", "gx", None), P(), P(), P(), P("gy", None, "gx")),
        out_specs=(P("gy", None, "gx"), P("gy", "gx", None), P(), P(), P()),
        check_vma=False,
    )
```
